32 devices in a mesh: pb: 8 (over z, y), ka: 4 (over x, core).
Axes of the slice: x: 2, y: 2, z: 4, core: 2. Of those that a mesh axis runs over, the one named last changes fastest.
Arguments:
- queries: bfloat16 [1, 4096, 4096], P(None, 'pb', 'ka'), may hold values from -12 to 12
- keys: bfloat16 [4096, 512], P('ka'), may hold values from -8 to 8
- values: bfloat16 [4096, 512], P('ka'), may hold values from -18 to 18
- block_ids: int32 [1, 8, 16], P(None, 'pb'), may hold values from 0 to 32, as said below
- counts: int32 [1, 8], P(None, 'pb'), may hold values from 1 to 16, as said below
- refresh: int32 [1, 8], P(None, 'pb'), may hold values 0 or 1
- cached_attn: bfloat16 [1, 4096, 4096], P(None, 'pb', 'ka'), may hold values from -3 to 3
- wo: bfloat16 [4096, 8192], P('pb', 'ka'), may hold values from -0.09375 to 0.09375
Outputs:
- mixed: bfloat16 [1, 4096, 8192], P(None, 'pb', 'ka')
The draws below stay inside these ranges and needn't reach their ends.
Inputs may be any that keep to these rules, and one draw needn't show every extreme that they name: `block_ids`: row (r, p) lists counts[r, p] distinct key-block numbers in ascending order in its first slots; the other slots hold 32. `counts`: some query block has exactly 16 active key blocks and some has exactly one.
All inputs are finite; a program needn't handle non-finite values. No bound on the sum of `refresh` on one device may be relied on, other than what follows from the above.
Results may differ from the reference program's by a relative error of at most 0.014.
Values may be sent and summed in bfloat16 or wider, within the bound.
No kernel may reach another device: no remote copies, remote signals or barrier semaphores. Data moves between devices by JAX's collectives and lax.ppermute only.
A program may use at most 128 MiB of HBM per device.

```python
import math
import jax
import jax.numpy as jnp
from jax import lax

D = 8192
HEAD_SIZE = 128
QUERY_HEAD_COUNT = 32
KEY_VALUE_HEADS = 4
QUERY_BLOCK_SIZE = 512
KEY_BLOCK_TOKENS = 128
QB_DEV = 1
KB_DEV = 8
NKB = 32
CACHED_KEY_COUNT = 4096
MAXACT = 16
N_PB = 8
N_KA = 4


def active_lists(key):
    base = jax.random.fold_in(key, 11)
    first_key, second_key = jax.random.split(base)
    total_rows = QB_DEV * N_PB
    row_index = jnp.arange(total_rows)
    drawn = jax.random.randint(first_key, (total_rows,), 1, MAXACT + 1)
    drawn = jnp.where(row_index == 0, MAXACT, jnp.where(row_index == 1, 1, drawn))
    priority = jax.random.randint(second_key, (total_rows, NKB), 0, 65536) * NKB + jnp.arange(NKB)[None, :]
    unused, chosen = lax.top_k(priority, MAXACT)
    slots = jnp.arange(MAXACT)[None, :]
    listed = jnp.where(slots < drawn[:, None], chosen, NKB)
    listed = jnp.sort(listed, axis=1)
    return (listed.reshape(QB_DEV, N_PB, MAXACT).astype(jnp.int32), drawn.reshape(QB_DEV, N_PB).astype(jnp.int32))


def random_sign_pattern(key):
    return jax.random.rademacher(jax.random.fold_in(key, 5), (HEAD_SIZE,), dtype=jnp.float32)


def draw_block_ids(key, part):
    listed, drawn = active_lists(key)
    return listed


def draw_counts(key, part):
    listed, drawn = active_lists(key)
    return drawn


def draw_queries(key, part):
    tensor_shape = (QB_DEV, N_PB * QUERY_BLOCK_SIZE, QUERY_HEAD_COUNT * HEAD_SIZE)
    noise = jnp.clip(2.0 * jax.random.normal(jax.random.fold_in(key, 1), tensor_shape, jnp.float32), -9.0, 9.0)
    position = jnp.arange(N_PB * QUERY_BLOCK_SIZE)[None, :, None]
    aligned = position % 64 == 5
    strength = (8 + 2 * (position // 64 % 3)).astype(jnp.float32)
    sign_row = jnp.tile(random_sign_pattern(key), QUERY_HEAD_COUNT)[None, None, :]
    result = jnp.where(aligned, strength * sign_row, noise)
    return result.astype(jnp.bfloat16)


def draw_keys(key, part):
    tensor_shape = (CACHED_KEY_COUNT, KEY_VALUE_HEADS * HEAD_SIZE)
    noise = jnp.clip(jax.random.normal(jax.random.fold_in(key, 2), tensor_shape, jnp.float32), -5.0, 5.0)
    position = jnp.arange(CACHED_KEY_COUNT)[:, None]
    within = position % KEY_BLOCK_TOKENS
    column = jnp.arange(KEY_VALUE_HEADS * HEAD_SIZE)[None, :] % HEAD_SIZE
    lowered = (within == 1) & (column < max(1, HEAD_SIZE // 64))
    strength = jnp.where(lowered, 7.0, 8.0)
    sign_row = jnp.tile(random_sign_pattern(key), KEY_VALUE_HEADS)[None, :]
    result = jnp.where(within < 2, strength * sign_row, noise)
    return result.astype(jnp.bfloat16)


def set_ends(values, key, low, largest):
    spot = [jax.random.randint(jax.random.fold_in(key, axis), (), 0, length) for axis, length in enumerate(values.shape)]
    longest = values.shape.index(max(values.shape))
    beside = spot[:longest] + [(spot[longest] + 1) % values.shape[longest]] + spot[longest + 1:]
    return values.at[tuple(spot)].set(low).at[tuple(beside)].set(largest)


def level_of(key, extent, shards, smallest, top_value):
    def one(axis_at, shards_of):
        draws = jax.random.uniform(jax.random.fold_in(jax.random.fold_in(key, 6), axis_at), (shards_of,), jnp.float32, smallest / len(shards), top_value / len(shards))
        return jnp.repeat(jnp.exp(draws), extent[axis_at] // shards_of).reshape((-1,) + (1,) * (len(extent) - axis_at - 1))

    loudness = one(*shards[0])
    for cut in shards[1:]:
        loudness = loudness * one(*cut)
    return loudness


def normal_values(key, dims, width, reach, pieces=(), kind=jnp.bfloat16):
    values = width * jax.random.normal(key, dims, jnp.float32)
    if pieces:
        values = values * level_of(key, dims, pieces, -0.22, 0.18)
    return jnp.clip(values, -reach, reach).astype(kind)


def setup_inputs(seed: int = 0) -> dict:
    splits = jax.random.split(jax.random.key(seed), 9)
    queries = draw_queries(jax.random.fold_in(splits[8], 71), 0)
    keys = draw_keys(jax.random.fold_in(splits[8], 71), 0)
    values = normal_values(splits[2], (CACHED_KEY_COUNT, KEY_VALUE_HEADS * HEAD_SIZE), 3.0, 18.0, ((0, 4),))
    block_ids = draw_block_ids(jax.random.fold_in(splits[8], 71), 0)
    counts = draw_counts(jax.random.fold_in(splits[8], 71), 0)
    refresh = set_ends((jax.random.randint(splits[5], (QB_DEV, N_PB), 0, 2) < 1).astype(jnp.int32), jax.random.fold_in(splits[5], 1), 0, 1)
    cached_attn = normal_values(splits[6], (QB_DEV, N_PB * QUERY_BLOCK_SIZE, QUERY_HEAD_COUNT * HEAD_SIZE), 0.5, 3.0, ((1, 8), (2, 4)))
    wo = normal_values(splits[7], (QUERY_HEAD_COUNT * HEAD_SIZE, D), (QUERY_HEAD_COUNT * HEAD_SIZE) ** -0.5, 0.09375, ((0, 8), (1, 4)))
    return dict(queries=queries, keys=keys, values=values, block_ids=block_ids, counts=counts, refresh=refresh, cached_attn=cached_attn, wo=wo)


def block_attention(current_query_block, block_list, live_count, refresh_flag, old_rows, cached_key_blocks, cached_value_blocks, wo):
    block_total_count = KB_DEV * N_KA
    group_ratio = QUERY_HEAD_COUNT // KEY_VALUE_HEADS
    scale = 1.0 / math.sqrt(HEAD_SIZE)
    safe = jnp.minimum(block_list, block_total_count - 1).astype(jnp.int32)
    valid = jnp.arange(block_list.shape[0]) < live_count
    key_tiles = cached_key_blocks[safe].astype(jnp.float32)
    value_tiles = cached_value_blocks[safe].astype(jnp.float32)
    owner = safe // KB_DEV
    member = (valid[:, None] & (owner[:, None] == jnp.arange(N_KA)[None, :])).astype(jnp.float32)
    query_float = current_query_block.astype(jnp.float32).reshape(QUERY_BLOCK_SIZE, KEY_VALUE_HEADS, group_ratio, HEAD_SIZE)

    def per_group(operands):
        query_g, key_g, value_g = operands
        scores = jnp.einsum('qrd,akd->rqak', query_g, key_g) * scale
        scores = jnp.where(valid[None, None, :, None], scores, -jnp.inf)
        peak = lax.optimization_barrier(jnp.max(scores, axis=(2, 3)))
        expo = jnp.exp(scores - peak[:, :, None, None])
        denom = lax.optimization_barrier(jnp.sum(expo, axis=(2, 3)))
        weights = lax.optimization_barrier(expo.astype(jnp.bfloat16)).astype(jnp.float32)
        terms = jnp.einsum('rqak,akd->aqrd', weights, value_g)
        parts = jnp.einsum('an,ax->nx', member, terms.reshape(terms.shape[0], -1))
        parts = lax.optimization_barrier(parts.astype(jnp.bfloat16)).astype(jnp.float32)
        total = lax.optimization_barrier(jnp.sum(parts, axis=0)).reshape(QUERY_BLOCK_SIZE, group_ratio, HEAD_SIZE)
        return total / jnp.transpose(denom)[:, :, None]
    heads = lax.map(per_group, (jnp.moveaxis(query_float, 1, 0), jnp.moveaxis(key_tiles, 2, 0), jnp.moveaxis(value_tiles, 2, 0)))
    fresh = jnp.transpose(heads, (1, 0, 2, 3)).reshape(QUERY_BLOCK_SIZE, QUERY_HEAD_COUNT * HEAD_SIZE)
    attn = jnp.where(refresh_flag > 0, fresh, old_rows.astype(jnp.float32)).astype(jnp.bfloat16)
    return jnp.dot(attn, wo, preferred_element_type=jnp.float32).astype(jnp.bfloat16)

def reference(queries, keys, values, block_ids, counts, refresh, cached_attn, wo):
    block_total_count = KB_DEV * N_KA
    cached_key_blocks = keys.reshape(block_total_count, KEY_BLOCK_TOKENS, KEY_VALUE_HEADS, HEAD_SIZE)
    cached_value_blocks = values.reshape(block_total_count, KEY_BLOCK_TOKENS, KEY_VALUE_HEADS, HEAD_SIZE)
    query_blocks = queries.reshape(QB_DEV * N_PB, QUERY_BLOCK_SIZE, QUERY_HEAD_COUNT * HEAD_SIZE)
    lists = block_ids.reshape(QB_DEV * N_PB, block_ids.shape[-1])
    live = counts.reshape(QB_DEV * N_PB)
    flags = refresh.reshape(QB_DEV * N_PB)
    old = cached_attn.reshape(QB_DEV * N_PB, QUERY_BLOCK_SIZE, QUERY_HEAD_COUNT * HEAD_SIZE)

    def one_block(operands):
        current_query_block, block_list, live_count, refresh_flag, old_rows = operands
        return block_attention(current_query_block, block_list, live_count, refresh_flag, old_rows, cached_key_blocks, cached_value_blocks, wo)
    mixed = lax.map(one_block, (query_blocks, lists, live, flags, old))
    return mixed.reshape(QB_DEV, N_PB * QUERY_BLOCK_SIZE, D)
```

```python
import functools
import math

import jax
import jax.numpy as jnp
from jax import lax
from jax.experimental import pallas as pl
from jax.experimental.pallas import tpu as pltpu
from jax.sharding import PartitionSpec as P

HEAD_SIZE = 128
QUERY_HEAD_COUNT = 32
KEY_VALUE_HEADS = 4
QUERY_BLOCK_SIZE = 512
KEY_BLOCK_TOKENS = 128
RATIO = QUERY_HEAD_COUNT // KEY_VALUE_HEADS
LOWEST = -1e30
EXP2_SCALE = math.log2(math.e) / math.sqrt(HEAD_SIZE)


def attention_kernel(heads, meta_ref, q_ref, kv_ref, old_ref, out_ref, peak_ref, denom_ref, acc_ref):
    live = meta_ref[0]
    flag = meta_ref[1]

    @pl.when(flag <= 0)
    def _():
        out_ref[...] = old_ref[...]

    @pl.when(flag > 0)
    def _():
        peak_ref[...] = jnp.full_like(peak_ref, LOWEST)
        denom_ref[...] = jnp.zeros_like(denom_ref)
        acc_ref[...] = jnp.zeros_like(acc_ref)

        def pair(step, carry):
            second = 2 * step + 1 < live
            first_row = pl.multiple_of(meta_ref[2 + 2 * step] * KEY_BLOCK_TOKENS, KEY_BLOCK_TOKENS)
            second_block = jnp.where(
                second, meta_ref[jnp.minimum(3 + 2 * step, meta_ref.shape[0] - 1)], 0
            )
            second_row = pl.multiple_of(second_block * KEY_BLOCK_TOKENS, KEY_BLOCK_TOKENS)
            bias = jnp.where(second, 0.0, LOWEST).astype(jnp.float32)
            tile = jnp.concatenate(
                [
                    kv_ref[pl.ds(first_row, KEY_BLOCK_TOKENS), :],
                    kv_ref[pl.ds(second_row, KEY_BLOCK_TOKENS), :],
                ],
                axis=0,
            )
            key_tile = tile[:, :HEAD_SIZE]
            value_tile = tile[:, HEAD_SIZE:]
            for head in range(heads):
                query = q_ref[:, head * HEAD_SIZE : (head + 1) * HEAD_SIZE]
                scores = lax.dot_general(
                    key_tile, query, (((1,), (1,)), ((), ())), preferred_element_type=jnp.float32
                )
                upper = scores[:KEY_BLOCK_TOKENS]
                lower = scores[KEY_BLOCK_TOKENS:] + bias
                old_peak = peak_ref[head]
                peak = jnp.maximum(
                    old_peak, jnp.max(jnp.maximum(upper, lower), axis=0, keepdims=True)
                )
                decay = jnp.exp2((old_peak - peak) * EXP2_SCALE)
                upper = jnp.exp2((upper - peak) * EXP2_SCALE)
                lower = jnp.exp2((lower - peak) * EXP2_SCALE)
                peak_ref[head] = peak
                denom_ref[head] = denom_ref[head] * decay + jnp.sum(
                    upper + lower, axis=0, keepdims=True
                )
                weights = jnp.concatenate(
                    [upper.astype(jnp.bfloat16), lower.astype(jnp.bfloat16)], axis=0
                )
                update = lax.dot_general(
                    value_tile, weights, (((0,), (0,)), ((), ())), preferred_element_type=jnp.float32
                )
                acc_ref[head] = acc_ref[head] * decay + update
            return carry

        lax.fori_loop(0, (live + 1) // 2, pair, 0)
        for head in range(heads):
            result = acc_ref[head] / denom_ref[head]
            out_ref[:, head * HEAD_SIZE : (head + 1) * HEAD_SIZE] = result.T.astype(jnp.bfloat16)


def attend(meta, queries, kv, old):
    rows, width = queries.shape
    heads = width // HEAD_SIZE
    whole = pl.BlockSpec(memory_space=pltpu.VMEM)
    return pl.pallas_call(
        functools.partial(attention_kernel, heads),
        out_shape=jax.ShapeDtypeStruct((rows, width), jnp.bfloat16),
        in_specs=[pl.BlockSpec(memory_space=pltpu.SMEM), whole, whole, whole],
        out_specs=whole,
        scratch_shapes=[
            pltpu.VMEM((heads, 1, rows), jnp.float32),
            pltpu.VMEM((heads, 1, rows), jnp.float32),
            pltpu.VMEM((heads, HEAD_SIZE, rows), jnp.float32),
        ],
        compiler_params=pltpu.CompilerParams(vmem_limit_bytes=40 << 20),
        cost_estimate=pl.CostEstimate(
            flops=4 * rows * width * 16 * KEY_BLOCK_TOKENS,
            transcendentals=rows * heads * 16 * KEY_BLOCK_TOKENS,
            bytes_accessed=2 * (3 * rows * width + kv.size),
        ),
        name="attend",
    )(meta, queries, kv, old)


def own_head_keys_values(keys, values, groups):
    rows = keys.shape[0]
    both = jnp.concatenate(
        [
            keys.reshape(rows, KEY_VALUE_HEADS, HEAD_SIZE),
            values.reshape(rows, KEY_VALUE_HEADS, HEAD_SIZE),
        ],
        axis=2,
    )
    both = jnp.repeat(both, groups // KEY_VALUE_HEADS, axis=1)
    return lax.all_to_all(
        both.reshape(rows, groups * 2 * HEAD_SIZE), "ka", split_axis=1, concat_axis=0, tiled=True
    )


def ring_of(pb_size):
    if pb_size == 8:
        return [0, 2, 4, 6, 7, 5, 3, 1]
    return list(range(pb_size))


def project_ring(attn, wo):
    pb_size = lax.axis_size("pb")
    depth, columns = wo.shape
    ring = ring_of(pb_size)
    place_of = [ring.index(p) for p in range(pb_size)]
    forward = [(ring[i], ring[(i + 1) % pb_size]) for i in range(pb_size)]
    backward = [(b, a) for a, b in forward]
    here = jnp.asarray(place_of, jnp.int32)[lax.axis_index("pb")]
    order = jnp.asarray(ring, jnp.int32)
    half = columns // 2
    far = pb_size // 2
    slabs = [[(0, wo[:, :half])], [(0, wo[:, half:])]]
    moving = [[slabs[0][0][1]] * 2, [slabs[1][0][1]] * 2]
    for hop in range(1, far + 1):
        for part in range(2):
            if hop < far or part == 0:
                moving[part][0] = lax.ppermute(moving[part][0], "pb", forward)
                slabs[part].append((-hop, moving[part][0]))
            if hop < far or part == 1:
                moving[part][1] = lax.ppermute(moving[part][1], "pb", backward)
                slabs[part].append((hop, moving[part][1]))
    attn_blocks = attn
    results = []
    for part in range(2):
        total = None
        for offset, slab in slabs[part]:
            source = order[(here + offset + pb_size) % pb_size]
            left = attn_blocks(source)
            term = jnp.dot(left, slab, preferred_element_type=jnp.float32)
            total = term if total is None else total + term
        results.append(total.astype(jnp.bfloat16))
    return jnp.concatenate(results, axis=1)


def shards(queries, keys, values, block_ids, counts, refresh, cached_attn, wo):
    groups = lax.axis_size("ka")
    pb_size = lax.axis_size("pb")
    me = lax.axis_index("ka")
    width = QUERY_HEAD_COUNT * HEAD_SIZE
    depth = wo.shape[0]
    kv = own_head_keys_values(keys, values, groups)
    meta = jnp.concatenate([counts[0], refresh[0], block_ids[0, 0]])
    attn = attend(meta, queries[0], kv, cached_attn[0])
    if pb_size == 8 and groups == 4:
        across = lax.ppermute(attn, "ka", [(i, i ^ 2) for i in range(4)])
        beside = lax.ppermute(attn, "ka", [(i, i ^ 1) for i in range(4)])
        corner = lax.ppermute(across, "ka", [(i, i ^ 1) for i in range(4)])
        pieces = jnp.stack([attn, beside, across, corner])
        per = attn.shape[1] // depth

        def block(source):
            slot = jnp.bitwise_xor(source // per, me)
            return lax.dynamic_slice(
                pieces, (slot, 0, (source % per) * depth), (1, attn.shape[0], depth)
            )[0]

        mixed = project_ring(block, wo)
    else:
        attn_full = lax.all_gather(attn, "ka", axis=1, tiled=True)
        mixed = jnp.dot(
            attn_full, lax.all_gather(wo, "pb", axis=0, tiled=True), preferred_element_type=jnp.float32
        ).astype(jnp.bfloat16)
    return mixed[None]


def solution(mesh):
    placed = (
        P(None, "pb", "ka"),
        P("ka", None),
        P("ka", None),
        P(None, "pb", None),
        P(None, "pb"),
        P(None, "pb"),
        P(None, "pb", "ka"),
        P("pb", "ka"),
    )
    return jax.shard_map(
        shards, mesh=mesh, in_specs=placed, out_specs=P(None, "pb", "ka"), check_vma=False
    )
```

```python
import functools
import math

import jax
import jax.numpy as jnp
from jax import lax
from jax.experimental import pallas as pl
from jax.experimental.pallas import tpu as pltpu
from jax.sharding import PartitionSpec as P

HEAD_SIZE = 128
QUERY_HEAD_COUNT = 32
KEY_VALUE_HEADS = 4
QUERY_BLOCK_SIZE = 512
KEY_BLOCK_TOKENS = 128
RATIO = QUERY_HEAD_COUNT // KEY_VALUE_HEADS
LOWEST = -1e30
EXP2_SCALE = math.log2(math.e) / math.sqrt(HEAD_SIZE)


def attention_kernel(heads, meta_ref, q_ref, kv_ref, old_ref, out_ref, peak_ref, denom_ref, acc_ref):
    live = meta_ref[0]
    flag = meta_ref[1]

    @pl.when(flag <= 0)
    def _():
        out_ref[...] = old_ref[...]

    @pl.when(flag > 0)
    def _():
        peak_ref[...] = jnp.full_like(peak_ref, LOWEST)
        denom_ref[...] = jnp.zeros_like(denom_ref)
        acc_ref[...] = jnp.zeros_like(acc_ref)

        def pair(step, carry):
            second = 2 * step + 1 < live
            first_row = pl.multiple_of(meta_ref[2 + 2 * step] * KEY_BLOCK_TOKENS, KEY_BLOCK_TOKENS)
            second_block = jnp.where(
                second, meta_ref[jnp.minimum(3 + 2 * step, meta_ref.shape[0] - 1)], 0
            )
            second_row = pl.multiple_of(second_block * KEY_BLOCK_TOKENS, KEY_BLOCK_TOKENS)
            bias = jnp.where(second, 0.0, LOWEST).astype(jnp.float32)
            tile = jnp.concatenate(
                [
                    kv_ref[pl.ds(first_row, KEY_BLOCK_TOKENS), :],
                    kv_ref[pl.ds(second_row, KEY_BLOCK_TOKENS), :],
                ],
                axis=0,
            )
            key_tile = tile[:, :HEAD_SIZE]
            value_tile = tile[:, HEAD_SIZE:]
            for head in range(heads):
                query = q_ref[:, head * HEAD_SIZE : (head + 1) * HEAD_SIZE]
                scores = lax.dot_general(
                    key_tile, query, (((1,), (1,)), ((), ())), preferred_element_type=jnp.float32
                )
                upper = scores[:KEY_BLOCK_TOKENS]
                lower = scores[KEY_BLOCK_TOKENS:] + bias
                old_peak = peak_ref[head]
                peak = jnp.maximum(
                    old_peak, jnp.max(jnp.maximum(upper, lower), axis=0, keepdims=True)
                )
                decay = jnp.exp2((old_peak - peak) * EXP2_SCALE)
                upper = jnp.exp2((upper - peak) * EXP2_SCALE)
                lower = jnp.exp2((lower - peak) * EXP2_SCALE)
                peak_ref[head] = peak
                denom_ref[head] = denom_ref[head] * decay + jnp.sum(
                    upper + lower, axis=0, keepdims=True
                )
                weights = jnp.concatenate(
                    [upper.astype(jnp.bfloat16), lower.astype(jnp.bfloat16)], axis=0
                )
                update = lax.dot_general(
                    value_tile, weights, (((0,), (0,)), ((), ())), preferred_element_type=jnp.float32
                )
                acc_ref[head] = acc_ref[head] * decay + update
            return carry

        lax.fori_loop(0, (live + 1) // 2, pair, 0)
        for head in range(heads):
            result = acc_ref[head] / denom_ref[head]
            out_ref[:, head * HEAD_SIZE : (head + 1) * HEAD_SIZE] = result.T.astype(jnp.bfloat16)


def attend(meta, queries, kv, old):
    rows, width = queries.shape
    heads = width // HEAD_SIZE
    whole = pl.BlockSpec(memory_space=pltpu.VMEM)
    return pl.pallas_call(
        functools.partial(attention_kernel, heads),
        out_shape=jax.ShapeDtypeStruct((rows, width), jnp.bfloat16),
        in_specs=[pl.BlockSpec(memory_space=pltpu.SMEM), whole, whole, whole],
        out_specs=whole,
        scratch_shapes=[
            pltpu.VMEM((heads, 1, rows), jnp.float32),
            pltpu.VMEM((heads, 1, rows), jnp.float32),
            pltpu.VMEM((heads, HEAD_SIZE, rows), jnp.float32),
        ],
        compiler_params=pltpu.CompilerParams(vmem_limit_bytes=40 << 20),
        cost_estimate=pl.CostEstimate(
            flops=4 * rows * width * 16 * KEY_BLOCK_TOKENS,
            transcendentals=rows * heads * 16 * KEY_BLOCK_TOKENS,
            bytes_accessed=2 * (3 * rows * width + kv.size),
        ),
        name="attend",
    )(meta, queries, kv, old)


def own_head_keys_values(keys, values, groups):
    rows = keys.shape[0]
    both = jnp.concatenate(
        [
            keys.reshape(rows, KEY_VALUE_HEADS, HEAD_SIZE),
            values.reshape(rows, KEY_VALUE_HEADS, HEAD_SIZE),
        ],
        axis=2,
    )
    both = jnp.repeat(both, groups // KEY_VALUE_HEADS, axis=1)
    return lax.all_to_all(
        both.reshape(rows, groups * 2 * HEAD_SIZE), "ka", split_axis=1, concat_axis=0, tiled=True
    )


def place_kernel(chunks, place_ref, *refs):
    own, received = refs[: len(chunks)], refs[len(chunks) : 2 * len(chunks)]
    out_ref, sems = refs[2 * len(chunks)], refs[2 * len(chunks) + 1]
    y = place_ref[1]
    half = out_ref.shape[1] // 2
    copies = []
    for side, pieces in enumerate((own, received)):
        start = 0
        for index, piece in enumerate(pieces):
            column = pl.multiple_of(jnp.bitwise_xor(y, side) * half + start, HEAD_SIZE)
            copies.append(
                pltpu.make_async_copy(
                    piece, out_ref.at[:, pl.ds(column, chunks[index])], sems.at[side, index]
                )
            )
            start += chunks[index]
    for copy in copies:
        copy.start()
    for copy in copies:
        copy.wait()


def place(chunks, where, own, received, columns):
    rows = own[0].shape[0]
    return pl.pallas_call(
        functools.partial(place_kernel, chunks),
        out_shape=jax.ShapeDtypeStruct((rows, columns), jnp.bfloat16),
        in_specs=[pl.BlockSpec(memory_space=pltpu.SMEM)]
        + [pl.BlockSpec(memory_space=pl.ANY)] * (2 * len(chunks)),
        out_specs=pl.BlockSpec(memory_space=pl.ANY),
        scratch_shapes=[pltpu.SemaphoreType.DMA((2, len(chunks)))],
        name="place",
    )(where, *own, *received)


def partial_kernel(first, chunks, place_ref, *refs):
    z, y, me = place_ref[0], place_ref[1], place_ref[2]
    own_rows, other_rows, slabs, refs = refs[:4], refs[4:8], refs[8:15], refs[15:]
    if first:
        outs, refs = refs[: len(chunks)], refs[len(chunks) :]
    else:
        base_ref, own_out, other_out, refs = refs[0], refs[1], refs[2], refs[3:]
    left, right, sems = refs
    rows, depth = own_rows[0].shape[0], slabs[0].shape[0]
    parity = y if first else 1 - y
    column = pl.multiple_of(parity * depth, depth)

    def left_copy(target, slot, side):
        source = (own_rows, other_rows)[side][slot]
        return pltpu.make_async_copy(
            source.at[:, pl.ds(column, depth)],
            left.at[pl.ds(side * rows, rows), pl.ds(target * depth, depth)],
            sems.at[target, side],
        )

    def slab_copy(target, slot):
        return pltpu.make_async_copy(
            slabs[slot], right.at[pl.ds(target * depth, depth), :], sems.at[target, 2]
        )

    for target in range(4):
        slot_here = jnp.bitwise_xor(me, target)
        for slot in range(4):

            @pl.when(slot_here == slot)
            def _(slot=slot):
                left_copy(target, slot, 0).start()
                left_copy(target, slot, 1).start()

        for position in range(4):

            @pl.when(z == position)
            def _(position=position):
                distance = target - position
                slab_copy(target, -distance if distance <= 0 else 3 + distance).start()

    for target in range(4):
        left_copy(target, 0, 0).wait()
        left_copy(target, 0, 1).wait()
        slab_copy(target, 0).wait()

    tile = 256

    def rows_tile(step, carry):
        at = pl.ds(pl.multiple_of(step * tile, tile), tile)
        product = jnp.dot(left[at, :], right[...], preferred_element_type=jnp.float32)
        if first:
            start = 0
            for out, chunk in zip(outs, chunks):
                out[at, :] = product[:, start : start + chunk]
                start += chunk
        else:
            total = (product + base_ref[at, :]).astype(jnp.bfloat16)

            @pl.when(step < rows // tile)
            def _():
                own_out[at, :] = total

            @pl.when(step >= rows // tile)
            def _():
                back = pl.ds(pl.multiple_of(step * tile - rows, tile), tile)
                other_out[back, :] = total

        return carry

    lax.fori_loop(0, 2 * rows // tile, rows_tile, 0)


def partial_product(where, own_rows, other_rows, slabs, chunks=None, base=None):
    rows = own_rows[0].shape[0]
    depth, columns = slabs[0].shape
    first = base is None
    if first:
        out_shape = [jax.ShapeDtypeStruct((2 * rows, chunk), jnp.float32) for chunk in chunks]
    else:
        out_shape = [jax.ShapeDtypeStruct((rows, columns), jnp.bfloat16)] * 2
    whole = pl.BlockSpec(memory_space=pltpu.VMEM)
    return pl.pallas_call(
        functools.partial(partial_kernel, first, chunks),
        out_shape=out_shape,
        in_specs=[pl.BlockSpec(memory_space=pltpu.SMEM)]
        + [pl.BlockSpec(memory_space=pl.ANY)] * 15
        + ([] if first else [whole]),
        out_specs=[whole] * len(out_shape),
        scratch_shapes=[
            pltpu.VMEM((2 * rows, 4 * depth), jnp.bfloat16),
            pltpu.VMEM((4 * depth, columns), jnp.bfloat16),
            pltpu.SemaphoreType.DMA((4, 3)),
        ],
        compiler_params=pltpu.CompilerParams(vmem_limit_bytes=32 << 20),
        cost_estimate=pl.CostEstimate(
            flops=2 * 2 * rows * 4 * depth * columns,
            transcendentals=0,
            bytes_accessed=2 * (2 * rows * 4 * depth + 4 * depth * columns) + 8 * rows * columns,
        ),
        name="partial_first" if first else "partial_rest",
    )(where, *own_rows, *other_rows, *slabs, *([] if first else [base]))


UP = [[(i, i + 2) for i in range(2 * s, 6)] for s in range(3)]
DOWN = [[(i + 2, i) for i in range(6 - 2 * s)] for s in range(3)]
ACROSS_Y = [(i, i ^ 1) for i in range(8)]
ACROSS_X = [(i, i ^ 2) for i in range(4)]
ACROSS_CORE = [(i, i ^ 1) for i in range(4)]


def along_z(piece):
    below, above = [piece], [piece]
    for hop in range(3):
        below.append(lax.ppermute(below[-1], "pb", UP[hop]))
        above.append(lax.ppermute(above[-1], "pb", DOWN[hop]))
    return [piece] + below[1:] + above[1:]


def project(where, attn, wo):
    y = where[1]
    depth, columns = wo.shape
    half = columns // 2
    chunks = (half * 5 // 8, half // 4, half // 8)
    kept = lax.dynamic_slice(wo, (0, y * half), (depth, half))
    kept_slabs = along_z(kept)
    rest_slabs = []
    start = 0
    for chunk in chunks:
        given = lax.dynamic_slice(wo, (0, (1 - y) * half + start), (depth, chunk))
        rest_slabs.append(along_z(lax.ppermute(given, "pb", ACROSS_Y)))
        start += chunk
    across_x = lax.ppermute(attn, "ka", ACROSS_X)
    across_y = lax.ppermute(attn, "pb", ACROSS_Y)
    corner = lax.ppermute(across_y, "ka", ACROSS_X)
    own_rows = [attn, lax.ppermute(attn, "ka", ACROSS_CORE), across_x, lax.ppermute(across_x, "ka", ACROSS_CORE)]
    other_rows = [across_y, lax.ppermute(across_y, "ka", ACROSS_CORE), corner, lax.ppermute(corner, "ka", ACROSS_CORE)]
    bases = partial_product(where, own_rows, other_rows, kept_slabs, chunks=chunks)
    own_out, received = [], []
    for base, slabs in zip(bases, rest_slabs):
        own, other = partial_product(where, own_rows, other_rows, slabs, base=base)
        own_out.append(own)
        received.append(lax.ppermute(other, "pb", ACROSS_Y))
    return place(chunks, where, own_out, received, columns)


def shards(queries, keys, values, block_ids, counts, refresh, cached_attn, wo):
    groups = lax.axis_size("ka")
    pb_size = lax.axis_size("pb")
    me = lax.axis_index("ka")
    kv = own_head_keys_values(keys, values, groups)
    meta = jnp.concatenate([counts[0], refresh[0], block_ids[0, 0]])
    attn = attend(meta, queries[0], kv, cached_attn[0])
    if pb_size == 8 and groups == 4:
        pb = lax.axis_index("pb")
        where = jnp.stack([pb // 2, pb % 2, me]).astype(jnp.int32)
        mixed = project(where, attn, wo)
    else:
        attn_full = lax.all_gather(attn, "ka", axis=1, tiled=True)
        mixed = jnp.dot(
            attn_full, lax.all_gather(wo, "pb", axis=0, tiled=True), preferred_element_type=jnp.float32
        ).astype(jnp.bfloat16)
    return mixed[None]


def solution(mesh):
    placed = (
        P(None, "pb", "ka"),
        P("ka", None),
        P("ka", None),
        P(None, "pb", None),
        P(None, "pb"),
        P(None, "pb"),
        P(None, "pb", "ka"),
        P("pb", "ka"),
    )
    return jax.shard_map(
        shards, mesh=mesh, in_specs=placed, out_specs=P(None, "pb", "ka"), check_vma=False
    )
```

```python
import functools
import math

import jax
import jax.numpy as jnp
from jax import lax
from jax.experimental import pallas as pl
from jax.experimental.pallas import tpu as pltpu
from jax.sharding import PartitionSpec as P

HEAD_SIZE = 128
QUERY_HEAD_COUNT = 32
KEY_VALUE_HEADS = 4
QUERY_BLOCK_SIZE = 512
KEY_BLOCK_TOKENS = 128
RATIO = QUERY_HEAD_COUNT // KEY_VALUE_HEADS
LOWEST = -1e30
EXP2_SCALE = math.log2(math.e) / math.sqrt(HEAD_SIZE)


def attention_kernel(heads, meta_ref, q_ref, kv_ref, old_ref, out_ref, peak_ref, denom_ref, acc_ref):
    live = meta_ref[0]
    flag = meta_ref[1]

    @pl.when(flag <= 0)
    def _():
        out_ref[...] = old_ref[...]

    @pl.when(flag > 0)
    def _():
        peak_ref[...] = jnp.full_like(peak_ref, LOWEST)
        denom_ref[...] = jnp.zeros_like(denom_ref)
        acc_ref[...] = jnp.zeros_like(acc_ref)

        def pair(step, carry):
            second = 2 * step + 1 < live
            first_row = pl.multiple_of(meta_ref[2 + 2 * step] * KEY_BLOCK_TOKENS, KEY_BLOCK_TOKENS)
            second_block = jnp.where(
                second, meta_ref[jnp.minimum(3 + 2 * step, meta_ref.shape[0] - 1)], 0
            )
            second_row = pl.multiple_of(second_block * KEY_BLOCK_TOKENS, KEY_BLOCK_TOKENS)
            bias = jnp.where(second, 0.0, LOWEST).astype(jnp.float32)
            tile = jnp.concatenate(
                [
                    kv_ref[pl.ds(first_row, KEY_BLOCK_TOKENS), :],
                    kv_ref[pl.ds(second_row, KEY_BLOCK_TOKENS), :],
                ],
                axis=0,
            )
            key_tile = tile[:, :HEAD_SIZE]
            value_tile = tile[:, HEAD_SIZE:]
            for head in range(heads):
                query = q_ref[:, head * HEAD_SIZE : (head + 1) * HEAD_SIZE]
                scores = lax.dot_general(
                    key_tile, query, (((1,), (1,)), ((), ())), preferred_element_type=jnp.float32
                )
                upper = scores[:KEY_BLOCK_TOKENS]
                lower = scores[KEY_BLOCK_TOKENS:] + bias
                old_peak = peak_ref[head]
                peak = jnp.maximum(
                    old_peak, jnp.max(jnp.maximum(upper, lower), axis=0, keepdims=True)
                )
                decay = jnp.exp2((old_peak - peak) * EXP2_SCALE)
                upper = jnp.exp2((upper - peak) * EXP2_SCALE)
                lower = jnp.exp2((lower - peak) * EXP2_SCALE)
                peak_ref[head] = peak
                denom_ref[head] = denom_ref[head] * decay + jnp.sum(
                    upper + lower, axis=0, keepdims=True
                )
                weights = jnp.concatenate(
                    [upper.astype(jnp.bfloat16), lower.astype(jnp.bfloat16)], axis=0
                )
                update = lax.dot_general(
                    value_tile, weights, (((0,), (0,)), ((), ())), preferred_element_type=jnp.float32
                )
                acc_ref[head] = acc_ref[head] * decay + update
            return carry

        lax.fori_loop(0, (live + 1) // 2, pair, 0)
        for head in range(heads):
            result = acc_ref[head] / denom_ref[head]
            out_ref[:, head * HEAD_SIZE : (head + 1) * HEAD_SIZE] = result.T.astype(jnp.bfloat16)


def attend(meta, queries, kv, old):
    rows, width = queries.shape
    heads = width // HEAD_SIZE
    whole = pl.BlockSpec(memory_space=pltpu.VMEM)
    return pl.pallas_call(
        functools.partial(attention_kernel, heads),
        out_shape=jax.ShapeDtypeStruct((rows, width), jnp.bfloat16),
        in_specs=[pl.BlockSpec(memory_space=pltpu.SMEM), whole, whole, whole],
        out_specs=whole,
        scratch_shapes=[
            pltpu.VMEM((heads, 1, rows), jnp.float32),
            pltpu.VMEM((heads, 1, rows), jnp.float32),
            pltpu.VMEM((heads, HEAD_SIZE, rows), jnp.float32),
        ],
        compiler_params=pltpu.CompilerParams(vmem_limit_bytes=16 << 20),
        cost_estimate=pl.CostEstimate(
            flops=24 * rows * width * 16 * KEY_BLOCK_TOKENS,
            transcendentals=rows * heads * 16 * KEY_BLOCK_TOKENS,
            bytes_accessed=2 * (3 * rows * width + kv.size),
        ),
        name="attend",
    )(meta, queries, kv, old)


def own_head_keys_values(keys, values, groups):
    rows = keys.shape[0]
    both = jnp.concatenate(
        [
            keys.reshape(rows, KEY_VALUE_HEADS, HEAD_SIZE),
            values.reshape(rows, KEY_VALUE_HEADS, HEAD_SIZE),
        ],
        axis=2,
    )
    both = jnp.repeat(both, groups // KEY_VALUE_HEADS, axis=1)
    return lax.all_to_all(
        both.reshape(rows, groups * 2 * HEAD_SIZE), "ka", split_axis=1, concat_axis=0, tiled=True
    )


def collect_copies(z, me, column, own_rows, other_rows, slabs, left, right, sems, start=0):
    rows, depth = left.shape[0] // 2, left.shape[1] // 4

    def left_copy(target, slot, side):
        source = (own_rows, other_rows)[side][slot]
        return pltpu.make_async_copy(
            source.at[:, pl.ds(column, depth)],
            left.at[pl.ds(side * rows, rows), pl.ds(target * depth, depth)],
            sems.at[target, side],
        )

    def slab_copy(target, slot):
        width = right.shape[1]
        source = slabs[slot]
        if source.shape[1] != width:
            source = source.at[:, pl.ds(start, width)]
        return pltpu.make_async_copy(
            source, right.at[pl.ds(target * depth, depth), :], sems.at[target, 2]
        )

    for target in range(4):
        if own_rows is not None:
            slot_here = jnp.bitwise_xor(me, target)
            for slot in range(4):

                @pl.when(slot_here == slot)
                def _(slot=slot):
                    left_copy(target, slot, 0).start()
                    left_copy(target, slot, 1).start()

        if slabs is not None:
            for position in range(4):

                @pl.when(z == position)
                def _(position=position):
                    distance = target - position
                    slab_copy(target, -distance if distance <= 0 else 3 + distance).start()

    def wait():
        for target in range(4):
            if own_rows is not None:
                left_copy(target, 0, 0).wait()
                left_copy(target, 0, 1).wait()
            if slabs is not None:
                slab_copy(target, 0).wait()

    return wait


ROW_TILE = 256


def first_kernel(chunks, place_ref, *refs):
    z, y, me = place_ref[0], place_ref[1], place_ref[2]
    own_rows, other_rows, slabs, refs = refs[:4], refs[4:8], refs[8:15], refs[15:]
    outs, spare, left, right, sems, spare_sems = (
        refs[: len(chunks)],
        *refs[len(chunks) : len(chunks) + 5],
    )
    depth = right.shape[0] // 4
    own_column = pl.multiple_of(y * depth, depth)
    other_column = pl.multiple_of((1 - y) * depth, depth)
    wait = collect_copies(z, me, own_column, own_rows, other_rows, slabs, left, right, sems)
    wait_spare = collect_copies(
        z, me, other_column, own_rows, other_rows, None, spare, None, spare_sems
    )
    wait()

    def rows_tile(step, carry):
        at = pl.ds(pl.multiple_of(step * ROW_TILE, ROW_TILE), ROW_TILE)
        product = jnp.dot(left[at, :], right[...], preferred_element_type=jnp.float32)
        start = 0
        for out, chunk in zip(outs, chunks):
            out[at, :] = product[:, start : start + chunk]
            start += chunk
        return carry

    lax.fori_loop(0, left.shape[0] // ROW_TILE, rows_tile, 0)
    wait_spare()


def rest_kernel(start, place_ref, left, base_ref, *refs):
    slabs, (own_out, other_out, right, sems) = refs[:7], refs[7:]
    rows = own_out.shape[0]
    wait = collect_copies(
        place_ref[0], place_ref[2], 0, None, None, slabs, left, right, sems, start
    )
    wait()

    def rows_tile(step, carry):
        for out, offset in ((own_out, 0), (other_out, rows)):
            at = pl.ds(pl.multiple_of(step * ROW_TILE + offset, ROW_TILE), ROW_TILE)
            product = jnp.dot(left[at, :], right[...], preferred_element_type=jnp.float32)
            out[pl.ds(pl.multiple_of(step * ROW_TILE, ROW_TILE), ROW_TILE), :] = (
                product + base_ref[at, :]
            ).astype(jnp.bfloat16)
        return carry

    lax.fori_loop(0, rows // ROW_TILE, rows_tile, 0)


IN_HBM = pl.BlockSpec(memory_space=pltpu.HBM)
IN_VMEM = pl.BlockSpec(memory_space=pltpu.VMEM)
IN_SMEM = pl.BlockSpec(memory_space=pltpu.SMEM)


def first_product(where, own_rows, other_rows, slabs, chunks):
    rows = own_rows[0].shape[0]
    depth, columns = slabs[0].shape
    return pl.pallas_call(
        functools.partial(first_kernel, chunks),
        out_shape=[jax.ShapeDtypeStruct((2 * rows, chunk), jnp.float32) for chunk in chunks]
        + [jax.ShapeDtypeStruct((2 * rows, 4 * depth), jnp.bfloat16)],
        in_specs=[IN_SMEM] + [IN_HBM] * 15,
        out_specs=[IN_VMEM] * (len(chunks) + 1),
        scratch_shapes=[
            pltpu.VMEM((2 * rows, 4 * depth), jnp.bfloat16),
            pltpu.VMEM((4 * depth, columns), jnp.bfloat16),
            pltpu.SemaphoreType.DMA((4, 3)),
            pltpu.SemaphoreType.DMA((4, 2)),
        ],
        compiler_params=pltpu.CompilerParams(vmem_limit_bytes=14 << 20),
        cost_estimate=pl.CostEstimate(
            flops=2 * 2 * rows * 4 * depth * columns,
            transcendentals=0,
            bytes_accessed=2 * (4 * rows * 4 * depth + 4 * depth * columns) + 8 * rows * columns,
        ),
        name="first_product",
    )(where, *own_rows, *other_rows, *slabs)


def rest_product(where, left, base, slabs, start):
    rows = left.shape[0] // 2
    depth = slabs[0].shape[0]
    columns = base.shape[1]
    return pl.pallas_call(
        functools.partial(rest_kernel, start),
        out_shape=[jax.ShapeDtypeStruct((rows, columns), jnp.bfloat16)] * 2,
        in_specs=[IN_SMEM, IN_VMEM, IN_VMEM] + [IN_HBM] * 7,
        out_specs=[IN_VMEM] * 2,
        scratch_shapes=[
            pltpu.VMEM((4 * depth, columns), jnp.bfloat16),
            pltpu.SemaphoreType.DMA((4, 3)),
        ],
        compiler_params=pltpu.CompilerParams(vmem_limit_bytes=8 << 20),
        cost_estimate=pl.CostEstimate(
            flops=2 * 2 * rows * 4 * depth * columns,
            transcendentals=0,
            bytes_accessed=2 * 4 * depth * columns + 8 * rows * columns,
        ),
        name="rest_product",
    )(where, left, base, *slabs)


UP = [[(i, i + 2) for i in range(2 * s, 6)] for s in range(3)]
DOWN = [[(i + 2, i) for i in range(6 - 2 * s)] for s in range(3)]
ACROSS_Y = [(i, i ^ 1) for i in range(8)]
ACROSS_X = [(i, i ^ 2) for i in range(4)]
ACROSS_CORE = [(i, i ^ 1) for i in range(4)]


def project(where, wo, inputs, attend_with):
    y = where[1]
    depth, columns = wo.shape
    half = columns // 2
    chunks = (half * 5 // 8, half // 4, half // 8)
    starts = (0, chunks[0], chunks[0] + chunks[1])

    def up(piece, hop):
        return lax.ppermute(piece, "pb", UP[hop])

    def down(piece, hop):
        return lax.ppermute(piece, "pb", DOWN[hop])

    def other_core(piece):
        return lax.ppermute(piece, "ka", ACROSS_CORE)

    kept = lax.dynamic_slice(wo, (0, y * half), (depth, half))
    given = lax.dynamic_slice(wo, (0, (1 - y) * half), (depth, half))
    taken = lax.ppermute(given, "pb", ACROSS_Y)
    kept_up, kept_down = [up(kept, 0)], [down(kept, 0)]
    taken_up, taken_down = [up(taken, 0)], [down(taken, 0)]
    kept_up.append(up(kept_up[0], 1))
    kept_down.append(down(kept_down[0], 1))
    inputs, taken_up[0], taken_down[0] = lax.optimization_barrier(
        (inputs, taken_up[0], taken_down[0])
    )
    taken_up.append(up(taken_up[0], 1))
    taken_down.append(down(taken_down[0], 1))
    attn = attend_with(inputs)
    attn, kept_up[1], kept_down[1] = lax.optimization_barrier((attn, kept_up[1], kept_down[1]))
    kept_up.append(up(kept_up[1], 2))
    kept_down.append(down(kept_down[1], 2))
    across_y = lax.ppermute(attn, "pb", ACROSS_Y)
    across_x = lax.ppermute(attn, "ka", ACROSS_X)
    across_y, across_x, taken_up[1], taken_down[1] = lax.optimization_barrier(
        (across_y, across_x, taken_up[1], taken_down[1])
    )
    last = []
    for chunk, start in zip(chunks, starts):
        piece = [taken_up[1][:, start : start + chunk], taken_down[1][:, start : start + chunk]]
        last.append((up(piece[0], 2), down(piece[1], 2)))
    corner = lax.ppermute(across_y, "ka", ACROSS_X)
    own_rows = [attn, other_core(attn), across_x, other_core(across_x)]
    other_rows = [across_y, other_core(across_y), corner, other_core(corner)]
    *bases, left = first_product(
        where, own_rows, other_rows, [kept] + kept_up + kept_down, chunks
    )
    own_out, received = [], []
    for base, start, (last_up, last_down) in zip(bases, starts, last):
        slabs = [taken] + taken_up + [last_up] + taken_down + [last_down]
        own, other = rest_product(where, left, base, slabs, start)
        own_out.append(own)
        received.append(lax.ppermute(other, "pb", ACROSS_Y))
    first_half = [jnp.where(y == 0, a, b) for a, b in zip(own_out, received)]
    second_half = [jnp.where(y == 0, b, a) for a, b in zip(own_out, received)]
    return jnp.concatenate(first_half + second_half, axis=1)


def shards(queries, keys, values, block_ids, counts, refresh, cached_attn, wo):
    groups = lax.axis_size("ka")
    pb_size = lax.axis_size("pb")
    me = lax.axis_index("ka")
    kv = own_head_keys_values(keys, values, groups)
    meta = jnp.concatenate([counts[0], refresh[0], block_ids[0, 0]])
    inputs = (meta, queries[0], kv, cached_attn[0])
    if pb_size == 8 and groups == 4:
        pb = lax.axis_index("pb")
        where = jnp.stack([pb // 2, pb % 2, me]).astype(jnp.int32)
        mixed = project(where, wo, inputs, lambda values: attend(*values))
    else:
        attn_full = lax.all_gather(attend(*inputs), "ka", axis=1, tiled=True)
        mixed = jnp.dot(
            attn_full, lax.all_gather(wo, "pb", axis=0, tiled=True), preferred_element_type=jnp.float32
        ).astype(jnp.bfloat16)
    return mixed[None]


def solution(mesh):
    placed = (
        P(None, "pb", "ka"),
        P("ka", None),
        P("ka", None),
        P(None, "pb", None),
        P(None, "pb"),
        P(None, "pb"),
        P(None, "pb", "ka"),
        P("pb", "ka"),
    )
    return jax.shard_map(
        shards, mesh=mesh, in_specs=placed, out_specs=P(None, "pb", "ka"), check_vma=False
    )
```

```python
import functools
import math

import jax
import jax.numpy as jnp
from jax import lax
from jax.experimental import pallas as pl
from jax.experimental.pallas import tpu as pltpu
from jax.sharding import PartitionSpec as P

HEAD_SIZE = 128
QUERY_HEAD_COUNT = 32
KEY_VALUE_HEADS = 4
QUERY_BLOCK_SIZE = 512
KEY_BLOCK_TOKENS = 128
RATIO = QUERY_HEAD_COUNT // KEY_VALUE_HEADS
LOWEST = -1e30
EXP2_SCALE = math.log2(math.e) / math.sqrt(HEAD_SIZE)


GROUP = 4


def attention_kernel(heads, meta_ref, q_ref, kv_ref, old_ref, out_ref, peak_ref, denom_ref, acc_ref):
    live = meta_ref[0]
    flag = meta_ref[1]

    @pl.when(flag <= 0)
    def _():
        out_ref[...] = old_ref[...]

    @pl.when(flag > 0)
    def _():
        peak_ref[...] = jnp.full_like(peak_ref, LOWEST)
        denom_ref[...] = jnp.zeros_like(denom_ref)
        acc_ref[...] = jnp.zeros_like(acc_ref)

        def group(step, carry):
            tiles, biases = [], []
            for member in range(GROUP):
                slot = step * GROUP + member
                if member > 0:
                    present = slot < live
                    block = jnp.where(
                        present, meta_ref[2 + jnp.minimum(slot, meta_ref.shape[0] - 3)], 0
                    )
                    biases.append(jnp.where(present, 0.0, LOWEST).astype(jnp.float32))
                else:
                    block = meta_ref[2 + slot]
                    biases.append(None)
                row = pl.multiple_of(block * KEY_BLOCK_TOKENS, KEY_BLOCK_TOKENS)
                tiles.append(kv_ref[pl.ds(row, KEY_BLOCK_TOKENS), :])
            tile = jnp.concatenate(tiles, axis=0)
            key_tile = tile[:, :HEAD_SIZE]
            value_tile = tile[:, HEAD_SIZE:].T
            value_tile = jnp.concatenate(
                [value_tile, jnp.ones((16, value_tile.shape[1]), jnp.bfloat16)], axis=0
            )
            for head in range(heads):
                query = q_ref[:, head * HEAD_SIZE : (head + 1) * HEAD_SIZE]
                scores = lax.dot_general(
                    key_tile, query, (((1,), (1,)), ((), ())), preferred_element_type=jnp.float32
                )
                parts = [
                    scores[member * KEY_BLOCK_TOKENS : (member + 1) * KEY_BLOCK_TOKENS]
                    for member in range(GROUP)
                ]
                parts = [p if b is None else p + b for p, b in zip(parts, biases)]
                top = functools.reduce(jnp.maximum, parts)
                old_peak = peak_ref[head]
                peak = jnp.maximum(old_peak, jnp.max(top, axis=0, keepdims=True))
                decay = jnp.exp2((old_peak - peak) * EXP2_SCALE)
                parts = [jnp.exp2((p - peak) * EXP2_SCALE) for p in parts]
                peak_ref[head] = peak
                weights = jnp.concatenate([p.astype(jnp.bfloat16) for p in parts], axis=0)
                update = lax.dot_general(
                    value_tile, weights, (((1,), (0,)), ((), ())), preferred_element_type=jnp.float32
                )
                denom_ref[head] = denom_ref[head] * decay + update[HEAD_SIZE : HEAD_SIZE + 1]
                acc_ref[head] = acc_ref[head] * decay + update[:HEAD_SIZE]
            return carry

        lax.fori_loop(0, (live + GROUP - 1) // GROUP, group, 0)
        for head in range(heads):
            result = acc_ref[head] / denom_ref[head]
            out_ref[:, head * HEAD_SIZE : (head + 1) * HEAD_SIZE] = result.T.astype(jnp.bfloat16)


def attend(meta, queries, kv, old):
    rows, width = queries.shape
    heads = width // HEAD_SIZE
    whole = pl.BlockSpec(memory_space=pltpu.VMEM)
    return pl.pallas_call(
        functools.partial(attention_kernel, heads),
        out_shape=jax.ShapeDtypeStruct((rows, width), jnp.bfloat16),
        in_specs=[pl.BlockSpec(memory_space=pltpu.SMEM), whole, whole, whole],
        out_specs=whole,
        scratch_shapes=[
            pltpu.VMEM((heads, 1, rows), jnp.float32),
            pltpu.VMEM((heads, 1, rows), jnp.float32),
            pltpu.VMEM((heads, HEAD_SIZE, rows), jnp.float32),
        ],
        compiler_params=pltpu.CompilerParams(vmem_limit_bytes=16 << 20),
        cost_estimate=pl.CostEstimate(
            flops=4 * rows * width * 16 * KEY_BLOCK_TOKENS,
            transcendentals=rows * heads * 16 * KEY_BLOCK_TOKENS,
            bytes_accessed=2 * (3 * rows * width + kv.size),
        ),
        name="attend",
    )(meta, queries, kv, old)


def own_head_keys_values(keys, values, groups):
    rows = keys.shape[0]
    both = jnp.concatenate(
        [
            keys.reshape(rows, KEY_VALUE_HEADS, HEAD_SIZE),
            values.reshape(rows, KEY_VALUE_HEADS, HEAD_SIZE),
        ],
        axis=2,
    )
    both = jnp.repeat(both, groups // KEY_VALUE_HEADS, axis=1)
    return lax.all_to_all(
        both.reshape(rows, groups * 2 * HEAD_SIZE), "ka", split_axis=1, concat_axis=0, tiled=True
    )


def collect_copies(z, me, column, own_rows, other_rows, slabs, left, right, sems, start=0):
    rows, depth = left.shape[0] // 2, left.shape[1] // 4

    def left_copy(target, slot, side):
        source = (own_rows, other_rows)[side][slot]
        return pltpu.make_async_copy(
            source.at[:, pl.ds(column, depth)],
            left.at[pl.ds(side * rows, rows), pl.ds(target * depth, depth)],
            sems.at[target, side],
        )

    def slab_copy(target, slot):
        width = right.shape[1]
        source = slabs[slot]
        if source.shape[1] != width:
            source = source.at[:, pl.ds(start, width)]
        return pltpu.make_async_copy(
            source, right.at[pl.ds(target * depth, depth), :], sems.at[target, 2]
        )

    for target in range(4):
        if own_rows is not None:
            slot_here = jnp.bitwise_xor(me, target)
            for slot in range(4):

                @pl.when(slot_here == slot)
                def _(slot=slot):
                    left_copy(target, slot, 0).start()
                    left_copy(target, slot, 1).start()

        if slabs is not None:
            for position in range(4):

                @pl.when(z == position)
                def _(position=position):
                    distance = target - position
                    slab_copy(target, -distance if distance <= 0 else 3 + distance).start()

    def wait():
        for target in range(4):
            if own_rows is not None:
                left_copy(target, 0, 0).wait()
                left_copy(target, 0, 1).wait()
            if slabs is not None:
                slab_copy(target, 0).wait()

    return wait


ROW_TILE = 256


def first_kernel(chunks, place_ref, *refs):
    z, y, me = place_ref[0], place_ref[1], place_ref[2]
    own_rows, other_rows, slabs, refs = refs[:4], refs[4:8], refs[8:15], refs[15:]
    outs, spare, left, right, sems, spare_sems = (
        refs[: len(chunks)],
        *refs[len(chunks) : len(chunks) + 5],
    )
    depth = right.shape[0] // 4
    own_column = pl.multiple_of(y * depth, depth)
    other_column = pl.multiple_of((1 - y) * depth, depth)
    wait = collect_copies(z, me, own_column, own_rows, other_rows, slabs, left, right, sems)
    wait_spare = collect_copies(
        z, me, other_column, own_rows, other_rows, None, spare, None, spare_sems
    )
    wait()

    def rows_tile(step, carry):
        at = pl.ds(pl.multiple_of(step * ROW_TILE, ROW_TILE), ROW_TILE)
        product = jnp.dot(left[at, :], right[...], preferred_element_type=jnp.float32)
        start = 0
        for out, chunk in zip(outs, chunks):
            out[at, :] = product[:, start : start + chunk]
            start += chunk
        return carry

    lax.fori_loop(0, left.shape[0] // ROW_TILE, rows_tile, 0)
    wait_spare()


def rest_kernel(start, place_ref, left_ref, base_ref, *refs):
    slabs, (own_out, other_out, left, right, sems, left_sem) = refs[:7], refs[7:]
    rows = own_out.shape[0]
    left_copy = pltpu.make_async_copy(left_ref, left, left_sem)
    left_copy.start()
    wait = collect_copies(
        place_ref[0], place_ref[2], 0, None, None, slabs, left, right, sems, start
    )
    left_copy.wait()
    wait()

    def rows_tile(step, carry):
        for out, offset in ((own_out, 0), (other_out, rows)):
            at = pl.ds(pl.multiple_of(step * ROW_TILE + offset, ROW_TILE), ROW_TILE)
            product = jnp.dot(left[at, :], right[...], preferred_element_type=jnp.float32)
            out[pl.ds(pl.multiple_of(step * ROW_TILE, ROW_TILE), ROW_TILE), :] = (
                product + base_ref[at, :]
            ).astype(jnp.bfloat16)
        return carry

    lax.fori_loop(0, rows // ROW_TILE, rows_tile, 0)


IN_HBM = pl.BlockSpec(memory_space=pltpu.HBM)
IN_VMEM = pl.BlockSpec(memory_space=pltpu.VMEM)
IN_SMEM = pl.BlockSpec(memory_space=pltpu.SMEM)


SMALL_COST = pl.CostEstimate(flops=1 << 20, transcendentals=0, bytes_accessed=1 << 20)


def first_product(where, own_rows, other_rows, slabs, chunks):
    rows = own_rows[0].shape[0]
    depth, columns = slabs[0].shape
    return pl.pallas_call(
        functools.partial(first_kernel, chunks),
        out_shape=[jax.ShapeDtypeStruct((2 * rows, chunk), jnp.float32) for chunk in chunks]
        + [jax.ShapeDtypeStruct((2 * rows, 4 * depth), jnp.bfloat16)],
        in_specs=[IN_SMEM] + [IN_HBM] * 15,
        out_specs=[IN_VMEM] * (len(chunks) + 1),
        scratch_shapes=[
            pltpu.VMEM((2 * rows, 4 * depth), jnp.bfloat16),
            pltpu.VMEM((4 * depth, columns), jnp.bfloat16),
            pltpu.SemaphoreType.DMA((4, 3)),
            pltpu.SemaphoreType.DMA((4, 2)),
        ],
        compiler_params=pltpu.CompilerParams(vmem_limit_bytes=14 << 20),
        cost_estimate=SMALL_COST,
        name="first_product",
    )(where, *[pltpu.with_memory_space_constraint(x, pltpu.HBM) for x in (*own_rows, *other_rows, *slabs)])


def rest_product(where, left, base, slabs, start):
    rows = left.shape[0] // 2
    depth = slabs[0].shape[0]
    columns = base.shape[1]
    return pl.pallas_call(
        functools.partial(rest_kernel, start),
        out_shape=[jax.ShapeDtypeStruct((rows, columns), jnp.bfloat16)] * 2,
        in_specs=[IN_SMEM, IN_HBM, IN_VMEM] + [IN_HBM] * 7,
        out_specs=[IN_VMEM] * 2,
        scratch_shapes=[
            pltpu.VMEM((2 * rows, 4 * depth), jnp.bfloat16),
            pltpu.VMEM((4 * depth, columns), jnp.bfloat16),
            pltpu.SemaphoreType.DMA((4, 3)),
            pltpu.SemaphoreType.DMA,
        ],
        compiler_params=pltpu.CompilerParams(vmem_limit_bytes=10 << 20),
        cost_estimate=SMALL_COST,
        name="rest_product",
    )(where, pltpu.with_memory_space_constraint(left, pltpu.HBM), base, *[pltpu.with_memory_space_constraint(x, pltpu.HBM) for x in slabs])


UP = [[(i, i + 2) for i in range(2 * s, 6)] for s in range(3)]
DOWN = [[(i + 2, i) for i in range(6 - 2 * s)] for s in range(3)]
ACROSS_Y = [(i, i ^ 1) for i in range(8)]
ACROSS_X = [(i, i ^ 2) for i in range(4)]
ACROSS_BOTH = [(i, i ^ 6) for i in range(32)]
ACROSS_CORE = [(i, i ^ 1) for i in range(4)]


def project(where, wo, inputs, attend_with):
    y = where[1]
    depth, columns = wo.shape
    half = columns // 2
    chunks = (half * 3 // 8, half * 3 // 8, half // 4)
    starts = (0, chunks[0], chunks[0] + chunks[1])

    def up(piece, hop):
        return lax.ppermute(piece, "pb", UP[hop])

    def down(piece, hop):
        return lax.ppermute(piece, "pb", DOWN[hop])

    def other_core(piece):
        return lax.ppermute(piece, "ka", ACROSS_CORE)

    kept = lax.dynamic_slice(wo, (0, y * half), (depth, half))
    given = lax.dynamic_slice(wo, (0, (1 - y) * half), (depth, half))
    taken = lax.ppermute(given, "pb", ACROSS_Y)
    kept_up, kept_down = [up(kept, 0)], [down(kept, 0)]
    taken_up, taken_down = [up(taken, 0)], [down(taken, 0)]
    for hop in (1, 2):
        kept_up.append(up(kept_up[-1], hop))
        kept_down.append(down(kept_down[-1], hop))
    taken_up.append(up(taken_up[0], 1))
    taken_down.append(down(taken_down[0], 1))
    last = []
    for chunk, start in zip(chunks, starts):
        piece = [taken_up[1][:, start : start + chunk], taken_down[1][:, start : start + chunk]]
        last.append((up(piece[0], 2), down(piece[1], 2)))
    attn = attend_with(inputs)
    across_y = lax.ppermute(attn, "pb", ACROSS_Y)
    across_x = lax.ppermute(attn, "ka", ACROSS_X)
    corner = lax.ppermute(attn, ("pb", "ka"), ACROSS_BOTH)
    own_rows = [attn, other_core(attn), across_x, other_core(across_x)]
    other_rows = [across_y, other_core(across_y), corner, other_core(corner)]
    *bases, left = first_product(
        where, own_rows, other_rows, [kept] + kept_up + kept_down, chunks
    )
    own_out, received = [], []
    for index, (base, start) in enumerate(zip(bases, starts)):
        last_up, last_down = last[index]
        slabs = [taken] + taken_up + [last_up] + taken_down + [last_down]
        own, other = rest_product(where, left, base, slabs, start)
        if not own_out:
            other, last[1], last[2] = lax.optimization_barrier((other, last[1], last[2]))
        own_out.append(own)
        received.append(lax.ppermute(other, "pb", ACROSS_Y))
    first_half = [jnp.where(y == 0, a, b) for a, b in zip(own_out, received)]
    second_half = [jnp.where(y == 0, b, a) for a, b in zip(own_out, received)]
    return jnp.concatenate(first_half + second_half, axis=1)


def shards(queries, keys, values, block_ids, counts, refresh, cached_attn, wo):
    groups = lax.axis_size("ka")
    pb_size = lax.axis_size("pb")
    me = lax.axis_index("ka")
    kv = own_head_keys_values(keys, values, groups)
    meta = jnp.concatenate([counts[0], refresh[0], block_ids[0, 0]])
    inputs = (meta, queries[0], kv, cached_attn[0])
    if pb_size == 8 and groups == 4:
        pb = lax.axis_index("pb")
        where = jnp.stack([pb // 2, pb % 2, me]).astype(jnp.int32)
        mixed = project(where, wo, inputs, lambda values: attend(*values))
    else:
        attn_full = lax.all_gather(attend(*inputs), "ka", axis=1, tiled=True)
        mixed = jnp.dot(
            attn_full, lax.all_gather(wo, "pb", axis=0, tiled=True), preferred_element_type=jnp.float32
        ).astype(jnp.bfloat16)
    return mixed[None]


def solution(mesh):
    placed = (
        P(None, "pb", "ka"),
        P("ka", None),
        P("ka", None),
        P(None, "pb", None),
        P(None, "pb"),
        P(None, "pb"),
        P(None, "pb", "ka"),
        P("pb", "ka"),
    )
    return jax.shard_map(
        shards, mesh=mesh, in_specs=placed, out_specs=P(None, "pb", "ka"), check_vma=False
    )
```

```python
import functools
import math

import jax
import jax.numpy as jnp
from jax import lax
from jax.experimental import pallas as pl
from jax.experimental.pallas import tpu as pltpu
from jax.sharding import PartitionSpec as P

HEAD_SIZE = 128
QUERY_HEAD_COUNT = 32
KEY_VALUE_HEADS = 4
QUERY_BLOCK_SIZE = 512
KEY_BLOCK_TOKENS = 128
RATIO = QUERY_HEAD_COUNT // KEY_VALUE_HEADS
LOWEST = -1e30
EXP2_SCALE = math.log2(math.e) / math.sqrt(HEAD_SIZE)


GROUP = 4


def attention_kernel(heads, slots, meta_ref, q_hbm, old_hbm, *refs):
    kv_parts, (out_ref, q_ref, kv_ref, peak_ref, denom_ref, acc_ref, sems) = refs[:-7], refs[-7:]
    live = meta_ref[0]
    flag = meta_ref[1]

    @pl.when(flag <= 0)
    def _():
        copy = pltpu.make_async_copy(old_hbm, out_ref, sems.at[0])
        copy.start()
        copy.wait()

    @pl.when(flag > 0)
    def _():
        copies = [pltpu.make_async_copy(q_hbm, q_ref, sems.at[0])]
        for index, part in enumerate(kv_parts):
            rows = part.shape[0]
            start = pl.multiple_of(meta_ref[2 + slots + index] * rows, rows)
            copies.append(
                pltpu.make_async_copy(part, kv_ref.at[pl.ds(start, rows), :], sems.at[1 + index])
            )
        for copy in copies:
            copy.start()
        peak_ref[...] = jnp.full_like(peak_ref, LOWEST)
        denom_ref[...] = jnp.zeros_like(denom_ref)
        acc_ref[...] = jnp.zeros_like(acc_ref)
        for copy in copies:
            copy.wait()

        def group(step, carry):
            tiles, biases = [], []
            for member in range(GROUP):
                slot = step * GROUP + member
                if member > 0:
                    present = slot < live
                    block = jnp.where(
                        present, meta_ref[2 + jnp.minimum(slot, slots - 1)], 0
                    )
                    biases.append(jnp.where(present, 0.0, LOWEST).astype(jnp.float32))
                else:
                    block = meta_ref[2 + slot]
                    biases.append(None)
                row = pl.multiple_of(block * KEY_BLOCK_TOKENS, KEY_BLOCK_TOKENS)
                tiles.append(kv_ref[pl.ds(row, KEY_BLOCK_TOKENS), :])
            tile = jnp.concatenate(tiles, axis=0)
            key_tile = tile[:, :HEAD_SIZE]
            value_tile = tile[:, HEAD_SIZE:].T
            value_tile = jnp.concatenate(
                [value_tile, jnp.ones((16, value_tile.shape[1]), jnp.bfloat16)], axis=0
            )
            for head in range(heads):
                query = q_ref[:, head * HEAD_SIZE : (head + 1) * HEAD_SIZE]
                scores = lax.dot_general(
                    key_tile, query, (((1,), (1,)), ((), ())), preferred_element_type=jnp.float32
                )
                parts = [
                    scores[member * KEY_BLOCK_TOKENS : (member + 1) * KEY_BLOCK_TOKENS]
                    for member in range(GROUP)
                ]
                parts = [p if b is None else p + b for p, b in zip(parts, biases)]
                top = functools.reduce(jnp.maximum, parts)
                old_peak = peak_ref[head]
                peak = jnp.maximum(old_peak, jnp.max(top, axis=0, keepdims=True))
                decay = jnp.exp2((old_peak - peak) * EXP2_SCALE)
                parts = [jnp.exp2((p - peak) * EXP2_SCALE) for p in parts]
                peak_ref[head] = peak
                weights = jnp.concatenate([p.astype(jnp.bfloat16) for p in parts], axis=0)
                update = lax.dot_general(
                    value_tile, weights, (((1,), (0,)), ((), ())), preferred_element_type=jnp.float32
                )
                denom_ref[head] = denom_ref[head] * decay + update[HEAD_SIZE : HEAD_SIZE + 1]
                acc_ref[head] = acc_ref[head] * decay + update[:HEAD_SIZE]
            return carry

        lax.fori_loop(0, (live + GROUP - 1) // GROUP, group, 0)
        for head in range(heads):
            result = acc_ref[head] / denom_ref[head]
            out_ref[:, head * HEAD_SIZE : (head + 1) * HEAD_SIZE] = result.T.astype(jnp.bfloat16)


def attend(block_list, live, flag, queries, old, kv_parts, places):
    rows, width = queries.shape
    heads = width // HEAD_SIZE
    slots = block_list.shape[0]
    meta = jnp.concatenate([live[None], flag[None], block_list, *[p[None] for p in places]])
    in_hbm = pl.BlockSpec(memory_space=pltpu.HBM)
    return pl.pallas_call(
        functools.partial(attention_kernel, heads, slots),
        out_shape=jax.ShapeDtypeStruct((rows, width), jnp.bfloat16),
        in_specs=[pl.BlockSpec(memory_space=pltpu.SMEM)] + [in_hbm] * (2 + len(kv_parts)),
        out_specs=pl.BlockSpec(memory_space=pltpu.VMEM),
        scratch_shapes=[
            pltpu.VMEM((rows, width), jnp.bfloat16),
            pltpu.VMEM((sum(p.shape[0] for p in kv_parts), 2 * HEAD_SIZE), jnp.bfloat16),
            pltpu.VMEM((heads, 1, rows), jnp.float32),
            pltpu.VMEM((heads, 1, rows), jnp.float32),
            pltpu.VMEM((heads, HEAD_SIZE, rows), jnp.float32),
            pltpu.SemaphoreType.DMA((1 + len(kv_parts),)),
        ],
        compiler_params=pltpu.CompilerParams(vmem_limit_bytes=24 << 20),
        cost_estimate=pl.CostEstimate(
            flops=1 << 20, transcendentals=0, bytes_accessed=1 << 20
        ),
        name="attend",
    )(
        meta,
        *[
            pltpu.with_memory_space_constraint(x, pltpu.HBM)
            for x in (queries, old, *kv_parts)
        ],
    )


def own_head_keys_values(keys, values):
    groups = lax.axis_size("ka")
    me = lax.axis_index("ka")
    rows = keys.shape[0]
    if groups == KEY_VALUE_HEADS:

        def head_of(device):
            start = (0, device * HEAD_SIZE)
            return jnp.concatenate(
                [lax.dynamic_slice(x, start, (rows, HEAD_SIZE)) for x in (keys, values)], axis=1
            )

        parts, places = [head_of(me)], [me]
        for step in range(1, groups):
            partner = jnp.bitwise_xor(me, step)
            parts.append(
                lax.ppermute(head_of(partner), "ka", [(i, i ^ step) for i in range(groups)])
            )
            places.append(partner)
        return parts, places
    both = jnp.concatenate(
        [
            keys.reshape(rows, KEY_VALUE_HEADS, HEAD_SIZE),
            values.reshape(rows, KEY_VALUE_HEADS, HEAD_SIZE),
        ],
        axis=2,
    )
    both = jnp.repeat(both, groups // KEY_VALUE_HEADS, axis=1)
    everything = lax.all_to_all(
        both.reshape(rows, groups * 2 * HEAD_SIZE), "ka", split_axis=1, concat_axis=0, tiled=True
    )
    return [everything], [jnp.int32(0)]


def ring_of(pb_size):
    if pb_size == 8:
        return [0, 2, 4, 6, 7, 5, 3, 1]
    return list(range(pb_size))


def project_ring(wo, inputs, attend_with):
    pb_size = lax.axis_size("pb")
    depth, columns = wo.shape
    ring = ring_of(pb_size)
    forward = [(ring[i], ring[(i + 1) % pb_size]) for i in range(pb_size)]
    backward = [(b, a) for a, b in forward]
    half = columns // 2
    far = pb_size // 2
    parts = [wo[:, :half], wo[:, half:]]
    inputs, parts[0], parts[1] = lax.optimization_barrier((inputs, parts[0], parts[1]))
    slabs = [[(0, part)] for part in parts]
    moving = [[part, part] for part in parts]
    for hop in range(1, far + 1):
        for part in range(2):
            if hop < far or part == 0:
                moving[part][0] = lax.ppermute(moving[part][0], "pb", forward)
                slabs[part].append((-hop, moving[part][0]))
            if hop < far or part == 1:
                moving[part][1] = lax.ppermute(moving[part][1], "pb", backward)
                slabs[part].append((hop, moving[part][1]))
    attn = attend_with(inputs)
    across = lax.ppermute(attn, "ka", [(i, i ^ 2) for i in range(4)])
    beside = lax.ppermute(attn, "ka", [(i, i ^ 1) for i in range(4)])
    corner = lax.ppermute(across, "ka", [(i, i ^ 1) for i in range(4)])
    pieces = jnp.stack([attn, beside, across, corner])
    per = attn.shape[1] // depth
    around = jnp.asarray(
        [[ring[(ring.index(p) + step) % pb_size] for step in range(pb_size)] for p in range(pb_size)],
        jnp.int32,
    )
    sources = lax.dynamic_slice(around, (lax.axis_index("pb"), 0), (1, pb_size))[0]
    slots = jnp.bitwise_xor(sources // per, lax.axis_index("ka"))
    shifts = (sources % per) * depth
    results = []
    for part in range(2):
        total = None
        for offset, slab in slabs[part]:
            at = offset % pb_size
            left = lax.dynamic_slice(
                pieces, (slots[at], 0, shifts[at]), (1, attn.shape[0], depth)
            )[0]
            term = jnp.dot(left, slab, preferred_element_type=jnp.float32)
            total = term if total is None else total + term
        results.append(total.astype(jnp.bfloat16))
    return jnp.concatenate(results, axis=1)


def shards(queries, keys, values, block_ids, counts, refresh, cached_attn, wo):
    groups = lax.axis_size("ka")

    def attend_with(inputs):
        queries, keys, values, old = inputs
        parts, places = own_head_keys_values(keys, values)
        return attend(block_ids[0, 0], counts[0, 0], refresh[0, 0], queries, old, parts, places)

    inputs = (queries[0], keys, values, cached_attn[0])
    if lax.axis_size("pb") == 8 and groups == 4:
        mixed = project_ring(wo, inputs, attend_with)
    else:
        attn_full = lax.all_gather(attend_with(inputs), "ka", axis=1, tiled=True)
        mixed = jnp.dot(
            attn_full, lax.all_gather(wo, "pb", axis=0, tiled=True), preferred_element_type=jnp.float32
        ).astype(jnp.bfloat16)
    return mixed[None]


def solution(mesh):
    placed = (
        P(None, "pb", "ka"),
        P("ka", None),
        P("ka", None),
        P(None, "pb", None),
        P(None, "pb"),
        P(None, "pb"),
        P(None, "pb", "ka"),
        P("pb", "ka"),
    )
    return jax.shard_map(
        shards, mesh=mesh, in_specs=placed, out_specs=P(None, "pb", "ka"), check_vma=False
    )
```

```python
import functools
import math

import jax
import jax.numpy as jnp
from jax import lax
from jax.experimental import pallas as pl
from jax.experimental.pallas import tpu as pltpu
from jax.sharding import PartitionSpec as P

HEAD_SIZE = 128
QUERY_HEAD_COUNT = 32
KEY_VALUE_HEADS = 4
QUERY_BLOCK_SIZE = 512
KEY_BLOCK_TOKENS = 128
RATIO = QUERY_HEAD_COUNT // KEY_VALUE_HEADS
LOWEST = -1e30
EXP2_SCALE = math.log2(math.e) / math.sqrt(HEAD_SIZE)


GROUP = 4


def attention_kernel(heads, slots, meta_ref, q_hbm, old_hbm, *refs):
    kv_parts, (out_ref, q_ref, kv_ref, peak_ref, denom_ref, acc_ref, sems) = refs[:-7], refs[-7:]
    live = meta_ref[0]
    flag = meta_ref[1]

    @pl.when(flag <= 0)
    def _():
        copy = pltpu.make_async_copy(old_hbm, out_ref, sems.at[0])
        copy.start()
        copy.wait()

    @pl.when(flag > 0)
    def _():
        copies = [pltpu.make_async_copy(q_hbm, q_ref, sems.at[0])]
        for index, part in enumerate(kv_parts):
            rows = part.shape[0]
            start = pl.multiple_of(meta_ref[2 + slots + index] * rows, rows)
            copies.append(
                pltpu.make_async_copy(part, kv_ref.at[pl.ds(start, rows), :], sems.at[1 + index])
            )
        for copy in copies:
            copy.start()
        peak_ref[...] = jnp.full_like(peak_ref, LOWEST)
        denom_ref[...] = jnp.zeros_like(denom_ref)
        acc_ref[...] = jnp.zeros_like(acc_ref)
        for copy in copies:
            copy.wait()

        def group(step, carry):
            tiles, biases = [], []
            for member in range(GROUP):
                slot = step * GROUP + member
                if member > 0:
                    present = slot < live
                    block = jnp.where(
                        present, meta_ref[2 + jnp.minimum(slot, slots - 1)], 0
                    )
                    biases.append(jnp.where(present, 0.0, LOWEST).astype(jnp.float32))
                else:
                    block = meta_ref[2 + slot]
                    biases.append(None)
                row = pl.multiple_of(block * KEY_BLOCK_TOKENS, KEY_BLOCK_TOKENS)
                tiles.append(kv_ref[pl.ds(row, KEY_BLOCK_TOKENS), :])
            tile = jnp.concatenate(tiles, axis=0)
            key_tile = tile[:, :HEAD_SIZE]
            value_tile = tile[:, HEAD_SIZE:].T
            value_tile = jnp.concatenate(
                [value_tile, jnp.ones((16, value_tile.shape[1]), jnp.bfloat16)], axis=0
            )
            for head in range(heads):
                query = q_ref[:, head * HEAD_SIZE : (head + 1) * HEAD_SIZE]
                scores = lax.dot_general(
                    key_tile, query, (((1,), (1,)), ((), ())), preferred_element_type=jnp.float32
                )
                parts = [
                    scores[member * KEY_BLOCK_TOKENS : (member + 1) * KEY_BLOCK_TOKENS]
                    for member in range(GROUP)
                ]
                parts = [p if b is None else p + b for p, b in zip(parts, biases)]
                top = functools.reduce(jnp.maximum, parts)
                old_peak = peak_ref[head]
                peak = jnp.maximum(old_peak, jnp.max(top, axis=0, keepdims=True))
                decay = jnp.exp2((old_peak - peak) * EXP2_SCALE)
                parts = [jnp.exp2((p - peak) * EXP2_SCALE) for p in parts]
                peak_ref[head] = peak
                weights = jnp.concatenate([p.astype(jnp.bfloat16) for p in parts], axis=0)
                update = lax.dot_general(
                    value_tile, weights, (((1,), (0,)), ((), ())), preferred_element_type=jnp.float32
                )
                denom_ref[head] = denom_ref[head] * decay + update[HEAD_SIZE : HEAD_SIZE + 1]
                acc_ref[head] = acc_ref[head] * decay + update[:HEAD_SIZE]
            return carry

        lax.fori_loop(0, (live + GROUP - 1) // GROUP, group, 0)
        for head in range(heads):
            result = acc_ref[head] / denom_ref[head]
            out_ref[:, head * HEAD_SIZE : (head + 1) * HEAD_SIZE] = result.T.astype(jnp.bfloat16)


def attend(block_list, live, flag, queries, old, kv_parts, places):
    rows, width = queries.shape
    heads = width // HEAD_SIZE
    slots = block_list.shape[0]
    meta = jnp.concatenate([live[None], flag[None], block_list, *[p[None] for p in places]])
    in_hbm = pl.BlockSpec(memory_space=pltpu.HBM)
    return pl.pallas_call(
        functools.partial(attention_kernel, heads, slots),
        out_shape=jax.ShapeDtypeStruct((rows, width), jnp.bfloat16),
        in_specs=[pl.BlockSpec(memory_space=pltpu.SMEM)] + [in_hbm] * (2 + len(kv_parts)),
        out_specs=pl.BlockSpec(memory_space=pltpu.VMEM),
        scratch_shapes=[
            pltpu.VMEM((rows, width), jnp.bfloat16),
            pltpu.VMEM((sum(p.shape[0] for p in kv_parts), 2 * HEAD_SIZE), jnp.bfloat16),
            pltpu.VMEM((heads, 1, rows), jnp.float32),
            pltpu.VMEM((heads, 1, rows), jnp.float32),
            pltpu.VMEM((heads, HEAD_SIZE, rows), jnp.float32),
            pltpu.SemaphoreType.DMA((1 + len(kv_parts),)),
        ],
        compiler_params=pltpu.CompilerParams(vmem_limit_bytes=24 << 20),
        cost_estimate=pl.CostEstimate(
            flops=1 << 20, transcendentals=0, bytes_accessed=1 << 20
        ),
        name="attend",
    )(
        meta,
        *[
            pltpu.with_memory_space_constraint(x, pltpu.HBM)
            for x in (queries, old, *kv_parts)
        ],
    )


def own_head_keys_values(keys, values):
    groups = lax.axis_size("ka")
    me = lax.axis_index("ka")
    rows = keys.shape[0]
    if groups == KEY_VALUE_HEADS:

        def head_of(device):
            start = (0, device * HEAD_SIZE)
            return jnp.concatenate(
                [lax.dynamic_slice(x, start, (rows, HEAD_SIZE)) for x in (keys, values)], axis=1
            )

        parts, places = [head_of(me)], [me]
        for step in range(1, groups):
            partner = jnp.bitwise_xor(me, step)
            parts.append(
                lax.ppermute(head_of(partner), "ka", [(i, i ^ step) for i in range(groups)])
            )
            places.append(partner)
        return parts, places
    both = jnp.concatenate(
        [
            keys.reshape(rows, KEY_VALUE_HEADS, HEAD_SIZE),
            values.reshape(rows, KEY_VALUE_HEADS, HEAD_SIZE),
        ],
        axis=2,
    )
    both = jnp.repeat(both, groups // KEY_VALUE_HEADS, axis=1)
    everything = lax.all_to_all(
        both.reshape(rows, groups * 2 * HEAD_SIZE), "ka", split_axis=1, concat_axis=0, tiled=True
    )
    return [everything], [jnp.int32(0)]


def ring_of(pb_size):
    if pb_size == 8:
        return [0, 2, 4, 6, 7, 5, 3, 1]
    return list(range(pb_size))


ROW_TILE = 128


def ring_product_kernel(steps, has_base, last, where_ref, *refs):
    count = len(steps)
    blocks, slabs, refs = refs[:4], (refs[4 : 4 + count], refs[4 + count : 4 + 2 * count]), refs[4 + 2 * count :]
    if has_base:
        base_ref, refs = refs[0], refs[1:]
    out_ref, left, right, block_sems, slab_sems = refs[:5]
    rows, depth = left.shape[0], right.shape[1] // count
    per = blocks[0].shape[1] // depth
    me = where_ref[where_ref.shape[0] - 1]

    def block_copy(index, slot, shift):
        return pltpu.make_async_copy(
            blocks[slot].at[:, pl.ds(shift, depth)],
            left.at[:, pl.ds(index * depth, depth)],
            block_sems.at[index],
        )

    def slab_copy(half, index):
        return pltpu.make_async_copy(
            slabs[half][index],
            right.at[half, pl.ds(index * depth, depth), :],
            slab_sems.at[half, index],
        )

    for index, step in enumerate(steps):
        source = where_ref[step]
        slot_here = jnp.bitwise_xor(source // per, me)
        shift = pl.multiple_of((source % per) * depth, depth)
        for slot in range(4):

            @pl.when(slot_here == slot)
            def _(slot=slot):
                block_copy(index, slot, shift).start()

    for half in range(2):
        for index in range(count):
            slab_copy(half, index).start()
    for index in range(count):
        block_copy(index, 0, 0).wait()
    half_columns = right.shape[2]
    if last:
        staged, out_sems = refs[5:]
    for half in range(2):
        columns = pl.ds(half * half_columns, half_columns)
        for index in range(count):
            slab_copy(half, index).wait()

        def rows_tile(step, carry):
            at = pl.ds(pl.multiple_of(step * ROW_TILE, ROW_TILE), ROW_TILE)
            product = jnp.dot(left[at, :], right[half], preferred_element_type=jnp.float32)
            if has_base:
                product = product + base_ref[at, columns]
            if last:
                staged[at, columns] = product.astype(jnp.bfloat16)
            else:
                out_ref[at, columns] = product
            return carry

        lax.fori_loop(0, rows // ROW_TILE, rows_tile, 0)
        if last:
            pltpu.make_async_copy(
                staged.at[:, columns], out_ref.at[:, columns], out_sems.at[half]
            ).start()
    if last:
        for half in range(2):
            columns = pl.ds(half * half_columns, half_columns)
            pltpu.make_async_copy(
                staged.at[:, columns], out_ref.at[:, columns], out_sems.at[half]
            ).wait()


def ring_product(where, blocks, steps, slabs, base, last):
    count = len(steps)
    rows = blocks[0].shape[0]
    depth, half = slabs[0][0].shape
    in_hbm = pl.BlockSpec(memory_space=pltpu.HBM)
    in_vmem = pl.BlockSpec(memory_space=pltpu.VMEM)
    scratch = [
        pltpu.VMEM((rows, count * depth), jnp.bfloat16),
        pltpu.VMEM((2, count * depth, half), jnp.bfloat16),
        pltpu.SemaphoreType.DMA((count,)),
        pltpu.SemaphoreType.DMA((2, count)),
    ]
    if last:
        scratch += [pltpu.VMEM((rows, 2 * half), jnp.bfloat16), pltpu.SemaphoreType.DMA((2,))]
    return pl.pallas_call(
        functools.partial(ring_product_kernel, steps, base is not None, last),
        out_shape=jax.ShapeDtypeStruct((rows, 2 * half), jnp.bfloat16 if last else jnp.float32),
        in_specs=[pl.BlockSpec(memory_space=pltpu.SMEM)]
        + [in_hbm] * (4 + 2 * count)
        + [in_vmem] * (base is not None),
        out_specs=in_hbm if last else in_vmem,
        scratch_shapes=scratch,
        compiler_params=pltpu.CompilerParams(vmem_limit_bytes=(8 + 4 * count) << 20),
        cost_estimate=pl.CostEstimate(
            flops=1 << 20, transcendentals=0, bytes_accessed=1 << 20
        ),
        name="ring_product",
    )(
        where,
        *[
            pltpu.with_memory_space_constraint(x, pltpu.HBM)
            for x in (*blocks, *slabs[0], *slabs[1])
        ],
        *([] if base is None else [base]),
    )


def project_ring(wo, inputs, attend_with):
    pb_size = lax.axis_size("pb")
    depth, columns = wo.shape
    ring = ring_of(pb_size)
    forward = [(ring[i], ring[(i + 1) % pb_size]) for i in range(pb_size)]
    backward = [(b, a) for a, b in forward]
    half = columns // 2
    far = pb_size // 2
    parts = [wo[:, :half], wo[:, half:]]
    inputs, parts[0], parts[1] = lax.optimization_barrier((inputs, parts[0], parts[1]))
    slabs = [[(0, part)] for part in parts]
    moving = [[part, part] for part in parts]
    for hop in range(1, far + 1):
        for part in range(2):
            if hop < far or part == 0:
                moving[part][0] = lax.ppermute(moving[part][0], "pb", forward)
                slabs[part].append((-hop, moving[part][0]))
            if hop < far or part == 1:
                moving[part][1] = lax.ppermute(moving[part][1], "pb", backward)
                slabs[part].append((hop, moving[part][1]))
    attn = attend_with(inputs)
    across = lax.ppermute(attn, "ka", [(i, i ^ 2) for i in range(4)])
    beside = lax.ppermute(attn, "ka", [(i, i ^ 1) for i in range(4)])
    corner = lax.ppermute(across, "ka", [(i, i ^ 1) for i in range(4)])
    around = jnp.asarray(
        [[ring[(ring.index(p) + step) % pb_size] for step in range(pb_size)] for p in range(pb_size)],
        jnp.int32,
    )
    mine = lax.dynamic_slice(around, (lax.axis_index("pb"), 0), (1, pb_size))[0]
    where = jnp.concatenate([mine, lax.axis_index("ka")[None].astype(jnp.int32)])
    blocks = [attn, beside, across, corner]
    at_step = [{offset % pb_size: slab for offset, slab in slabs[part]} for part in range(2)]
    total = None
    for offsets in ((0, -1, 1, -2, 2), (-3, 3), (4,)):
        chosen = [[at_step[part][offset % pb_size] for offset in offsets] for part in range(2)]
        steps = tuple(offset % pb_size for offset in offsets)
        total = ring_product(where, blocks, steps, chosen, total, offsets == (far,))
    return total


def shards(queries, keys, values, block_ids, counts, refresh, cached_attn, wo):
    groups = lax.axis_size("ka")

    def attend_with(inputs):
        queries, keys, values, old = inputs
        parts, places = own_head_keys_values(keys, values)
        return attend(block_ids[0, 0], counts[0, 0], refresh[0, 0], queries, old, parts, places)

    inputs = (queries[0], keys, values, cached_attn[0])
    if lax.axis_size("pb") == 8 and groups == 4:
        mixed = project_ring(wo, inputs, attend_with)
    else:
        attn_full = lax.all_gather(attend_with(inputs), "ka", axis=1, tiled=True)
        mixed = jnp.dot(
            attn_full, lax.all_gather(wo, "pb", axis=0, tiled=True), preferred_element_type=jnp.float32
        ).astype(jnp.bfloat16)
    return mixed[None]


def solution(mesh):
    placed = (
        P(None, "pb", "ka"),
        P("ka", None),
        P("ka", None),
        P(None, "pb", None),
        P(None, "pb"),
        P(None, "pb"),
        P(None, "pb", "ka"),
        P("pb", "ka"),
    )
    return jax.shard_map(
        shards, mesh=mesh, in_specs=placed, out_specs=P(None, "pb", "ka"), check_vma=False
    )
```

```python
import functools
import math

import jax
import jax.numpy as jnp
from jax import lax
from jax.experimental import pallas as pl
from jax.experimental.pallas import tpu as pltpu
from jax.sharding import PartitionSpec as P

HEAD_SIZE = 128
QUERY_HEAD_COUNT = 32
KEY_VALUE_HEADS = 4
QUERY_BLOCK_SIZE = 512
KEY_BLOCK_TOKENS = 128
RATIO = QUERY_HEAD_COUNT // KEY_VALUE_HEADS
LOWEST = -1e30
EXP2_SCALE = math.log2(math.e) / math.sqrt(HEAD_SIZE)


GROUP = 4


def attention_kernel(heads, slots, meta_ref, q_hbm, old_hbm, *refs):
    kv_parts, (out_ref, q_ref, kv_ref, peak_ref, denom_ref, acc_ref, sems) = refs[:-7], refs[-7:]
    live = meta_ref[0]
    flag = meta_ref[1]

    @pl.when(flag <= 0)
    def _():
        copy = pltpu.make_async_copy(old_hbm, out_ref, sems.at[0])
        copy.start()
        copy.wait()

    @pl.when(flag > 0)
    def _():
        copies = [pltpu.make_async_copy(q_hbm, q_ref, sems.at[0])]
        for index, part in enumerate(kv_parts):
            rows = part.shape[0]
            start = pl.multiple_of(meta_ref[2 + slots + index] * rows, rows)
            copies.append(
                pltpu.make_async_copy(part, kv_ref.at[pl.ds(start, rows), :], sems.at[1 + index])
            )
        for copy in copies:
            copy.start()
        peak_ref[...] = jnp.full_like(peak_ref, LOWEST)
        denom_ref[...] = jnp.zeros_like(denom_ref)
        acc_ref[...] = jnp.zeros_like(acc_ref)
        for copy in copies:
            copy.wait()

        def group(step, carry):
            tiles, biases = [], []
            for member in range(GROUP):
                slot = step * GROUP + member
                if member > 0:
                    present = slot < live
                    block = jnp.where(
                        present, meta_ref[2 + jnp.minimum(slot, slots - 1)], 0
                    )
                    biases.append(jnp.where(present, 0.0, LOWEST).astype(jnp.float32))
                else:
                    block = meta_ref[2 + slot]
                    biases.append(None)
                row = pl.multiple_of(block * KEY_BLOCK_TOKENS, KEY_BLOCK_TOKENS)
                tiles.append(kv_ref[pl.ds(row, KEY_BLOCK_TOKENS), :])
            tile = jnp.concatenate(tiles, axis=0)
            key_tile = tile[:, :HEAD_SIZE]
            value_tile = tile[:, HEAD_SIZE:].T
            value_tile = jnp.concatenate(
                [value_tile, jnp.ones((16, value_tile.shape[1]), jnp.bfloat16)], axis=0
            )
            for head in range(heads):
                query = q_ref[:, head * HEAD_SIZE : (head + 1) * HEAD_SIZE]
                scores = lax.dot_general(
                    key_tile, query, (((1,), (1,)), ((), ())), preferred_element_type=jnp.float32
                )
                parts = [
                    scores[member * KEY_BLOCK_TOKENS : (member + 1) * KEY_BLOCK_TOKENS]
                    for member in range(GROUP)
                ]
                parts = [p if b is None else p + b for p, b in zip(parts, biases)]
                top = functools.reduce(jnp.maximum, parts)
                old_peak = peak_ref[head]
                peak = jnp.maximum(old_peak, jnp.max(top, axis=0, keepdims=True))
                decay = jnp.exp2((old_peak - peak) * EXP2_SCALE)
                parts = [jnp.exp2((p - peak) * EXP2_SCALE) for p in parts]
                peak_ref[head] = peak
                weights = jnp.concatenate([p.astype(jnp.bfloat16) for p in parts], axis=0)
                update = lax.dot_general(
                    value_tile, weights, (((1,), (0,)), ((), ())), preferred_element_type=jnp.float32
                )
                denom_ref[head] = denom_ref[head] * decay + update[HEAD_SIZE : HEAD_SIZE + 1]
                acc_ref[head] = acc_ref[head] * decay + update[:HEAD_SIZE]
            return carry

        lax.fori_loop(0, (live + GROUP - 1) // GROUP, group, 0)
        for head in range(heads):
            result = acc_ref[head] / denom_ref[head]
            out_ref[:, head * HEAD_SIZE : (head + 1) * HEAD_SIZE] = result.T.astype(jnp.bfloat16)


def attend(block_list, live, flag, queries, old, kv_parts, places):
    rows, width = queries.shape
    heads = width // HEAD_SIZE
    slots = block_list.shape[0]
    meta = jnp.concatenate([live[None], flag[None], block_list, *[p[None] for p in places]])
    in_hbm = pl.BlockSpec(memory_space=pltpu.HBM)
    return pl.pallas_call(
        functools.partial(attention_kernel, heads, slots),
        out_shape=jax.ShapeDtypeStruct((rows, width), jnp.bfloat16),
        in_specs=[pl.BlockSpec(memory_space=pltpu.SMEM)] + [in_hbm] * (2 + len(kv_parts)),
        out_specs=pl.BlockSpec(memory_space=pltpu.VMEM),
        scratch_shapes=[
            pltpu.VMEM((rows, width), jnp.bfloat16),
            pltpu.VMEM((sum(p.shape[0] for p in kv_parts), 2 * HEAD_SIZE), jnp.bfloat16),
            pltpu.VMEM((heads, 1, rows), jnp.float32),
            pltpu.VMEM((heads, 1, rows), jnp.float32),
            pltpu.VMEM((heads, HEAD_SIZE, rows), jnp.float32),
            pltpu.SemaphoreType.DMA((1 + len(kv_parts),)),
        ],
        compiler_params=pltpu.CompilerParams(vmem_limit_bytes=24 << 20),
        cost_estimate=pl.CostEstimate(
            flops=1 << 20, transcendentals=0, bytes_accessed=1 << 20
        ),
        name="attend",
    )(
        meta,
        *[
            pltpu.with_memory_space_constraint(x, pltpu.HBM)
            for x in (queries, old, *kv_parts)
        ],
    )


def own_head_keys_values(keys, values):
    groups = lax.axis_size("ka")
    me = lax.axis_index("ka")
    rows = keys.shape[0]
    if groups == KEY_VALUE_HEADS:

        def head_of(device):
            start = (0, device * HEAD_SIZE)
            return jnp.concatenate(
                [lax.dynamic_slice(x, start, (rows, HEAD_SIZE)) for x in (keys, values)], axis=1
            )

        parts, places = [head_of(me)], [me]
        for step in range(1, groups):
            partner = jnp.bitwise_xor(me, step)
            parts.append(
                lax.ppermute(head_of(partner), "ka", [(i, i ^ step) for i in range(groups)])
            )
            places.append(partner)
        return parts, places
    both = jnp.concatenate(
        [
            keys.reshape(rows, KEY_VALUE_HEADS, HEAD_SIZE),
            values.reshape(rows, KEY_VALUE_HEADS, HEAD_SIZE),
        ],
        axis=2,
    )
    both = jnp.repeat(both, groups // KEY_VALUE_HEADS, axis=1)
    everything = lax.all_to_all(
        both.reshape(rows, groups * 2 * HEAD_SIZE), "ka", split_axis=1, concat_axis=0, tiled=True
    )
    return [everything], [jnp.int32(0)]


ROW_TILE = 256
IN_HBM = pl.BlockSpec(memory_space=pltpu.HBM)
IN_VMEM = pl.BlockSpec(memory_space=pltpu.VMEM)
IN_SMEM = pl.BlockSpec(memory_space=pltpu.SMEM)
SMALL_COST = pl.CostEstimate(flops=1 << 20, transcendentals=0, bytes_accessed=1 << 20)


def in_hbm(values):
    return [pltpu.with_memory_space_constraint(x, pltpu.HBM) for x in values]


def in_vmem(values):
    return [pltpu.with_memory_space_constraint(x, pltpu.VMEM) for x in values]


def slab_product_kernel(kind, distances, start, has_base, out_count, where_ref, *refs):
    z, y, me = where_ref[0], where_ref[1], where_ref[2]
    own_rows, other_rows, slabs, refs = refs[:4], refs[4:8], refs[8 : 8 + len(distances)], refs[8 + len(distances) :]
    if has_base:
        base_ref, refs = refs[0], refs[1:]
    outs, (left, right, sems) = refs[:out_count], refs[out_count:]
    rows = own_rows[0].shape[0]
    depth, width = slabs[0].shape[0], right.shape[1]
    if kind == "kept":
        targets = [jnp.int32(i) for i in range(4)]
    elif kind == "near":
        targets = [(4 - z + i) % 4 for i in range(3)]
    else:
        targets = [3 - z]
    column = pl.multiple_of((y if kind == "kept" else 1 - y) * depth, depth)

    def left_copy(index, slot, side):
        source = (own_rows, other_rows)[side][slot]
        return pltpu.make_async_copy(
            source.at[:, pl.ds(column, depth)],
            left.at[pl.ds(side * rows, rows), pl.ds(index * depth, depth)],
            sems.at[index, side],
        )

    def slab_copy(index, slab):
        source = slabs[slab]
        if source.shape[1] != width:
            source = source.at[:, pl.ds(start, width)]
        return pltpu.make_async_copy(
            source, right.at[pl.ds(index * depth, depth), :], sems.at[index, 2]
        )

    for index, target in enumerate(targets):
        slot_here = jnp.bitwise_xor(me, target)
        for slot in range(4):

            @pl.when(slot_here == slot)
            def _(slot=slot):
                left_copy(index, slot, 0).start()
                left_copy(index, slot, 1).start()

        away = target - z
        for slab, distance in enumerate(distances):
            here = away == distance
            if distance == 3:
                here = here | (away == -3)

            @pl.when(here)
            def _(slab=slab):
                slab_copy(index, slab).start()

    for index in range(len(targets)):
        left_copy(index, 0, 0).wait()
        left_copy(index, 0, 1).wait()
        slab_copy(index, 0).wait()

    def rows_tile(step, carry):
        for side in range(2):
            at = pl.ds(pl.multiple_of(step * ROW_TILE + side * rows, ROW_TILE), ROW_TILE)
            product = jnp.dot(left[at, :], right[...], preferred_element_type=jnp.float32)
            if has_base:
                product = product + base_ref[at, :]
            if kind == "far":
                within = pl.ds(pl.multiple_of(step * ROW_TILE, ROW_TILE), ROW_TILE)
                outs[side][within, :] = product.astype(jnp.bfloat16)
            else:
                first = 0
                for out in outs:
                    out[at, :] = product[:, first : first + out.shape[1]]
                    first += out.shape[1]
        return carry

    lax.fori_loop(0, rows // ROW_TILE, rows_tile, 0)


def slab_product(kind, where, own_rows, other_rows, slabs, base, widths, start=0):
    rows = own_rows[0].shape[0]
    depth = slabs[0][1].shape[0]
    count = {"kept": 4, "near": 3, "far": 1}[kind]
    if kind == "far":
        out_shape = [jax.ShapeDtypeStruct((rows, widths[0]), jnp.bfloat16)] * 2
    else:
        out_shape = [jax.ShapeDtypeStruct((2 * rows, width), jnp.float32) for width in widths]
    return pl.pallas_call(
        functools.partial(
            slab_product_kernel,
            kind,
            tuple(distance for distance, _ in slabs),
            start,
            base is not None,
            len(out_shape),
        ),
        out_shape=out_shape,
        in_specs=[IN_SMEM] + [IN_HBM] * (8 + len(slabs)) + [IN_VMEM] * (base is not None),
        out_specs=[IN_VMEM] * len(out_shape),
        scratch_shapes=[
            pltpu.VMEM((2 * rows, count * depth), jnp.bfloat16),
            pltpu.VMEM((count * depth, sum(widths)), jnp.bfloat16),
            pltpu.SemaphoreType.DMA((count, 3)),
        ],
        compiler_params=pltpu.CompilerParams(vmem_limit_bytes=(4 + 3 * count) << 20),
        cost_estimate=SMALL_COST,
        name="product_" + kind,
    )(
        where,
        *in_hbm([*own_rows, *other_rows, *[slab for _, slab in slabs]]),
        *([] if base is None else in_vmem([base])),
    )


def finish_kernel(widths, where_ref, *refs):
    count = len(widths)
    out_ref, sems = refs[2 * count :]
    half = sum(widths)
    copies = []
    for side in range(2):
        start = 0
        for index, width in enumerate(widths):
            place = jnp.bitwise_xor(where_ref[1], side) * half + start
            copies.append(
                pltpu.make_async_copy(
                    refs[side * count + index],
                    out_ref.at[:, pl.ds(pl.multiple_of(place, HEAD_SIZE), width)],
                    sems.at[side, index],
                )
            )
            start += width
    for copy in copies:
        copy.start()
    for copy in copies:
        copy.wait()


def finish(where, own, received):
    widths = tuple(piece.shape[1] for piece in own)
    return pl.pallas_call(
        functools.partial(finish_kernel, widths),
        out_shape=jax.ShapeDtypeStruct((own[0].shape[0], 2 * sum(widths)), jnp.bfloat16),
        in_specs=[IN_SMEM] + [IN_VMEM] * (2 * len(widths)),
        out_specs=IN_HBM,
        scratch_shapes=[pltpu.SemaphoreType.DMA((2, len(widths)))],
        cost_estimate=SMALL_COST,
        name="finish",
    )(where, *in_vmem([*own, *received]))


UP = [[(i, i + 2) for i in range(2 * s, 6)] for s in range(2)]
DOWN = [[(i + 2, i) for i in range(6 - 2 * s)] for s in range(2)]
OUTWARD = [(2, 0), (3, 1), (4, 6), (5, 7)]
ACROSS_Y = [(i, i ^ 1) for i in range(8)]
ACROSS_X = [(i, i ^ 2) for i in range(4)]
ACROSS_CORE = [(i, i ^ 1) for i in range(4)]


def project(wo, inputs, attend_with):
    pb = lax.axis_index("pb")
    y = pb % 2
    where = jnp.stack([pb // 2, y, lax.axis_index("ka")]).astype(jnp.int32)
    depth, columns = wo.shape
    half = columns // 2
    widths = (half * 3 // 8, half * 3 // 8, half // 4)
    kept = lax.dynamic_slice(wo, (0, y * half), (depth, half))
    given = lax.dynamic_slice(wo, (0, (1 - y) * half), (depth, half))
    inputs, kept, given = lax.optimization_barrier((inputs, kept, given))

    def hop(up, down, step):
        up = up + [lax.ppermute(up[-1], "pb", UP[step])]
        down = down + [lax.ppermute(down[-1], "pb", DOWN[step])]
        return (up[1:], down[1:]) if step == 0 else (up, down)

    def other_core(piece):
        return lax.ppermute(piece, "ka", ACROSS_CORE)

    tie = lax.optimization_barrier
    kept_up, kept_down = hop([kept], [kept], 0)
    taken = lax.ppermute(given, "pb", ACROSS_Y)
    queries, keys, values, old = inputs
    parts, places = own_head_keys_values(keys, values)
    parts, kept_up[0], kept_down[0], taken = tie((parts, kept_up[0], kept_down[0], taken))
    kept_up, kept_down = hop(kept_up, kept_down, 1)
    taken_up, taken_down = hop([taken], [taken], 0)
    attn = attend_with(queries, old, parts, places)
    attn, kept_up[1], kept_down[1] = tie((attn, kept_up[1], kept_down[1]))
    kept_end = lax.ppermute(kept_up[1] + kept_down[1], "pb", OUTWARD)
    across_y = lax.ppermute(attn, "pb", ACROSS_Y)
    across_x = lax.ppermute(attn, "ka", ACROSS_X)
    across_y, across_x, taken_up[0], taken_down[0] = tie(
        (across_y, across_x, taken_up[0], taken_down[0])
    )
    taken_up, taken_down = hop(taken_up, taken_down, 1)
    ends = []
    start = 0
    for width in widths:
        piece = taken_up[1][:, start : start + width] + taken_down[1][:, start : start + width]
        ends.append(lax.ppermute(piece, "pb", OUTWARD))
        start += width
    corner = lax.ppermute(across_y, "ka", ACROSS_X)
    own_rows = [attn, other_core(attn), across_x, other_core(across_x)]
    other_rows = [across_y, other_core(across_y), corner, other_core(corner)]

    def near_slabs(piece, up, down):
        return [(0, piece), (-1, up[0]), (-2, up[1]), (1, down[0]), (2, down[1])]

    (base,) = slab_product(
        "kept",
        where,
        own_rows,
        other_rows,
        near_slabs(kept, kept_up, kept_down) + [(3, kept_end)],
        None,
        (half,),
    )
    bases = slab_product(
        "near", where, own_rows, other_rows, near_slabs(taken, taken_up, taken_down), base, widths
    )
    own_out, received = [], []
    start = 0
    for base, width, end in zip(bases, widths, ends):
        own, other = slab_product(
            "far",
            where,
            own_rows,
            other_rows,
            [(3, end), (-1, taken_up[0]), (1, taken_down[0])],
            base,
            (width,),
            start,
        )
        own_out.append(own)
        received.append(lax.ppermute(other, "pb", ACROSS_Y))
        start += width
    return finish(where, own_out, received)


def shards(queries, keys, values, block_ids, counts, refresh, cached_attn, wo):
    groups = lax.axis_size("ka")

    def attend_with(queries, old, parts, places):
        return attend(block_ids[0, 0], counts[0, 0], refresh[0, 0], queries, old, parts, places)

    if lax.axis_size("pb") == 8 and groups == 4:
        mixed = project(wo, (queries[0], keys, values, cached_attn[0]), attend_with)
    else:
        attn = attend_with(queries[0], cached_attn[0], *own_head_keys_values(keys, values))
        attn_full = lax.all_gather(attn, "ka", axis=1, tiled=True)
        mixed = jnp.dot(
            attn_full, lax.all_gather(wo, "pb", axis=0, tiled=True), preferred_element_type=jnp.float32
        ).astype(jnp.bfloat16)
    return mixed[None]


def solution(mesh):
    placed = (
        P(None, "pb", "ka"),
        P("ka", None),
        P("ka", None),
        P(None, "pb", None),
        P(None, "pb"),
        P(None, "pb"),
        P(None, "pb", "ka"),
        P("pb", "ka"),
    )
    return jax.shard_map(
        shards, mesh=mesh, in_specs=placed, out_specs=P(None, "pb", "ka"), check_vma=False
    )
```

```python
import functools
import math

import jax
import jax.numpy as jnp
from jax import lax
from jax.experimental import pallas as pl
from jax.experimental.pallas import tpu as pltpu
from jax.sharding import PartitionSpec as P

HEAD_SIZE = 128
QUERY_HEAD_COUNT = 32
KEY_VALUE_HEADS = 4
QUERY_BLOCK_SIZE = 512
KEY_BLOCK_TOKENS = 128
RATIO = QUERY_HEAD_COUNT // KEY_VALUE_HEADS
LOWEST = -1e30
EXP2_SCALE = math.log2(math.e) / math.sqrt(HEAD_SIZE)


GROUP = 4


def attention_kernel(heads, slots, row_starts, meta_ref, q_hbm, old_hbm, *refs):
    kv_parts, (out_ref, q_ref, kv_ref, peak_ref, denom_ref, acc_ref, sems) = refs[:-7], refs[-7:]
    live = meta_ref[0]
    flag = meta_ref[1]

    @pl.when(flag <= 0)
    def _():
        copy = pltpu.make_async_copy(old_hbm, out_ref, sems.at[0])
        copy.start()
        copy.wait()

    @pl.when(flag > 0)
    def _():
        copies = [pltpu.make_async_copy(q_hbm, q_ref, sems.at[0])]
        rows = kv_ref.shape[0] // len(kv_parts)
        pick = pl.multiple_of(meta_ref[2 + slots + len(kv_parts)] * HEAD_SIZE, HEAD_SIZE)
        for index, part in enumerate(kv_parts):
            start = pl.multiple_of(meta_ref[2 + slots + index] * rows, rows)
            source_rows, target_rows = pl.ds(row_starts[index], rows), pl.ds(start, rows)
            if part.shape[1] == 2 * HEAD_SIZE:
                pairs = [(pl.ds(0, 2 * HEAD_SIZE), pl.ds(0, 2 * HEAD_SIZE))]
            else:
                pairs = [
                    (pl.ds(pick, HEAD_SIZE), pl.ds(0, HEAD_SIZE)),
                    (pl.ds(part.shape[1] // 2 + pick, HEAD_SIZE), pl.ds(HEAD_SIZE, HEAD_SIZE)),
                ]
            for side, (source_columns, target_columns) in enumerate(pairs):
                copies.append(
                    pltpu.make_async_copy(
                        part.at[source_rows, source_columns],
                        kv_ref.at[target_rows, target_columns],
                        sems.at[1 + 2 * index + side],
                    )
                )
        for copy in copies:
            copy.start()
        peak_ref[...] = jnp.full_like(peak_ref, LOWEST)
        denom_ref[...] = jnp.zeros_like(denom_ref)
        acc_ref[...] = jnp.zeros_like(acc_ref)
        for copy in copies:
            copy.wait()

        def group(step, carry):
            tiles, biases = [], []
            for member in range(GROUP):
                slot = step * GROUP + member
                if member > 0:
                    present = slot < live
                    block = jnp.where(
                        present, meta_ref[2 + jnp.minimum(slot, slots - 1)], 0
                    )
                    biases.append(jnp.where(present, 0.0, LOWEST).astype(jnp.float32))
                else:
                    block = meta_ref[2 + slot]
                    biases.append(None)
                row = pl.multiple_of(block * KEY_BLOCK_TOKENS, KEY_BLOCK_TOKENS)
                tiles.append(kv_ref[pl.ds(row, KEY_BLOCK_TOKENS), :])
            tile = jnp.concatenate(tiles, axis=0)
            key_tile = tile[:, :HEAD_SIZE]
            value_tile = tile[:, HEAD_SIZE:].T
            value_tile = jnp.concatenate(
                [value_tile, jnp.ones((16, value_tile.shape[1]), jnp.bfloat16)], axis=0
            )
            for head in range(heads):
                query = q_ref[:, head * HEAD_SIZE : (head + 1) * HEAD_SIZE]
                scores = lax.dot_general(
                    key_tile, query, (((1,), (1,)), ((), ())), preferred_element_type=jnp.float32
                )
                parts = [
                    scores[member * KEY_BLOCK_TOKENS : (member + 1) * KEY_BLOCK_TOKENS]
                    for member in range(GROUP)
                ]
                parts = [p if b is None else p + b for p, b in zip(parts, biases)]
                top = functools.reduce(jnp.maximum, parts)
                old_peak = peak_ref[head]
                peak = jnp.maximum(old_peak, jnp.max(top, axis=0, keepdims=True))
                decay = jnp.exp2((old_peak - peak) * EXP2_SCALE)
                parts = [jnp.exp2((p - peak) * EXP2_SCALE) for p in parts]
                peak_ref[head] = peak
                weights = jnp.concatenate([p.astype(jnp.bfloat16) for p in parts], axis=0)
                update = lax.dot_general(
                    value_tile, weights, (((1,), (0,)), ((), ())), preferred_element_type=jnp.float32
                )
                denom_ref[head] = denom_ref[head] * decay + update[HEAD_SIZE : HEAD_SIZE + 1]
                acc_ref[head] = acc_ref[head] * decay + update[:HEAD_SIZE]
            return carry

        lax.fori_loop(0, (live + GROUP - 1) // GROUP, group, 0)
        for head in range(heads):
            result = acc_ref[head] / denom_ref[head]
            out_ref[:, head * HEAD_SIZE : (head + 1) * HEAD_SIZE] = result.T.astype(jnp.bfloat16)


def attend(block_list, live, flag, queries, old, key_values):
    arrays, row_starts, places, pick = key_values
    rows, width = queries.shape
    heads = width // HEAD_SIZE
    slots = block_list.shape[0]
    part_rows = min(x.shape[0] for x in arrays)
    meta = jnp.concatenate(
        [live[None], flag[None], block_list, *[p[None] for p in places], pick[None]]
    )
    in_hbm = pl.BlockSpec(memory_space=pltpu.HBM)
    return pl.pallas_call(
        functools.partial(attention_kernel, heads, slots, tuple(row_starts)),
        out_shape=jax.ShapeDtypeStruct((rows, width), jnp.bfloat16),
        in_specs=[pl.BlockSpec(memory_space=pltpu.SMEM)] + [in_hbm] * (2 + len(arrays)),
        out_specs=pl.BlockSpec(memory_space=pltpu.VMEM),
        scratch_shapes=[
            pltpu.VMEM((rows, width), jnp.bfloat16),
            pltpu.VMEM((part_rows * len(arrays), 2 * HEAD_SIZE), jnp.bfloat16),
            pltpu.VMEM((heads, 1, rows), jnp.float32),
            pltpu.VMEM((heads, 1, rows), jnp.float32),
            pltpu.VMEM((heads, HEAD_SIZE, rows), jnp.float32),
            pltpu.SemaphoreType.DMA((1 + 2 * len(arrays),)),
        ],
        compiler_params=pltpu.CompilerParams(vmem_limit_bytes=24 << 20),
        cost_estimate=pl.CostEstimate(
            flops=1 << 20, transcendentals=0, bytes_accessed=1 << 20
        ),
        name="attend",
    )(
        meta,
        *[
            pltpu.with_memory_space_constraint(x, pltpu.HBM)
            for x in (queries, old, *arrays)
        ],
    )


def own_head_keys_values(keys, values):
    groups = lax.axis_size("ka")
    me = lax.axis_index("ka")
    rows = keys.shape[0]
    if groups == KEY_VALUE_HEADS == 4:
        x, core = me // 2, me % 2
        pair = 2 * HEAD_SIZE

        def heads_of(chip):
            return jnp.concatenate(
                [lax.dynamic_slice(a, (0, chip * pair), (rows, pair)) for a in (keys, values)], axis=1
            )

        def head_of(both):
            picked = [
                lax.dynamic_slice(both, (0, side * pair + (1 - core) * HEAD_SIZE), (rows, HEAD_SIZE))
                for side in range(2)
            ]
            return jnp.concatenate(picked, axis=1)

        across = lax.ppermute(heads_of(1 - x), "ka", [(i, i ^ 2) for i in range(4)])
        mine = heads_of(x)
        beside = lax.ppermute(
            jnp.concatenate([head_of(mine), head_of(across)], axis=0),
            "ka",
            [(i, i ^ 1) for i in range(4)],
        )
        places = [jnp.bitwise_xor(me, step) for step in (0, 2, 1, 3)]
        return [mine, across, beside, beside], [0, 0, 0, rows], places, core
    both = jnp.concatenate(
        [
            keys.reshape(rows, KEY_VALUE_HEADS, HEAD_SIZE),
            values.reshape(rows, KEY_VALUE_HEADS, HEAD_SIZE),
        ],
        axis=2,
    )
    both = jnp.repeat(both, groups // KEY_VALUE_HEADS, axis=1)
    everything = lax.all_to_all(
        both.reshape(rows, groups * 2 * HEAD_SIZE), "ka", split_axis=1, concat_axis=0, tiled=True
    )
    return [everything], [0], [jnp.int32(0)], jnp.int32(0)


def ring_of(pb_size):
    if pb_size == 8:
        return [0, 2, 4, 6, 7, 5, 3, 1]
    return list(range(pb_size))


ROW_TILE = 128


def ring_product_kernel(steps, has_base, last, where_ref, *refs):
    count = len(steps)
    blocks, slabs, refs = refs[:4], (refs[4 : 4 + count], refs[4 + count : 4 + 2 * count]), refs[4 + 2 * count :]
    if has_base:
        base_ref, refs = refs[0], refs[1:]
    out_ref, left, right, block_sems, slab_sems = refs[:5]
    rows, depth = left.shape[0], right.shape[1] // count
    per = blocks[0].shape[1] // depth
    me = where_ref[where_ref.shape[0] - 1]

    def block_copy(index, slot, shift):
        return pltpu.make_async_copy(
            blocks[slot].at[:, pl.ds(shift, depth)],
            left.at[:, pl.ds(index * depth, depth)],
            block_sems.at[index],
        )

    def slab_copy(half, index):
        return pltpu.make_async_copy(
            slabs[half][index],
            right.at[half, pl.ds(index * depth, depth), :],
            slab_sems.at[half, index],
        )

    for index, step in enumerate(steps):
        source = where_ref[step]
        slot_here = jnp.bitwise_xor(source // per, me)
        shift = pl.multiple_of((source % per) * depth, depth)
        for slot in range(4):

            @pl.when(slot_here == slot)
            def _(slot=slot):
                block_copy(index, slot, shift).start()

    for half in range(2):
        for index in range(count):
            slab_copy(half, index).start()
    for index in range(count):
        block_copy(index, 0, 0).wait()
    half_columns = right.shape[2]
    if last:
        staged, out_sems = refs[5:]
    for half in range(2):
        columns = pl.ds(half * half_columns, half_columns)
        for index in range(count):
            slab_copy(half, index).wait()

        def rows_tile(step, carry):
            at = pl.ds(pl.multiple_of(step * ROW_TILE, ROW_TILE), ROW_TILE)
            product = jnp.dot(left[at, :], right[half], preferred_element_type=jnp.float32)
            if has_base:
                product = product + base_ref[at, columns]
            if last:
                staged[at, columns] = product.astype(jnp.bfloat16)
            else:
                out_ref[at, columns] = product
            return carry

        lax.fori_loop(0, rows // ROW_TILE, rows_tile, 0)
        if last:
            pltpu.make_async_copy(
                staged.at[:, columns], out_ref.at[:, columns], out_sems.at[half]
            ).start()
    if last:
        for half in range(2):
            columns = pl.ds(half * half_columns, half_columns)
            pltpu.make_async_copy(
                staged.at[:, columns], out_ref.at[:, columns], out_sems.at[half]
            ).wait()


def ring_product(where, blocks, steps, slabs, base, last):
    count = len(steps)
    rows = blocks[0].shape[0]
    depth, half = slabs[0][0].shape
    in_hbm = pl.BlockSpec(memory_space=pltpu.HBM)
    in_vmem = pl.BlockSpec(memory_space=pltpu.VMEM)
    scratch = [
        pltpu.VMEM((rows, count * depth), jnp.bfloat16),
        pltpu.VMEM((2, count * depth, half), jnp.bfloat16),
        pltpu.SemaphoreType.DMA((count,)),
        pltpu.SemaphoreType.DMA((2, count)),
    ]
    if last:
        scratch += [pltpu.VMEM((rows, 2 * half), jnp.bfloat16), pltpu.SemaphoreType.DMA((2,))]
    return pl.pallas_call(
        functools.partial(ring_product_kernel, steps, base is not None, last),
        out_shape=jax.ShapeDtypeStruct((rows, 2 * half), jnp.bfloat16 if last else jnp.float32),
        in_specs=[pl.BlockSpec(memory_space=pltpu.SMEM)]
        + [in_hbm] * (4 + 2 * count)
        + [in_vmem] * (base is not None),
        out_specs=in_hbm if last else in_vmem,
        scratch_shapes=scratch,
        compiler_params=pltpu.CompilerParams(vmem_limit_bytes=(8 + 4 * count) << 20),
        cost_estimate=pl.CostEstimate(
            flops=1 << 20, transcendentals=0, bytes_accessed=1 << 20
        ),
        name="ring_product",
    )(
        where,
        *[
            pltpu.with_memory_space_constraint(x, pltpu.HBM)
            for x in (*blocks, *slabs[0], *slabs[1])
        ],
        *([] if base is None else [base]),
    )


def project_ring(wo, inputs, attend_with):
    pb_size = lax.axis_size("pb")
    depth, columns = wo.shape
    ring = ring_of(pb_size)
    forward = [(ring[i], ring[(i + 1) % pb_size]) for i in range(pb_size)]
    backward = [(b, a) for a, b in forward]
    half = columns // 2
    far = pb_size // 2
    parts = [wo[:, :half], wo[:, half:]]
    inputs, parts[0], parts[1] = lax.optimization_barrier((inputs, parts[0], parts[1]))
    slabs = [[(0, part)] for part in parts]
    moving = [[part, part] for part in parts]
    for hop in range(1, far + 1):
        for part in range(2):
            if hop < far or part == 0:
                moving[part][0] = lax.ppermute(moving[part][0], "pb", forward)
                slabs[part].append((-hop, moving[part][0]))
            if hop < far or part == 1:
                moving[part][1] = lax.ppermute(moving[part][1], "pb", backward)
                slabs[part].append((hop, moving[part][1]))
    attn = attend_with(inputs)
    across = lax.ppermute(attn, "ka", [(i, i ^ 2) for i in range(4)])
    beside = lax.ppermute(attn, "ka", [(i, i ^ 1) for i in range(4)])
    corner = lax.ppermute(across, "ka", [(i, i ^ 1) for i in range(4)])
    around = jnp.asarray(
        [[ring[(ring.index(p) + step) % pb_size] for step in range(pb_size)] for p in range(pb_size)],
        jnp.int32,
    )
    mine = lax.dynamic_slice(around, (lax.axis_index("pb"), 0), (1, pb_size))[0]
    where = jnp.concatenate([mine, lax.axis_index("ka")[None].astype(jnp.int32)])
    blocks = [attn, beside, across, corner]
    at_step = [{offset % pb_size: slab for offset, slab in slabs[part]} for part in range(2)]
    total = None
    for offsets in ((0, -1, 1, -2, 2), (-3, 3), (4,)):
        chosen = [[at_step[part][offset % pb_size] for offset in offsets] for part in range(2)]
        steps = tuple(offset % pb_size for offset in offsets)
        total = ring_product(where, blocks, steps, chosen, total, offsets == (far,))
    return total


def shards(queries, keys, values, block_ids, counts, refresh, cached_attn, wo):
    groups = lax.axis_size("ka")

    def attend_with(inputs):
        queries, keys, values, old = inputs
        return attend(
            block_ids[0, 0], counts[0, 0], refresh[0, 0], queries, old, own_head_keys_values(keys, values)
        )

    inputs = (queries[0], keys, values, cached_attn[0])
    if lax.axis_size("pb") == 8 and groups == 4:
        mixed = project_ring(wo, inputs, attend_with)
    else:
        attn_full = lax.all_gather(attend_with(inputs), "ka", axis=1, tiled=True)
        mixed = jnp.dot(
            attn_full, lax.all_gather(wo, "pb", axis=0, tiled=True), preferred_element_type=jnp.float32
        ).astype(jnp.bfloat16)
    return mixed[None]


def solution(mesh):
    placed = (
        P(None, "pb", "ka"),
        P("ka", None),
        P("ka", None),
        P(None, "pb", None),
        P(None, "pb"),
        P(None, "pb"),
        P(None, "pb", "ka"),
        P("pb", "ka"),
    )
    return jax.shard_map(
        shards, mesh=mesh, in_specs=placed, out_specs=P(None, "pb", "ka"), check_vma=False
    )
```

```python
import functools
import math

import jax
import jax.numpy as jnp
from jax import lax
from jax.experimental import pallas as pl
from jax.experimental.pallas import tpu as pltpu
from jax.sharding import PartitionSpec as P

HEAD_SIZE = 128
QUERY_HEAD_COUNT = 32
KEY_VALUE_HEADS = 4
QUERY_BLOCK_SIZE = 512
KEY_BLOCK_TOKENS = 128
RATIO = QUERY_HEAD_COUNT // KEY_VALUE_HEADS
LOWEST = -1e30
EXP2_SCALE = math.log2(math.e) / math.sqrt(HEAD_SIZE)


GROUP = 4


def attention_kernel(
    heads, slots, part_rows, first_rows, targets, meta_ref, q_hbm, old_hbm, *refs
):
    kv_parts, (out_ref, q_ref, kv_ref, peak_ref, denom_ref, acc_ref, sems) = refs[:-7], refs[-7:]
    live = meta_ref[0]
    flag = meta_ref[1]

    @pl.when(flag <= 0)
    def _():
        copy = pltpu.make_async_copy(old_hbm, out_ref, sems.at[0])
        copy.start()
        copy.wait()

    @pl.when(flag > 0)
    def _():
        copies = [pltpu.make_async_copy(q_hbm, q_ref, sems.at[0])]
        for index, (part, first_row, target) in enumerate(zip(kv_parts, first_rows, targets)):
            column = pl.multiple_of(meta_ref[2 + slots + 2 * index] * HEAD_SIZE, HEAD_SIZE)
            start = pl.multiple_of(meta_ref[3 + slots + 2 * index] * part_rows, part_rows)
            copies.append(
                pltpu.make_async_copy(
                    part.at[pl.ds(first_row, part_rows), pl.ds(column, HEAD_SIZE)],
                    kv_ref.at[pl.ds(start, part_rows), pl.ds(target * HEAD_SIZE, HEAD_SIZE)],
                    sems.at[1 + index],
                )
            )
        for copy in copies:
            copy.start()
        peak_ref[...] = jnp.full_like(peak_ref, LOWEST)
        denom_ref[...] = jnp.zeros_like(denom_ref)
        acc_ref[...] = jnp.zeros_like(acc_ref)
        for copy in copies:
            copy.wait()

        def group(step, carry):
            tiles, biases = [], []
            for member in range(GROUP):
                slot = step * GROUP + member
                if member > 0:
                    present = slot < live
                    block = jnp.where(
                        present, meta_ref[2 + jnp.minimum(slot, slots - 1)], 0
                    )
                    biases.append(jnp.where(present, 0.0, LOWEST).astype(jnp.float32))
                else:
                    block = meta_ref[2 + slot]
                    biases.append(None)
                row = pl.multiple_of(block * KEY_BLOCK_TOKENS, KEY_BLOCK_TOKENS)
                tiles.append(kv_ref[pl.ds(row, KEY_BLOCK_TOKENS), :])
            tile = jnp.concatenate(tiles, axis=0)
            key_tile = tile[:, :HEAD_SIZE]
            value_tile = tile[:, HEAD_SIZE:].T
            value_tile = jnp.concatenate(
                [value_tile, jnp.ones((16, value_tile.shape[1]), jnp.bfloat16)], axis=0
            )
            for head in range(heads):
                query = q_ref[:, head * HEAD_SIZE : (head + 1) * HEAD_SIZE]
                scores = lax.dot_general(
                    key_tile, query, (((1,), (1,)), ((), ())), preferred_element_type=jnp.float32
                )
                parts = [
                    scores[member * KEY_BLOCK_TOKENS : (member + 1) * KEY_BLOCK_TOKENS]
                    for member in range(GROUP)
                ]
                parts = [p if b is None else p + b for p, b in zip(parts, biases)]
                top = functools.reduce(jnp.maximum, parts)
                old_peak = peak_ref[head]
                peak = jnp.maximum(old_peak, jnp.max(top, axis=0, keepdims=True))
                decay = jnp.exp2((old_peak - peak) * EXP2_SCALE)
                parts = [jnp.exp2((p - peak) * EXP2_SCALE) for p in parts]
                peak_ref[head] = peak
                weights = jnp.concatenate([p.astype(jnp.bfloat16) for p in parts], axis=0)
                update = lax.dot_general(
                    value_tile, weights, (((1,), (0,)), ((), ())), preferred_element_type=jnp.float32
                )
                denom_ref[head] = denom_ref[head] * decay + update[HEAD_SIZE : HEAD_SIZE + 1]
                acc_ref[head] = acc_ref[head] * decay + update[:HEAD_SIZE]
            return carry

        lax.fori_loop(0, (live + GROUP - 1) // GROUP, group, 0)
        for head in range(heads):
            result = acc_ref[head] / denom_ref[head]
            out_ref[:, head * HEAD_SIZE : (head + 1) * HEAD_SIZE] = result.T.astype(jnp.bfloat16)


def attend(block_list, live, flag, queries, old, key_values):
    part_rows, sources = key_values
    arrays, first_rows, heads_at, targets, places = zip(*sources)
    rows, width = queries.shape
    heads = width // HEAD_SIZE
    slots = block_list.shape[0]
    spots = [value[None] for pair in zip(heads_at, places) for value in pair]
    meta = jnp.concatenate([live[None], flag[None], block_list, *spots])
    in_hbm = pl.BlockSpec(memory_space=pltpu.HBM)
    return pl.pallas_call(
        functools.partial(attention_kernel, heads, slots, part_rows, first_rows, targets),
        out_shape=jax.ShapeDtypeStruct((rows, width), jnp.bfloat16),
        in_specs=[pl.BlockSpec(memory_space=pltpu.SMEM)] + [in_hbm] * (2 + len(arrays)),
        out_specs=pl.BlockSpec(memory_space=pltpu.VMEM),
        scratch_shapes=[
            pltpu.VMEM((rows, width), jnp.bfloat16),
            pltpu.VMEM((part_rows * len(arrays) // 2, 2 * HEAD_SIZE), jnp.bfloat16),
            pltpu.VMEM((heads, 1, rows), jnp.float32),
            pltpu.VMEM((heads, 1, rows), jnp.float32),
            pltpu.VMEM((heads, HEAD_SIZE, rows), jnp.float32),
            pltpu.SemaphoreType.DMA((1 + len(arrays),)),
        ],
        compiler_params=pltpu.CompilerParams(vmem_limit_bytes=24 << 20),
        cost_estimate=pl.CostEstimate(
            flops=1 << 20, transcendentals=0, bytes_accessed=1 << 20
        ),
        name="attend",
    )(
        meta,
        *[
            pltpu.with_memory_space_constraint(x, pltpu.HBM)
            for x in (queries, old, *arrays)
        ],
    )


def own_head_keys_values(keys, values, gate=lambda x: x):
    groups = lax.axis_size("ka")
    me = lax.axis_index("ka")
    rows = keys.shape[0]
    if groups == KEY_VALUE_HEADS == 4:
        x, core = me // 2, me % 2
        pair = 2 * HEAD_SIZE

        def heads_of(array, chip):
            return lax.dynamic_slice(array, (0, chip * pair), (rows, pair))

        def head_of(array, head):
            return lax.dynamic_slice(array, (0, head * HEAD_SIZE), (rows, HEAD_SIZE))

        across = [
            lax.ppermute(heads_of(a, 1 - x), "ka", [(i, i ^ 2) for i in range(4)])
            for a in (keys, values)
        ]
        across = gate(across)
        beside = lax.ppermute(
            jnp.concatenate(
                [
                    jnp.concatenate([head_of(a, 2 * x + 1 - core) for a in (keys, values)], axis=1),
                    jnp.concatenate([head_of(a, 1 - core) for a in across], axis=1),
                ],
                axis=0,
            ),
            "ka",
            [(i, i ^ 1) for i in range(4)],
        )
        near, far = jnp.bitwise_xor(me, 1), jnp.bitwise_xor(me, 3)
        sources = [
            (keys, 0, me, 0, me),
            (values, 0, me, 1, me),
            (across[0], 0, core, 0, jnp.bitwise_xor(me, 2)),
            (across[1], 0, core, 1, jnp.bitwise_xor(me, 2)),
        ]
        for side in range(2):
            for row, place in ((0, near), (rows, far)):
                sources.append((beside, row, jnp.int32(side), side, place))
        return rows, sources
    both = jnp.concatenate(
        [
            keys.reshape(rows, KEY_VALUE_HEADS, HEAD_SIZE),
            values.reshape(rows, KEY_VALUE_HEADS, HEAD_SIZE),
        ],
        axis=2,
    )
    both = jnp.repeat(both, groups // KEY_VALUE_HEADS, axis=1)
    everything = lax.all_to_all(
        both.reshape(rows, groups * 2 * HEAD_SIZE), "ka", split_axis=1, concat_axis=0, tiled=True
    )
    first = jnp.int32(0)
    return everything.shape[0], [(everything, 0, jnp.int32(side), side, first) for side in range(2)]


def ring_of(pb_size):
    if pb_size == 8:
        return [0, 2, 4, 6, 7, 5, 3, 1]
    return list(range(pb_size))


ROW_TILE = 128


def ring_product_kernel(steps, has_base, last, where_ref, *refs):
    count = len(steps)
    blocks, slabs, refs = refs[:4], (refs[4 : 4 + count], refs[4 + count : 4 + 2 * count]), refs[4 + 2 * count :]
    if has_base:
        base_ref, refs = refs[0], refs[1:]
    out_ref, left, right, block_sems, slab_sems = refs[:5]
    rows, depth = left.shape[0], right.shape[1] // count
    per = blocks[0].shape[1] // depth
    me = where_ref[where_ref.shape[0] - 1]

    def block_copy(index, slot, shift):
        return pltpu.make_async_copy(
            blocks[slot].at[:, pl.ds(shift, depth)],
            left.at[:, pl.ds(index * depth, depth)],
            block_sems.at[index],
        )

    def slab_copy(half, index):
        return pltpu.make_async_copy(
            slabs[half][index],
            right.at[half, pl.ds(index * depth, depth), :],
            slab_sems.at[half, index],
        )

    for index, step in enumerate(steps):
        source = where_ref[step]
        slot_here = jnp.bitwise_xor(source // per, me)
        shift = pl.multiple_of((source % per) * depth, depth)
        for slot in range(4):

            @pl.when(slot_here == slot)
            def _(slot=slot):
                block_copy(index, slot, shift).start()

    for half in range(2):
        for index in range(count):
            slab_copy(half, index).start()
    for index in range(count):
        block_copy(index, 0, 0).wait()
    half_columns = right.shape[2]
    if last:
        staged, out_sems = refs[5:]
    for half in range(2):
        columns = pl.ds(half * half_columns, half_columns)
        for index in range(count):
            slab_copy(half, index).wait()

        def rows_tile(step, carry):
            at = pl.ds(pl.multiple_of(step * ROW_TILE, ROW_TILE), ROW_TILE)
            product = jnp.dot(left[at, :], right[half], preferred_element_type=jnp.float32)
            if has_base:
                product = product + base_ref[at, columns]
            if last:
                staged[at, columns] = product.astype(jnp.bfloat16)
            else:
                out_ref[at, columns] = product
            return carry

        lax.fori_loop(0, rows // ROW_TILE, rows_tile, 0)
        if last:
            pltpu.make_async_copy(
                staged.at[:, columns], out_ref.at[:, columns], out_sems.at[half]
            ).start()
    if last:
        for half in range(2):
            columns = pl.ds(half * half_columns, half_columns)
            pltpu.make_async_copy(
                staged.at[:, columns], out_ref.at[:, columns], out_sems.at[half]
            ).wait()


def ring_product(where, blocks, steps, slabs, base, last):
    count = len(steps)
    rows = blocks[0].shape[0]
    depth, half = slabs[0][0].shape
    in_hbm = pl.BlockSpec(memory_space=pltpu.HBM)
    in_vmem = pl.BlockSpec(memory_space=pltpu.VMEM)
    scratch = [
        pltpu.VMEM((rows, count * depth), jnp.bfloat16),
        pltpu.VMEM((2, count * depth, half), jnp.bfloat16),
        pltpu.SemaphoreType.DMA((count,)),
        pltpu.SemaphoreType.DMA((2, count)),
    ]
    if last:
        scratch += [pltpu.VMEM((rows, 2 * half), jnp.bfloat16), pltpu.SemaphoreType.DMA((2,))]
    return pl.pallas_call(
        functools.partial(ring_product_kernel, steps, base is not None, last),
        out_shape=jax.ShapeDtypeStruct((rows, 2 * half), jnp.bfloat16 if last else jnp.float32),
        in_specs=[pl.BlockSpec(memory_space=pltpu.SMEM)]
        + [in_hbm] * (4 + 2 * count)
        + [in_vmem] * (base is not None),
        out_specs=in_hbm if last else in_vmem,
        scratch_shapes=scratch,
        compiler_params=pltpu.CompilerParams(vmem_limit_bytes=(8 + 4 * count) << 20),
        cost_estimate=pl.CostEstimate(
            flops=1 << 20, transcendentals=0, bytes_accessed=1 << 20
        ),
        name="ring_product",
    )(
        where,
        *[
            pltpu.with_memory_space_constraint(x, pltpu.HBM)
            for x in (*blocks, *slabs[0], *slabs[1])
        ],
        *([] if base is None else [base]),
    )


def project_ring(wo, inputs, attend_with):
    pb_size = lax.axis_size("pb")
    depth, columns = wo.shape
    ring = ring_of(pb_size)
    forward = [(ring[i], ring[(i + 1) % pb_size]) for i in range(pb_size)]
    backward = [(b, a) for a, b in forward]
    half = columns // 2
    far = pb_size // 2
    parts = [wo[:, :half], wo[:, half:]]
    inputs, parts[0], parts[1] = lax.optimization_barrier((inputs, parts[0], parts[1]))
    slabs = [[(0, part)] for part in parts]
    moving = [[part, part] for part in parts]

    def travel(hop):
        for part in range(2):
            if hop < far or part == 0:
                moving[part][0] = lax.ppermute(moving[part][0], "pb", forward)
            if hop < far or part == 1:
                moving[part][1] = lax.ppermute(moving[part][1], "pb", backward)

    def keep(hop):
        for part in range(2):
            if hop < far or part == 0:
                slabs[part].append((-hop, moving[part][0]))
            if hop < far or part == 1:
                slabs[part].append((hop, moving[part][1]))

    def gate(value):
        value, moving[0][0], moving[0][1] = lax.optimization_barrier(
            (value, moving[0][0], moving[0][1])
        )
        return value

    travel(1)
    attn = attend_with(inputs, gate)
    keep(1)
    for hop in range(2, far + 1):
        travel(hop)
        keep(hop)
    across = lax.ppermute(attn, "ka", [(i, i ^ 2) for i in range(4)])
    beside = lax.ppermute(attn, "ka", [(i, i ^ 1) for i in range(4)])
    corner = lax.ppermute(attn, "ka", [(i, i ^ 3) for i in range(4)])
    around = jnp.asarray(
        [[ring[(ring.index(p) + step) % pb_size] for step in range(pb_size)] for p in range(pb_size)],
        jnp.int32,
    )
    mine = lax.dynamic_slice(around, (lax.axis_index("pb"), 0), (1, pb_size))[0]
    where = jnp.concatenate([mine, lax.axis_index("ka")[None].astype(jnp.int32)])
    blocks = [attn, beside, across, corner]
    at_step = [{offset % pb_size: slab for offset, slab in slabs[part]} for part in range(2)]
    total = None
    for offsets in ((0, -1, 1, -2, 2), (-3, 3), (4,)):
        chosen = [[at_step[part][offset % pb_size] for offset in offsets] for part in range(2)]
        steps = tuple(offset % pb_size for offset in offsets)
        total = ring_product(where, blocks, steps, chosen, total, offsets == (far,))
    return total


def shards(queries, keys, values, block_ids, counts, refresh, cached_attn, wo):
    groups = lax.axis_size("ka")

    def attend_with(inputs, gate=lambda x: x):
        queries, keys, values, old = inputs
        return attend(
            block_ids[0, 0], counts[0, 0], refresh[0, 0], queries, old, own_head_keys_values(keys, values, gate)
        )

    inputs = (queries[0], keys, values, cached_attn[0])
    if lax.axis_size("pb") == 8 and groups == 4:
        mixed = project_ring(wo, inputs, attend_with)
    else:
        attn_full = lax.all_gather(attend_with(inputs), "ka", axis=1, tiled=True)
        mixed = jnp.dot(
            attn_full, lax.all_gather(wo, "pb", axis=0, tiled=True), preferred_element_type=jnp.float32
        ).astype(jnp.bfloat16)
    return mixed[None]


def solution(mesh):
    placed = (
        P(None, "pb", "ka"),
        P("ka", None),
        P("ka", None),
        P(None, "pb", None),
        P(None, "pb"),
        P(None, "pb"),
        P(None, "pb", "ka"),
        P("pb", "ka"),
    )
    return jax.shard_map(
        shards, mesh=mesh, in_specs=placed, out_specs=P(None, "pb", "ka"), check_vma=False
    )
```

```python
import functools
import math

import jax
import jax.numpy as jnp
from jax import lax
from jax.experimental import pallas as pl
from jax.experimental.pallas import tpu as pltpu
from jax.sharding import PartitionSpec as P

HEAD_SIZE = 128
QUERY_HEAD_COUNT = 32
KEY_VALUE_HEADS = 4
QUERY_BLOCK_SIZE = 512
KEY_BLOCK_TOKENS = 128
RATIO = QUERY_HEAD_COUNT // KEY_VALUE_HEADS
LOWEST = -1e30
EXP2_SCALE = math.log2(math.e) / math.sqrt(HEAD_SIZE)


GROUP = 4


def attention_kernel(
    heads, slots, part_rows, first_rows, targets, meta_ref, q_hbm, old_hbm, *refs
):
    kv_parts, (out_ref, q_ref, kv_ref, peak_ref, denom_ref, acc_ref, sems) = refs[:-7], refs[-7:]
    live = meta_ref[0]
    flag = meta_ref[1]

    @pl.when(flag <= 0)
    def _():
        copy = pltpu.make_async_copy(old_hbm, out_ref, sems.at[0])
        copy.start()
        copy.wait()

    @pl.when(flag > 0)
    def _():
        copies = [pltpu.make_async_copy(q_hbm, q_ref, sems.at[0])]
        for index, (part, first_row, target) in enumerate(zip(kv_parts, first_rows, targets)):
            column = pl.multiple_of(meta_ref[2 + slots + 2 * index] * HEAD_SIZE, HEAD_SIZE)
            start = pl.multiple_of(meta_ref[3 + slots + 2 * index] * part_rows, part_rows)
            copies.append(
                pltpu.make_async_copy(
                    part.at[pl.ds(first_row, part_rows), pl.ds(column, HEAD_SIZE)],
                    kv_ref.at[pl.ds(start, part_rows), pl.ds(target * HEAD_SIZE, HEAD_SIZE)],
                    sems.at[1 + index],
                )
            )
        for copy in copies:
            copy.start()
        peak_ref[...] = jnp.full_like(peak_ref, LOWEST)
        denom_ref[...] = jnp.zeros_like(denom_ref)
        acc_ref[...] = jnp.zeros_like(acc_ref)
        for copy in copies:
            copy.wait()

        def group(step, carry):
            tiles, biases = [], []
            for member in range(GROUP):
                slot = step * GROUP + member
                if member > 0:
                    present = slot < live
                    block = jnp.where(
                        present, meta_ref[2 + jnp.minimum(slot, slots - 1)], 0
                    )
                    biases.append(jnp.where(present, 0.0, LOWEST).astype(jnp.float32))
                else:
                    block = meta_ref[2 + slot]
                    biases.append(None)
                row = pl.multiple_of(block * KEY_BLOCK_TOKENS, KEY_BLOCK_TOKENS)
                tiles.append(kv_ref[pl.ds(row, KEY_BLOCK_TOKENS), :])
            tile = jnp.concatenate(tiles, axis=0)
            key_tile = tile[:, :HEAD_SIZE]
            value_tile = tile[:, HEAD_SIZE:].T
            value_tile = jnp.concatenate(
                [value_tile, jnp.ones((16, value_tile.shape[1]), jnp.bfloat16)], axis=0
            )
            for head in range(heads):
                query = q_ref[:, head * HEAD_SIZE : (head + 1) * HEAD_SIZE]
                scores = lax.dot_general(
                    key_tile, query, (((1,), (1,)), ((), ())), preferred_element_type=jnp.float32
                )
                parts = [
                    scores[member * KEY_BLOCK_TOKENS : (member + 1) * KEY_BLOCK_TOKENS]
                    for member in range(GROUP)
                ]
                parts = [p if b is None else p + b for p, b in zip(parts, biases)]
                top = functools.reduce(jnp.maximum, parts)
                old_peak = peak_ref[head]
                peak = jnp.maximum(old_peak, jnp.max(top, axis=0, keepdims=True))
                decay = jnp.exp2((old_peak - peak) * EXP2_SCALE)
                parts = [jnp.exp2((p - peak) * EXP2_SCALE) for p in parts]
                peak_ref[head] = peak
                weights = jnp.concatenate([p.astype(jnp.bfloat16) for p in parts], axis=0)
                update = lax.dot_general(
                    value_tile, weights, (((1,), (0,)), ((), ())), preferred_element_type=jnp.float32
                )
                denom_ref[head] = denom_ref[head] * decay + update[HEAD_SIZE : HEAD_SIZE + 1]
                acc_ref[head] = acc_ref[head] * decay + update[:HEAD_SIZE]
            return carry

        lax.fori_loop(0, (live + GROUP - 1) // GROUP, group, 0)
        for head in range(heads):
            result = acc_ref[head] / denom_ref[head]
            out_ref[:, head * HEAD_SIZE : (head + 1) * HEAD_SIZE] = result.T.astype(jnp.bfloat16)


def attend(block_list, live, flag, queries, old, key_values):
    part_rows, sources = key_values
    arrays, first_rows, heads_at, targets, places = zip(*sources)
    rows, width = queries.shape
    heads = width // HEAD_SIZE
    slots = block_list.shape[0]
    spots = [value[None] for pair in zip(heads_at, places) for value in pair]
    meta = jnp.concatenate([live[None], flag[None], block_list, *spots])
    in_hbm = pl.BlockSpec(memory_space=pltpu.HBM)
    return pl.pallas_call(
        functools.partial(attention_kernel, heads, slots, part_rows, first_rows, targets),
        out_shape=jax.ShapeDtypeStruct((rows, width), jnp.bfloat16),
        in_specs=[pl.BlockSpec(memory_space=pltpu.SMEM)] + [in_hbm] * (2 + len(arrays)),
        out_specs=pl.BlockSpec(memory_space=pltpu.VMEM),
        scratch_shapes=[
            pltpu.VMEM((rows, width), jnp.bfloat16),
            pltpu.VMEM((part_rows * len(arrays) // 2, 2 * HEAD_SIZE), jnp.bfloat16),
            pltpu.VMEM((heads, 1, rows), jnp.float32),
            pltpu.VMEM((heads, 1, rows), jnp.float32),
            pltpu.VMEM((heads, HEAD_SIZE, rows), jnp.float32),
            pltpu.SemaphoreType.DMA((1 + len(arrays),)),
        ],
        compiler_params=pltpu.CompilerParams(vmem_limit_bytes=24 << 20),
        cost_estimate=pl.CostEstimate(
            flops=1 << 20, transcendentals=0, bytes_accessed=1 << 20
        ),
        name="attend",
    )(
        meta,
        *[
            pltpu.with_memory_space_constraint(x, pltpu.HBM)
            for x in (queries, old, *arrays)
        ],
    )


def own_head_keys_values(keys, values, gate=lambda x: x):
    groups = lax.axis_size("ka")
    me = lax.axis_index("ka")
    rows = keys.shape[0]
    if groups == KEY_VALUE_HEADS == 4:
        x, core = me // 2, me % 2
        pair = 2 * HEAD_SIZE

        def heads_of(array, chip):
            return lax.dynamic_slice(array, (0, chip * pair), (rows, pair))

        def head_of(array, head):
            return lax.dynamic_slice(array, (0, head * HEAD_SIZE), (rows, HEAD_SIZE))

        across = [
            lax.ppermute(heads_of(a, 1 - x), "ka", [(i, i ^ 2) for i in range(4)])
            for a in (keys, values)
        ]
        across = gate(across)
        beside = lax.ppermute(
            jnp.concatenate(
                [
                    jnp.concatenate([head_of(a, 2 * x + 1 - core) for a in (keys, values)], axis=1),
                    jnp.concatenate([head_of(a, 1 - core) for a in across], axis=1),
                ],
                axis=0,
            ),
            "ka",
            [(i, i ^ 1) for i in range(4)],
        )
        near, far = jnp.bitwise_xor(me, 1), jnp.bitwise_xor(me, 3)
        sources = [
            (keys, 0, me, 0, me),
            (values, 0, me, 1, me),
            (across[0], 0, core, 0, jnp.bitwise_xor(me, 2)),
            (across[1], 0, core, 1, jnp.bitwise_xor(me, 2)),
        ]
        for side in range(2):
            for row, place in ((0, near), (rows, far)):
                sources.append((beside, row, jnp.int32(side), side, place))
        return rows, sources
    both = jnp.concatenate(
        [
            keys.reshape(rows, KEY_VALUE_HEADS, HEAD_SIZE),
            values.reshape(rows, KEY_VALUE_HEADS, HEAD_SIZE),
        ],
        axis=2,
    )
    both = jnp.repeat(both, groups // KEY_VALUE_HEADS, axis=1)
    everything = lax.all_to_all(
        both.reshape(rows, groups * 2 * HEAD_SIZE), "ka", split_axis=1, concat_axis=0, tiled=True
    )
    first = jnp.int32(0)
    return everything.shape[0], [(everything, 0, jnp.int32(side), side, first) for side in range(2)]


def ring_of(pb_size):
    if pb_size == 8:
        return [0, 2, 4, 6, 7, 5, 3, 1]
    return list(range(pb_size))


ROW_TILE = 128
IN_HBM = pl.BlockSpec(memory_space=pltpu.HBM)
IN_VMEM = pl.BlockSpec(memory_space=pltpu.VMEM)
IN_SMEM = pl.BlockSpec(memory_space=pltpu.SMEM)
SMALL_COST = pl.CostEstimate(flops=1 << 20, transcendentals=0, bytes_accessed=1 << 20)


def pinned(values, space):
    return [pltpu.with_memory_space_constraint(x, space) for x in values]


def ring_product_kernel(steps, spare_step, where_ref, *refs):
    count = len(steps)
    blocks, slabs, refs = refs[:4], (refs[4 : 4 + count], refs[4 + count : 4 + 2 * count]), refs[4 + 2 * count :]
    if spare_step is not None:
        base_ref, out_ref, spare_ref = refs[:3]
        refs = refs[3:]
    else:
        out_ref, refs = refs[0], refs[1:]
    left, right, block_sems, slab_sems = refs
    rows, depth = left.shape[0], right.shape[1] // count
    per = blocks[0].shape[1] // depth
    me = where_ref[where_ref.shape[0] - 1]

    def block_copy(index, slot, shift):
        target = spare_ref if index == count else left.at[:, pl.ds(index * depth, depth)]
        return pltpu.make_async_copy(
            blocks[slot].at[:, pl.ds(shift, depth)], target, block_sems.at[index]
        )

    def slab_copy(half, index):
        return pltpu.make_async_copy(
            slabs[half][index],
            right.at[half, pl.ds(index * depth, depth), :],
            slab_sems.at[half, index],
        )

    all_steps = steps if spare_step is None else (*steps, spare_step)
    for index, step in enumerate(all_steps):
        source = where_ref[step]
        slot_here = jnp.bitwise_xor(source // per, me)
        shift = pl.multiple_of((source % per) * depth, depth)
        for slot in range(4):

            @pl.when(slot_here == slot)
            def _(slot=slot):
                block_copy(index, slot, shift).start()

    for half in range(2):
        for index in range(count):
            slab_copy(half, index).start()
    for index in range(len(all_steps)):
        block_copy(index, 0, 0).wait()
    half_columns = right.shape[2]
    for half in range(2):
        columns = pl.ds(half * half_columns, half_columns)
        for index in range(count):
            slab_copy(half, index).wait()

        def rows_tile(step, carry):
            at = pl.ds(pl.multiple_of(step * ROW_TILE, ROW_TILE), ROW_TILE)
            product = jnp.dot(left[at, :], right[half], preferred_element_type=jnp.float32)
            if spare_step is not None:
                product = product + base_ref[at, columns]
            out_ref[at, columns] = product
            return carry

        lax.fori_loop(0, rows // ROW_TILE, rows_tile, 0)


def ring_product(where, blocks, steps, slabs, base=None, spare_step=None):
    count = len(steps)
    rows = blocks[0].shape[0]
    depth, half = slabs[0][0].shape
    spare = spare_step is not None
    out_shape = [jax.ShapeDtypeStruct((rows, 2 * half), jnp.float32)]
    if spare:
        out_shape.append(jax.ShapeDtypeStruct((rows, depth), jnp.bfloat16))
    return pl.pallas_call(
        functools.partial(ring_product_kernel, steps, spare_step),
        out_shape=out_shape,
        in_specs=[IN_SMEM] + [IN_HBM] * (4 + 2 * count) + [IN_VMEM] * spare,
        out_specs=[IN_VMEM] * len(out_shape),
        scratch_shapes=[
            pltpu.VMEM((rows, count * depth), jnp.bfloat16),
            pltpu.VMEM((2, count * depth, half), jnp.bfloat16),
            pltpu.SemaphoreType.DMA((count + spare,)),
            pltpu.SemaphoreType.DMA((2, count)),
        ],
        compiler_params=pltpu.CompilerParams(vmem_limit_bytes=(6 + 4 * count) << 20),
        cost_estimate=SMALL_COST,
        name="ring_product",
    )(
        where,
        *pinned([*blocks, *slabs[0], *slabs[1]], pltpu.HBM),
        *(pinned([base], pltpu.VMEM) if spare else []),
    )


def last_product_kernel(block_ref, left_slab, right_slab, base_ref, out_ref, staged, sems):
    half = left_slab.shape[1]

    def tile_copy(tile):
        at = pl.ds(tile * ROW_TILE, ROW_TILE)
        return pltpu.make_async_copy(staged.at[at, :], out_ref.at[at, :], sems.at[tile])

    tiles = block_ref.shape[0] // ROW_TILE
    for tile in range(tiles):
        at = pl.ds(tile * ROW_TILE, ROW_TILE)
        for slab, start in ((left_slab, 0), (right_slab, half)):
            columns = pl.ds(start, half)
            product = jnp.dot(block_ref[at, :], slab[...], preferred_element_type=jnp.float32)
            staged[at, columns] = (product + base_ref[at, columns]).astype(jnp.bfloat16)
        tile_copy(tile).start()
    for tile in range(tiles):
        tile_copy(tile).wait()


def last_product(block, left_slab, right_slab, base):
    rows, columns = base.shape
    return pl.pallas_call(
        last_product_kernel,
        out_shape=jax.ShapeDtypeStruct((rows, columns), jnp.bfloat16),
        in_specs=[IN_VMEM] * 4,
        out_specs=IN_HBM,
        scratch_shapes=[
            pltpu.VMEM((rows, columns), jnp.bfloat16),
            pltpu.SemaphoreType.DMA((rows // ROW_TILE,)),
        ],
        compiler_params=pltpu.CompilerParams(vmem_limit_bytes=8 << 20),
        cost_estimate=SMALL_COST,
        name="last_product",
    )(*pinned([block, left_slab, right_slab, base], pltpu.VMEM))


def project_ring(wo, inputs, attend_with):
    pb_size = lax.axis_size("pb")
    depth, columns = wo.shape
    ring = ring_of(pb_size)
    forward = [(ring[i], ring[(i + 1) % pb_size]) for i in range(pb_size)]
    backward = [(b, a) for a, b in forward]
    half = columns // 2
    far = pb_size // 2
    parts = [wo[:, :half], wo[:, half:]]
    inputs, parts[0], parts[1] = lax.optimization_barrier((inputs, parts[0], parts[1]))
    slabs = [[(0, part)] for part in parts]
    moving = [[part, part] for part in parts]

    def travel(hop):
        for part in range(2):
            if hop < far or part == 0:
                moving[part][0] = lax.ppermute(moving[part][0], "pb", forward)
            if hop < far or part == 1:
                moving[part][1] = lax.ppermute(moving[part][1], "pb", backward)

    def keep(hop):
        for part in range(2):
            if hop < far or part == 0:
                slabs[part].append((-hop, moving[part][0]))
            if hop < far or part == 1:
                slabs[part].append((hop, moving[part][1]))

    def gate(value):
        value, moving[0][0], moving[0][1] = lax.optimization_barrier(
            (value, moving[0][0], moving[0][1])
        )
        return value

    travel(1)
    attn = attend_with(inputs, gate)
    keep(1)
    for hop in range(2, far + 1):
        travel(hop)
        keep(hop)
    across = lax.ppermute(attn, "ka", [(i, i ^ 2) for i in range(4)])
    beside = lax.ppermute(attn, "ka", [(i, i ^ 1) for i in range(4)])
    corner = lax.ppermute(attn, "ka", [(i, i ^ 3) for i in range(4)])
    around = jnp.asarray(
        [[ring[(ring.index(p) + step) % pb_size] for step in range(pb_size)] for p in range(pb_size)],
        jnp.int32,
    )
    mine = lax.dynamic_slice(around, (lax.axis_index("pb"), 0), (1, pb_size))[0]
    where = jnp.concatenate([mine, lax.axis_index("ka")[None].astype(jnp.int32)])
    blocks = [attn, beside, across, corner]
    at_step = [{offset % pb_size: slab for offset, slab in slabs[part]} for part in range(2)]

    def chosen(offsets):
        return [[at_step[part][offset % pb_size] for offset in offsets] for part in range(2)]

    def steps(offsets):
        return tuple(offset % pb_size for offset in offsets)

    early, late = (0, -1, 1, -2, 2), (-3, 3)
    (base,) = ring_product(where, blocks, steps(early), chosen(early))
    base, block = ring_product(where, blocks, steps(late), chosen(late), base, far)
    return last_product(block, at_step[0][far], at_step[1][far], base)


def shards(queries, keys, values, block_ids, counts, refresh, cached_attn, wo):
    groups = lax.axis_size("ka")

    def attend_with(inputs, gate=lambda x: x):
        queries, keys, values, old = inputs
        return attend(
            block_ids[0, 0], counts[0, 0], refresh[0, 0], queries, old, own_head_keys_values(keys, values, gate)
        )

    inputs = (queries[0], keys, values, cached_attn[0])
    if lax.axis_size("pb") == 8 and groups == 4:
        mixed = project_ring(wo, inputs, attend_with)
    else:
        attn_full = lax.all_gather(attend_with(inputs), "ka", axis=1, tiled=True)
        mixed = jnp.dot(
            attn_full, lax.all_gather(wo, "pb", axis=0, tiled=True), preferred_element_type=jnp.float32
        ).astype(jnp.bfloat16)
    return mixed[None]


def solution(mesh):
    placed = (
        P(None, "pb", "ka"),
        P("ka", None),
        P("ka", None),
        P(None, "pb", None),
        P(None, "pb"),
        P(None, "pb"),
        P(None, "pb", "ka"),
        P("pb", "ka"),
    )
    return jax.shard_map(
        shards, mesh=mesh, in_specs=placed, out_specs=P(None, "pb", "ka"), check_vma=False
    )
```

```python
import functools
import math

import jax
import jax.numpy as jnp
from jax import lax
from jax.experimental import pallas as pl
from jax.experimental.pallas import tpu as pltpu
from jax.sharding import PartitionSpec as P

HEAD_SIZE = 128
QUERY_HEAD_COUNT = 32
KEY_VALUE_HEADS = 4
QUERY_BLOCK_SIZE = 512
KEY_BLOCK_TOKENS = 128
RATIO = QUERY_HEAD_COUNT // KEY_VALUE_HEADS
LOWEST = -1e30
EXP2_SCALE = math.log2(math.e) / math.sqrt(HEAD_SIZE)


GROUP = 4


def attention_kernel(
    heads, slots, part_rows, first_rows, targets, meta_ref, q_hbm, old_hbm, *refs
):
    kv_parts, (out_ref, q_ref, kv_ref, peak_ref, denom_ref, acc_ref, sems) = refs[:-7], refs[-7:]
    live = meta_ref[0]
    flag = meta_ref[1]

    @pl.when(flag <= 0)
    def _():
        copy = pltpu.make_async_copy(old_hbm, out_ref, sems.at[0])
        copy.start()
        copy.wait()

    @pl.when(flag > 0)
    def _():
        copies = [pltpu.make_async_copy(q_hbm, q_ref, sems.at[0])]
        for index, (part, first_row, target) in enumerate(zip(kv_parts, first_rows, targets)):
            column = pl.multiple_of(meta_ref[2 + slots + 2 * index] * HEAD_SIZE, HEAD_SIZE)
            start = pl.multiple_of(meta_ref[3 + slots + 2 * index] * part_rows, part_rows)
            copies.append(
                pltpu.make_async_copy(
                    part.at[pl.ds(first_row, part_rows), pl.ds(column, HEAD_SIZE)],
                    kv_ref.at[pl.ds(start, part_rows), pl.ds(target * HEAD_SIZE, HEAD_SIZE)],
                    sems.at[1 + index],
                )
            )
        for copy in copies:
            copy.start()
        peak_ref[...] = jnp.full_like(peak_ref, LOWEST)
        denom_ref[...] = jnp.zeros_like(denom_ref)
        acc_ref[...] = jnp.zeros_like(acc_ref)
        for copy in copies:
            copy.wait()

        def group(step, carry):
            tiles, biases = [], []
            for member in range(GROUP):
                slot = step * GROUP + member
                if member > 0:
                    present = slot < live
                    block = jnp.where(
                        present, meta_ref[2 + jnp.minimum(slot, slots - 1)], 0
                    )
                    biases.append(jnp.where(present, 0.0, LOWEST).astype(jnp.float32))
                else:
                    block = meta_ref[2 + slot]
                    biases.append(None)
                row = pl.multiple_of(block * KEY_BLOCK_TOKENS, KEY_BLOCK_TOKENS)
                tiles.append(kv_ref[pl.ds(row, KEY_BLOCK_TOKENS), :])
            tile = jnp.concatenate(tiles, axis=0)
            key_tile = tile[:, :HEAD_SIZE]
            value_tile = tile[:, HEAD_SIZE:].T
            value_tile = jnp.concatenate(
                [value_tile, jnp.ones((16, value_tile.shape[1]), jnp.bfloat16)], axis=0
            )
            for head in range(heads):
                query = q_ref[:, head * HEAD_SIZE : (head + 1) * HEAD_SIZE]
                scores = lax.dot_general(
                    key_tile, query, (((1,), (1,)), ((), ())), preferred_element_type=jnp.float32
                )
                parts = [
                    scores[member * KEY_BLOCK_TOKENS : (member + 1) * KEY_BLOCK_TOKENS]
                    for member in range(GROUP)
                ]
                parts = [p if b is None else p + b for p, b in zip(parts, biases)]
                top = functools.reduce(jnp.maximum, parts)
                old_peak = peak_ref[head]
                peak = jnp.maximum(old_peak, jnp.max(top, axis=0, keepdims=True))
                decay = jnp.exp2((old_peak - peak) * EXP2_SCALE)
                parts = [jnp.exp2((p - peak) * EXP2_SCALE) for p in parts]
                peak_ref[head] = peak
                weights = jnp.concatenate([p.astype(jnp.bfloat16) for p in parts], axis=0)
                update = lax.dot_general(
                    value_tile, weights, (((1,), (0,)), ((), ())), preferred_element_type=jnp.float32
                )
                denom_ref[head] = denom_ref[head] * decay + update[HEAD_SIZE : HEAD_SIZE + 1]
                acc_ref[head] = acc_ref[head] * decay + update[:HEAD_SIZE]
            return carry

        lax.fori_loop(0, (live + GROUP - 1) // GROUP, group, 0)
        for head in range(heads):
            result = acc_ref[head] / denom_ref[head]
            out_ref[:, head * HEAD_SIZE : (head + 1) * HEAD_SIZE] = result.T.astype(jnp.bfloat16)


def attend(block_list, live, flag, queries, old, key_values):
    part_rows, sources = key_values
    arrays, first_rows, heads_at, targets, places = zip(*sources)
    rows, width = queries.shape
    heads = width // HEAD_SIZE
    slots = block_list.shape[0]
    spots = [value[None] for pair in zip(heads_at, places) for value in pair]
    meta = jnp.concatenate([live[None], flag[None], block_list, *spots])
    in_hbm = pl.BlockSpec(memory_space=pltpu.HBM)
    return pl.pallas_call(
        functools.partial(attention_kernel, heads, slots, part_rows, first_rows, targets),
        out_shape=jax.ShapeDtypeStruct((rows, width), jnp.bfloat16),
        in_specs=[pl.BlockSpec(memory_space=pltpu.SMEM)] + [in_hbm] * (2 + len(arrays)),
        out_specs=pl.BlockSpec(memory_space=pltpu.VMEM),
        scratch_shapes=[
            pltpu.VMEM((rows, width), jnp.bfloat16),
            pltpu.VMEM((part_rows * len(arrays) // 2, 2 * HEAD_SIZE), jnp.bfloat16),
            pltpu.VMEM((heads, 1, rows), jnp.float32),
            pltpu.VMEM((heads, 1, rows), jnp.float32),
            pltpu.VMEM((heads, HEAD_SIZE, rows), jnp.float32),
            pltpu.SemaphoreType.DMA((1 + len(arrays),)),
        ],
        compiler_params=pltpu.CompilerParams(vmem_limit_bytes=24 << 20),
        cost_estimate=pl.CostEstimate(
            flops=1 << 20, transcendentals=0, bytes_accessed=1 << 20
        ),
        name="attend",
    )(
        meta,
        *[
            pltpu.with_memory_space_constraint(x, pltpu.HBM)
            for x in (queries, old, *arrays)
        ],
    )


def own_head_keys_values(keys, values, gate=lambda x: x):
    groups = lax.axis_size("ka")
    me = lax.axis_index("ka")
    rows = keys.shape[0]
    if groups == KEY_VALUE_HEADS == 4:
        x, core = me // 2, me % 2
        pair = 2 * HEAD_SIZE

        def heads_of(array, chip):
            return lax.dynamic_slice(array, (0, chip * pair), (rows, pair))

        def head_of(array, head):
            return lax.dynamic_slice(array, (0, head * HEAD_SIZE), (rows, HEAD_SIZE))

        across = [
            lax.ppermute(heads_of(a, 1 - x), "ka", [(i, i ^ 2) for i in range(4)])
            for a in (keys, values)
        ]
        across = gate(across)
        beside = lax.ppermute(
            jnp.concatenate(
                [
                    jnp.concatenate([head_of(a, 2 * x + 1 - core) for a in (keys, values)], axis=1),
                    jnp.concatenate([head_of(a, 1 - core) for a in across], axis=1),
                ],
                axis=0,
            ),
            "ka",
            [(i, i ^ 1) for i in range(4)],
        )
        near, far = jnp.bitwise_xor(me, 1), jnp.bitwise_xor(me, 3)
        sources = [
            (keys, 0, me, 0, me),
            (values, 0, me, 1, me),
            (across[0], 0, core, 0, jnp.bitwise_xor(me, 2)),
            (across[1], 0, core, 1, jnp.bitwise_xor(me, 2)),
        ]
        for side in range(2):
            for row, place in ((0, near), (rows, far)):
                sources.append((beside, row, jnp.int32(side), side, place))
        return rows, sources
    both = jnp.concatenate(
        [
            keys.reshape(rows, KEY_VALUE_HEADS, HEAD_SIZE),
            values.reshape(rows, KEY_VALUE_HEADS, HEAD_SIZE),
        ],
        axis=2,
    )
    both = jnp.repeat(both, groups // KEY_VALUE_HEADS, axis=1)
    everything = lax.all_to_all(
        both.reshape(rows, groups * 2 * HEAD_SIZE), "ka", split_axis=1, concat_axis=0, tiled=True
    )
    first = jnp.int32(0)
    return everything.shape[0], [(everything, 0, jnp.int32(side), side, first) for side in range(2)]


def ring_of(pb_size):
    if pb_size == 8:
        return [0, 2, 4, 6, 7, 5, 3, 1]
    return list(range(pb_size))


ROW_TILE = 128
IN_HBM = pl.BlockSpec(memory_space=pltpu.HBM)
IN_VMEM = pl.BlockSpec(memory_space=pltpu.VMEM)
IN_SMEM = pl.BlockSpec(memory_space=pltpu.SMEM)
SMALL_COST = pl.CostEstimate(flops=1 << 20, transcendentals=0, bytes_accessed=1 << 20)


def pinned(values, space):
    return [pltpu.with_memory_space_constraint(x, space) for x in values]


def ring_product_kernel(steps, spare_step, where_ref, *refs):
    count = len(steps)
    blocks, slabs, refs = refs[:4], (refs[4 : 4 + count], refs[4 + count : 4 + 2 * count]), refs[4 + 2 * count :]
    if spare_step is not None:
        base_ref, out_ref, spare_ref = refs[:3]
        refs = refs[3:]
    else:
        out_ref, refs = refs[0], refs[1:]
    left, block_sems = refs
    depth = slabs[0][0].shape[0]
    per = blocks[0].shape[1] // depth
    me = where_ref[where_ref.shape[0] - 1]

    def block_copy(index, slot, shift):
        target = spare_ref if index == count else left.at[:, pl.ds(index * depth, depth)]
        return pltpu.make_async_copy(
            blocks[slot].at[:, pl.ds(shift, depth)], target, block_sems.at[index]
        )

    all_steps = steps if spare_step is None else (*steps, spare_step)
    for index, step in enumerate(all_steps):
        source = where_ref[step]
        slot_here = jnp.bitwise_xor(source // per, me)
        shift = pl.multiple_of((source % per) * depth, depth)
        for slot in range(4):

            @pl.when(slot_here == slot)
            def _(slot=slot):
                block_copy(index, slot, shift).start()

    for index in range(len(all_steps)):
        block_copy(index, 0, 0).wait()
    half_columns = slabs[0][0].shape[1]
    for half in range(2):
        columns = pl.ds(half * half_columns, half_columns)

        def rows_tile(step, carry):
            at = pl.ds(pl.multiple_of(step * ROW_TILE, ROW_TILE), ROW_TILE)
            total = None if spare_step is None else base_ref[at, columns]
            for index in range(count):
                product = jnp.dot(
                    left[at, index * depth : (index + 1) * depth],
                    slabs[half][index][...],
                    preferred_element_type=jnp.float32,
                )
                total = product if total is None else total + product
            out_ref[at, columns] = total
            return carry

        lax.fori_loop(0, left.shape[0] // ROW_TILE, rows_tile, 0)


def ring_product(where, blocks, steps, slabs, base=None, spare_step=None):
    count = len(steps)
    rows = blocks[0].shape[0]
    depth, half = slabs[0][0].shape
    spare = spare_step is not None
    out_shape = [jax.ShapeDtypeStruct((rows, 2 * half), jnp.float32)]
    if spare:
        out_shape.append(jax.ShapeDtypeStruct((rows, depth), jnp.bfloat16))
    return pl.pallas_call(
        functools.partial(ring_product_kernel, steps, spare_step),
        out_shape=out_shape,
        in_specs=[IN_SMEM] + [IN_HBM] * 4 + [IN_VMEM] * (2 * count + spare),
        out_specs=[IN_VMEM] * len(out_shape),
        scratch_shapes=[
            pltpu.VMEM((rows, count * depth), jnp.bfloat16),
            pltpu.SemaphoreType.DMA((count + spare,)),
        ],
        compiler_params=pltpu.CompilerParams(vmem_limit_bytes=12 << 20),
        cost_estimate=SMALL_COST,
        name="ring_product",
    )(
        where,
        *pinned(blocks, pltpu.HBM),
        *pinned([*slabs[0], *slabs[1], *([base] if spare else [])], pltpu.VMEM),
    )


def last_product_kernel(block_ref, left_slab, right_slab, base_ref, out_ref, staged, sems):
    half = left_slab.shape[1]

    def tile_copy(tile):
        at = pl.ds(tile * ROW_TILE, ROW_TILE)
        return pltpu.make_async_copy(staged.at[at, :], out_ref.at[at, :], sems.at[tile])

    tiles = block_ref.shape[0] // ROW_TILE
    for tile in range(tiles):
        at = pl.ds(tile * ROW_TILE, ROW_TILE)
        for slab, start in ((left_slab, 0), (right_slab, half)):
            columns = pl.ds(start, half)
            product = jnp.dot(block_ref[at, :], slab[...], preferred_element_type=jnp.float32)
            staged[at, columns] = (product + base_ref[at, columns]).astype(jnp.bfloat16)
        tile_copy(tile).start()
    for tile in range(tiles):
        tile_copy(tile).wait()


def last_product(block, left_slab, right_slab, base):
    rows, columns = base.shape
    return pl.pallas_call(
        last_product_kernel,
        out_shape=jax.ShapeDtypeStruct((rows, columns), jnp.bfloat16),
        in_specs=[IN_VMEM] * 4,
        out_specs=IN_HBM,
        scratch_shapes=[
            pltpu.VMEM((rows, columns), jnp.bfloat16),
            pltpu.SemaphoreType.DMA((rows // ROW_TILE,)),
        ],
        compiler_params=pltpu.CompilerParams(vmem_limit_bytes=8 << 20),
        cost_estimate=SMALL_COST,
        name="last_product",
    )(*pinned([block, left_slab, right_slab, base], pltpu.VMEM))


def project_ring(wo, inputs, attend_with):
    pb_size = lax.axis_size("pb")
    depth, columns = wo.shape
    ring = ring_of(pb_size)
    forward = [(ring[i], ring[(i + 1) % pb_size]) for i in range(pb_size)]
    backward = [(b, a) for a, b in forward]
    half = columns // 2
    far = pb_size // 2
    parts = [wo[:, :half], wo[:, half:]]
    inputs, parts[0], parts[1] = lax.optimization_barrier((inputs, parts[0], parts[1]))
    slabs = [[(0, part)] for part in parts]
    moving = [[part, part] for part in parts]

    def travel(hop):
        for part in range(2):
            if hop < far or part == 0:
                moving[part][0] = lax.ppermute(moving[part][0], "pb", forward)
            if hop < far or part == 1:
                moving[part][1] = lax.ppermute(moving[part][1], "pb", backward)

    def keep(hop):
        for part in range(2):
            if hop < far or part == 0:
                slabs[part].append((-hop, moving[part][0]))
            if hop < far or part == 1:
                slabs[part].append((hop, moving[part][1]))

    def gate(value):
        value, moving[0][0], moving[0][1] = lax.optimization_barrier(
            (value, moving[0][0], moving[0][1])
        )
        return value

    travel(1)
    attn = attend_with(inputs, gate)
    keep(1)
    for hop in range(2, far + 1):
        travel(hop)
        keep(hop)
    across = lax.ppermute(attn, "ka", [(i, i ^ 2) for i in range(4)])
    beside = lax.ppermute(attn, "ka", [(i, i ^ 1) for i in range(4)])
    corner = lax.ppermute(attn, "ka", [(i, i ^ 3) for i in range(4)])
    around = jnp.asarray(
        [[ring[(ring.index(p) + step) % pb_size] for step in range(pb_size)] for p in range(pb_size)],
        jnp.int32,
    )
    mine = lax.dynamic_slice(around, (lax.axis_index("pb"), 0), (1, pb_size))[0]
    where = jnp.concatenate([mine, lax.axis_index("ka")[None].astype(jnp.int32)])
    blocks = [attn, beside, across, corner]
    at_step = [{offset % pb_size: slab for offset, slab in slabs[part]} for part in range(2)]

    def chosen(offsets):
        return [[at_step[part][offset % pb_size] for offset in offsets] for part in range(2)]

    def steps(offsets):
        return tuple(offset % pb_size for offset in offsets)

    early, late = (0, -1, 1, -2, 2), (-3, 3)
    (base,) = ring_product(where, blocks, steps(early), chosen(early))
    base, block = ring_product(where, blocks, steps(late), chosen(late), base, far)
    return last_product(block, at_step[0][far], at_step[1][far], base)


def shards(queries, keys, values, block_ids, counts, refresh, cached_attn, wo):
    groups = lax.axis_size("ka")

    def attend_with(inputs, gate=lambda x: x):
        queries, keys, values, old = inputs
        return attend(
            block_ids[0, 0], counts[0, 0], refresh[0, 0], queries, old, own_head_keys_values(keys, values, gate)
        )

    inputs = (queries[0], keys, values, cached_attn[0])
    if lax.axis_size("pb") == 8 and groups == 4:
        mixed = project_ring(wo, inputs, attend_with)
    else:
        attn_full = lax.all_gather(attend_with(inputs), "ka", axis=1, tiled=True)
        mixed = jnp.dot(
            attn_full, lax.all_gather(wo, "pb", axis=0, tiled=True), preferred_element_type=jnp.float32
        ).astype(jnp.bfloat16)
    return mixed[None]


def solution(mesh):
    placed = (
        P(None, "pb", "ka"),
        P("ka", None),
        P("ka", None),
        P(None, "pb", None),
        P(None, "pb"),
        P(None, "pb"),
        P(None, "pb", "ka"),
        P("pb", "ka"),
    )
    return jax.shard_map(
        shards, mesh=mesh, in_specs=placed, out_specs=P(None, "pb", "ka"), check_vma=False
    )
```

```python
import functools
import math

import jax
import jax.numpy as jnp
from jax import lax
from jax.experimental import pallas as pl
from jax.experimental.pallas import tpu as pltpu
from jax.sharding import PartitionSpec as P

HEAD_SIZE = 128
QUERY_HEAD_COUNT = 32
KEY_VALUE_HEADS = 4
QUERY_BLOCK_SIZE = 512
KEY_BLOCK_TOKENS = 128
RATIO = QUERY_HEAD_COUNT // KEY_VALUE_HEADS
LOWEST = -1e30
EXP2_SCALE = math.log2(math.e) / math.sqrt(HEAD_SIZE)


GROUP = 4


def attention_kernel(
    heads, slots, part_rows, first_rows, targets, meta_ref, q_hbm, old_hbm, *refs
):
    kv_parts, (out_ref, q_ref, kv_ref, peak_ref, denom_ref, acc_ref, sems) = refs[:-7], refs[-7:]
    live = meta_ref[0]
    flag = meta_ref[1]

    @pl.when(flag <= 0)
    def _():
        copy = pltpu.make_async_copy(old_hbm, out_ref, sems.at[0])
        copy.start()
        copy.wait()

    @pl.when(flag > 0)
    def _():
        copies = [pltpu.make_async_copy(q_hbm, q_ref, sems.at[0])]
        for index, (part, first_row, target) in enumerate(zip(kv_parts, first_rows, targets)):
            column = pl.multiple_of(meta_ref[2 + slots + 2 * index] * HEAD_SIZE, HEAD_SIZE)
            start = pl.multiple_of(meta_ref[3 + slots + 2 * index] * part_rows, part_rows)
            copies.append(
                pltpu.make_async_copy(
                    part.at[pl.ds(first_row, part_rows), pl.ds(column, HEAD_SIZE)],
                    kv_ref.at[pl.ds(start, part_rows), pl.ds(target * HEAD_SIZE, HEAD_SIZE)],
                    sems.at[1 + index],
                )
            )
        for copy in copies:
            copy.start()
        peak_ref[...] = jnp.full_like(peak_ref, LOWEST)
        denom_ref[...] = jnp.zeros_like(denom_ref)
        acc_ref[...] = jnp.zeros_like(acc_ref)
        for copy in copies:
            copy.wait()

        def group(step, carry):
            tiles, biases = [], []
            for member in range(GROUP):
                slot = step * GROUP + member
                if member > 0:
                    present = slot < live
                    block = jnp.where(
                        present, meta_ref[2 + jnp.minimum(slot, slots - 1)], 0
                    )
                    biases.append(jnp.where(present, 0.0, LOWEST).astype(jnp.float32))
                else:
                    block = meta_ref[2 + slot]
                    biases.append(None)
                row = pl.multiple_of(block * KEY_BLOCK_TOKENS, KEY_BLOCK_TOKENS)
                tiles.append(kv_ref[pl.ds(row, KEY_BLOCK_TOKENS), :])
            tile = jnp.concatenate(tiles, axis=0)
            key_tile = tile[:, :HEAD_SIZE]
            value_tile = tile[:, HEAD_SIZE:].T
            value_tile = jnp.concatenate(
                [value_tile, jnp.ones((16, value_tile.shape[1]), jnp.bfloat16)], axis=0
            )
            for head in range(heads):
                query = q_ref[:, head * HEAD_SIZE : (head + 1) * HEAD_SIZE]
                scores = lax.dot_general(
                    key_tile, query, (((1,), (1,)), ((), ())), preferred_element_type=jnp.float32
                )
                parts = [
                    scores[member * KEY_BLOCK_TOKENS : (member + 1) * KEY_BLOCK_TOKENS]
                    for member in range(GROUP)
                ]
                parts = [p if b is None else p + b for p, b in zip(parts, biases)]
                top = functools.reduce(jnp.maximum, parts)
                old_peak = peak_ref[head]
                peak = jnp.maximum(old_peak, jnp.max(top, axis=0, keepdims=True))
                decay = jnp.exp2((old_peak - peak) * EXP2_SCALE)
                parts = [jnp.exp2((p - peak) * EXP2_SCALE) for p in parts]
                peak_ref[head] = peak
                weights = jnp.concatenate([p.astype(jnp.bfloat16) for p in parts], axis=0)
                update = lax.dot_general(
                    value_tile, weights, (((1,), (0,)), ((), ())), preferred_element_type=jnp.float32
                )
                denom_ref[head] = denom_ref[head] * decay + update[HEAD_SIZE : HEAD_SIZE + 1]
                acc_ref[head] = acc_ref[head] * decay + update[:HEAD_SIZE]
            return carry

        lax.fori_loop(0, (live + GROUP - 1) // GROUP, group, 0)
        for head in range(heads):
            result = acc_ref[head] / denom_ref[head]
            out_ref[:, head * HEAD_SIZE : (head + 1) * HEAD_SIZE] = result.T.astype(jnp.bfloat16)


def attend(block_list, live, flag, queries, old, key_values):
    part_rows, sources = key_values
    arrays, first_rows, heads_at, targets, places = zip(*sources)
    rows, width = queries.shape
    heads = width // HEAD_SIZE
    slots = block_list.shape[0]
    spots = [value[None] for pair in zip(heads_at, places) for value in pair]
    meta = jnp.concatenate([live[None], flag[None], block_list, *spots])
    in_hbm = pl.BlockSpec(memory_space=pltpu.HBM)
    return pl.pallas_call(
        functools.partial(attention_kernel, heads, slots, part_rows, first_rows, targets),
        out_shape=jax.ShapeDtypeStruct((rows, width), jnp.bfloat16),
        in_specs=[pl.BlockSpec(memory_space=pltpu.SMEM)] + [in_hbm] * (2 + len(arrays)),
        out_specs=pl.BlockSpec(memory_space=pltpu.VMEM),
        scratch_shapes=[
            pltpu.VMEM((rows, width), jnp.bfloat16),
            pltpu.VMEM((part_rows * len(arrays) // 2, 2 * HEAD_SIZE), jnp.bfloat16),
            pltpu.VMEM((heads, 1, rows), jnp.float32),
            pltpu.VMEM((heads, 1, rows), jnp.float32),
            pltpu.VMEM((heads, HEAD_SIZE, rows), jnp.float32),
            pltpu.SemaphoreType.DMA((1 + len(arrays),)),
        ],
        compiler_params=pltpu.CompilerParams(vmem_limit_bytes=24 << 20),
        cost_estimate=pl.CostEstimate(
            flops=1 << 20, transcendentals=0, bytes_accessed=1 << 20
        ),
        name="attend",
    )(
        meta,
        *[
            pltpu.with_memory_space_constraint(x, pltpu.HBM)
            for x in (queries, old, *arrays)
        ],
    )


def own_head_keys_values(keys, values, gate=lambda x: x):
    groups = lax.axis_size("ka")
    me = lax.axis_index("ka")
    rows = keys.shape[0]
    if groups == KEY_VALUE_HEADS == 4:
        x, core = me // 2, me % 2
        pair = 2 * HEAD_SIZE

        def heads_of(array, chip):
            return lax.dynamic_slice(array, (0, chip * pair), (rows, pair))

        def head_of(array, head):
            return lax.dynamic_slice(array, (0, head * HEAD_SIZE), (rows, HEAD_SIZE))

        across = [
            lax.ppermute(heads_of(a, 1 - x), "ka", [(i, i ^ 2) for i in range(4)])
            for a in (keys, values)
        ]
        across = gate(across)
        beside = lax.ppermute(
            jnp.concatenate(
                [
                    jnp.concatenate([head_of(a, 2 * x + 1 - core) for a in (keys, values)], axis=1),
                    jnp.concatenate([head_of(a, 1 - core) for a in across], axis=1),
                ],
                axis=0,
            ),
            "ka",
            [(i, i ^ 1) for i in range(4)],
        )
        near, far = jnp.bitwise_xor(me, 1), jnp.bitwise_xor(me, 3)
        sources = [
            (keys, 0, me, 0, me),
            (values, 0, me, 1, me),
            (across[0], 0, core, 0, jnp.bitwise_xor(me, 2)),
            (across[1], 0, core, 1, jnp.bitwise_xor(me, 2)),
        ]
        for side in range(2):
            for row, place in ((0, near), (rows, far)):
                sources.append((beside, row, jnp.int32(side), side, place))
        return rows, sources
    both = jnp.concatenate(
        [
            keys.reshape(rows, KEY_VALUE_HEADS, HEAD_SIZE),
            values.reshape(rows, KEY_VALUE_HEADS, HEAD_SIZE),
        ],
        axis=2,
    )
    both = jnp.repeat(both, groups // KEY_VALUE_HEADS, axis=1)
    everything = lax.all_to_all(
        both.reshape(rows, groups * 2 * HEAD_SIZE), "ka", split_axis=1, concat_axis=0, tiled=True
    )
    first = jnp.int32(0)
    return everything.shape[0], [(everything, 0, jnp.int32(side), side, first) for side in range(2)]


ROW_TILE = 256
IN_HBM = pl.BlockSpec(memory_space=pltpu.HBM)
IN_VMEM = pl.BlockSpec(memory_space=pltpu.VMEM)
IN_SMEM = pl.BlockSpec(memory_space=pltpu.SMEM)
SMALL_COST = pl.CostEstimate(flops=1 << 20, transcendentals=0, bytes_accessed=1 << 20)


def in_hbm(values):
    return [pltpu.with_memory_space_constraint(x, pltpu.HBM) for x in values]


def in_vmem(values):
    return [pltpu.with_memory_space_constraint(x, pltpu.VMEM) for x in values]


def slab_product_kernel(kind, distances, start, has_base, out_count, where_ref, *refs):
    z, y, me = where_ref[0], where_ref[1], where_ref[2]
    own_rows, other_rows, slabs, refs = refs[:4], refs[4:8], refs[8 : 8 + len(distances)], refs[8 + len(distances) :]
    if has_base:
        base_ref, refs = refs[0], refs[1:]
    outs, (left, right, sems) = refs[:out_count], refs[out_count:]
    rows = own_rows[0].shape[0]
    depth, width = slabs[0].shape[0], right.shape[1]
    if kind == "kept":
        targets = [jnp.int32(i) for i in range(4)]
    elif kind == "near":
        targets = [(4 - z + i) % 4 for i in range(3)]
    else:
        targets = [3 - z]
    column = pl.multiple_of((y if kind == "kept" else 1 - y) * depth, depth)

    def left_copy(index, slot, side):
        source = (own_rows, other_rows)[side][slot]
        return pltpu.make_async_copy(
            source.at[:, pl.ds(column, depth)],
            left.at[pl.ds(side * rows, rows), pl.ds(index * depth, depth)],
            sems.at[index, side],
        )

    def slab_copy(index, slab):
        source = slabs[slab]
        if source.shape[1] != width:
            source = source.at[:, pl.ds(start, width)]
        return pltpu.make_async_copy(
            source, right.at[pl.ds(index * depth, depth), :], sems.at[index, 2]
        )

    for index, target in enumerate(targets):
        slot_here = jnp.bitwise_xor(me, target)
        for slot in range(4):

            @pl.when(slot_here == slot)
            def _(slot=slot):
                left_copy(index, slot, 0).start()
                left_copy(index, slot, 1).start()

        away = target - z
        for slab, distance in enumerate(distances):
            here = away == distance
            if distance == 3:
                here = here | (away == -3)

            @pl.when(here)
            def _(slab=slab):
                slab_copy(index, slab).start()

    for index in range(len(targets)):
        left_copy(index, 0, 0).wait()
        left_copy(index, 0, 1).wait()
        slab_copy(index, 0).wait()

    def rows_tile(step, carry):
        for side in range(2):
            at = pl.ds(pl.multiple_of(step * ROW_TILE + side * rows, ROW_TILE), ROW_TILE)
            product = jnp.dot(left[at, :], right[...], preferred_element_type=jnp.float32)
            if has_base:
                product = product + base_ref[at, :]
            if kind == "far":
                within = pl.ds(pl.multiple_of(step * ROW_TILE, ROW_TILE), ROW_TILE)
                outs[side][within, :] = product.astype(jnp.bfloat16)
            else:
                first = 0
                for out in outs:
                    out[at, :] = product[:, first : first + out.shape[1]]
                    first += out.shape[1]
        return carry

    lax.fori_loop(0, rows // ROW_TILE, rows_tile, 0)


def slab_product(kind, where, own_rows, other_rows, slabs, base, widths, start=0):
    rows = own_rows[0].shape[0]
    depth = slabs[0][1].shape[0]
    count = {"kept": 4, "near": 3, "far": 1}[kind]
    if kind == "far":
        out_shape = [jax.ShapeDtypeStruct((rows, widths[0]), jnp.bfloat16)] * 2
    else:
        out_shape = [jax.ShapeDtypeStruct((2 * rows, width), jnp.float32) for width in widths]
    return pl.pallas_call(
        functools.partial(
            slab_product_kernel,
            kind,
            tuple(distance for distance, _ in slabs),
            start,
            base is not None,
            len(out_shape),
        ),
        out_shape=out_shape,
        in_specs=[IN_SMEM] + [IN_HBM] * (8 + len(slabs)) + [IN_VMEM] * (base is not None),
        out_specs=[IN_VMEM] * len(out_shape),
        scratch_shapes=[
            pltpu.VMEM((2 * rows, count * depth), jnp.bfloat16),
            pltpu.VMEM((count * depth, sum(widths)), jnp.bfloat16),
            pltpu.SemaphoreType.DMA((count, 3)),
        ],
        compiler_params=pltpu.CompilerParams(vmem_limit_bytes=(4 + 3 * count) << 20),
        cost_estimate=SMALL_COST,
        name="product_" + kind,
    )(
        where,
        *in_hbm([*own_rows, *other_rows, *[slab for _, slab in slabs]]),
        *([] if base is None else in_vmem([base])),
    )


def finish_kernel(widths, where_ref, *refs):
    count = len(widths)
    out_ref, sems = refs[2 * count :]
    half = sum(widths)
    copies = []
    for side in range(2):
        start = 0
        for index, width in enumerate(widths):
            place = jnp.bitwise_xor(where_ref[1], side) * half + start
            copies.append(
                pltpu.make_async_copy(
                    refs[side * count + index],
                    out_ref.at[:, pl.ds(pl.multiple_of(place, HEAD_SIZE), width)],
                    sems.at[side, index],
                )
            )
            start += width
    for copy in copies:
        copy.start()
    for copy in copies:
        copy.wait()


def finish(where, own, received):
    widths = tuple(piece.shape[1] for piece in own)
    return pl.pallas_call(
        functools.partial(finish_kernel, widths),
        out_shape=jax.ShapeDtypeStruct((own[0].shape[0], 2 * sum(widths)), jnp.bfloat16),
        in_specs=[IN_SMEM] + [IN_VMEM] * (2 * len(widths)),
        out_specs=IN_HBM,
        scratch_shapes=[pltpu.SemaphoreType.DMA((2, len(widths)))],
        cost_estimate=SMALL_COST,
        name="finish",
    )(where, *in_vmem([*own, *received]))


UP = [[(i, i + 2) for i in range(2 * s, 6)] for s in range(2)]
DOWN = [[(i + 2, i) for i in range(6 - 2 * s)] for s in range(2)]
OUTWARD = [(2, 0), (3, 1), (4, 6), (5, 7)]
ACROSS_Y = [(i, i ^ 1) for i in range(8)]
ACROSS_X = [(i, i ^ 2) for i in range(4)]
ACROSS_CORE = [(i, i ^ 1) for i in range(4)]


def project(wo, inputs, attend_with):
    pb = lax.axis_index("pb")
    y = pb % 2
    where = jnp.stack([pb // 2, y, lax.axis_index("ka")]).astype(jnp.int32)
    depth, columns = wo.shape
    half = columns // 2
    widths = (half * 3 // 8, half * 3 // 8, half // 4)
    kept = lax.dynamic_slice(wo, (0, y * half), (depth, half))
    given = lax.dynamic_slice(wo, (0, (1 - y) * half), (depth, half))
    inputs, kept, given = lax.optimization_barrier((inputs, kept, given))

    def hop(up, down, step):
        up = up + [lax.ppermute(up[-1], "pb", UP[step])]
        down = down + [lax.ppermute(down[-1], "pb", DOWN[step])]
        return (up[1:], down[1:]) if step == 0 else (up, down)

    def other_core(piece):
        return lax.ppermute(piece, "ka", ACROSS_CORE)

    tie = lax.optimization_barrier
    first = [*hop([kept], [kept], 0), lax.ppermute(given, "pb", ACROSS_Y)]

    def gate(value):
        value, first[:] = lax.optimization_barrier((value, first))
        return value

    attn = attend_with(inputs, gate)
    kept_up, kept_down, taken = first
    kept_up, kept_down = hop(kept_up, kept_down, 1)
    taken_up, taken_down = hop([taken], [taken], 0)
    attn, kept_up[1], kept_down[1] = tie((attn, kept_up[1], kept_down[1]))
    kept_end = lax.ppermute(kept_up[1] + kept_down[1], "pb", OUTWARD)
    across_y = lax.ppermute(attn, "pb", ACROSS_Y)
    across_x = lax.ppermute(attn, "ka", ACROSS_X)
    across_y, across_x, taken_up[0], taken_down[0] = tie(
        (across_y, across_x, taken_up[0], taken_down[0])
    )
    taken_up, taken_down = hop(taken_up, taken_down, 1)
    ends = []
    start = 0
    for width in widths:
        piece = taken_up[1][:, start : start + width] + taken_down[1][:, start : start + width]
        ends.append(lax.ppermute(piece, "pb", OUTWARD))
        start += width
    corner = lax.ppermute(across_y, "ka", ACROSS_X)
    corner, kept_end = tie((corner, kept_end))
    own_rows = [attn, other_core(attn), across_x, other_core(across_x)]
    other_rows = [across_y, other_core(across_y), corner, other_core(corner)]

    def near_slabs(piece, up, down):
        return [(0, piece), (-1, up[0]), (-2, up[1]), (1, down[0]), (2, down[1])]

    (base,) = slab_product(
        "kept",
        where,
        own_rows,
        other_rows,
        near_slabs(kept, kept_up, kept_down) + [(3, kept_end)],
        None,
        (half,),
    )
    bases = slab_product(
        "near", where, own_rows, other_rows, near_slabs(taken, taken_up, taken_down), base, widths
    )
    own_out, received = [], []
    start = 0
    for base, width, end in zip(bases, widths, ends):
        own, other = slab_product(
            "far",
            where,
            own_rows,
            other_rows,
            [(3, end), (-1, taken_up[0]), (1, taken_down[0])],
            base,
            (width,),
            start,
        )
        own_out.append(own)
        received.append(lax.ppermute(other, "pb", ACROSS_Y))
        start += width
    return finish(where, own_out, received)


def shards(queries, keys, values, block_ids, counts, refresh, cached_attn, wo):
    groups = lax.axis_size("ka")

    def attend_with(inputs, gate=lambda x: x):
        queries, keys, values, old = inputs
        return attend(
            block_ids[0, 0], counts[0, 0], refresh[0, 0], queries, old, own_head_keys_values(keys, values, gate)
        )

    inputs = (queries[0], keys, values, cached_attn[0])
    if lax.axis_size("pb") == 8 and groups == 4:
        mixed = project(wo, inputs, attend_with)
    else:
        attn_full = lax.all_gather(attend_with(inputs), "ka", axis=1, tiled=True)
        mixed = jnp.dot(
            attn_full, lax.all_gather(wo, "pb", axis=0, tiled=True), preferred_element_type=jnp.float32
        ).astype(jnp.bfloat16)
    return mixed[None]


def solution(mesh):
    placed = (
        P(None, "pb", "ka"),
        P("ka", None),
        P("ka", None),
        P(None, "pb", None),
        P(None, "pb"),
        P(None, "pb"),
        P(None, "pb", "ka"),
        P("pb", "ka"),
    )
    return jax.shard_map(
        shards, mesh=mesh, in_specs=placed, out_specs=P(None, "pb", "ka"), check_vma=False
    )
```

```python
import functools
import math

import jax
import jax.numpy as jnp
from jax import lax
from jax.experimental import pallas as pl
from jax.experimental.pallas import tpu as pltpu
from jax.sharding import PartitionSpec as P

HEAD_SIZE = 128
QUERY_HEAD_COUNT = 32
KEY_VALUE_HEADS = 4
QUERY_BLOCK_SIZE = 512
KEY_BLOCK_TOKENS = 128
RATIO = QUERY_HEAD_COUNT // KEY_VALUE_HEADS
LOWEST = -1e30
EXP2_SCALE = math.log2(math.e) / math.sqrt(HEAD_SIZE)


GROUP = 4


def attention_kernel(
    heads, slots, part_rows, first_rows, targets, meta_ref, q_hbm, old_hbm, *refs
):
    kv_parts, (out_ref, q_ref, kv_ref, peak_ref, denom_ref, acc_ref, sems) = refs[:-7], refs[-7:]
    live = meta_ref[0]
    flag = meta_ref[1]

    @pl.when(flag <= 0)
    def _():
        copy = pltpu.make_async_copy(old_hbm, out_ref, sems.at[0])
        copy.start()
        copy.wait()

    @pl.when(flag > 0)
    def _():
        copies = [pltpu.make_async_copy(q_hbm, q_ref, sems.at[0])]
        for index, (part, first_row, target) in enumerate(zip(kv_parts, first_rows, targets)):
            column = pl.multiple_of(meta_ref[2 + slots + 2 * index] * HEAD_SIZE, HEAD_SIZE)
            start = pl.multiple_of(meta_ref[3 + slots + 2 * index] * part_rows, part_rows)
            copies.append(
                pltpu.make_async_copy(
                    part.at[pl.ds(first_row, part_rows), pl.ds(column, HEAD_SIZE)],
                    kv_ref.at[pl.ds(start, part_rows), pl.ds(target * HEAD_SIZE, HEAD_SIZE)],
                    sems.at[1 + index],
                )
            )
        for copy in copies:
            copy.start()
        peak_ref[...] = jnp.full_like(peak_ref, LOWEST)
        denom_ref[...] = jnp.zeros_like(denom_ref)
        acc_ref[...] = jnp.zeros_like(acc_ref)
        for copy in copies:
            copy.wait()

        def group(step, carry):
            tiles, biases = [], []
            for member in range(GROUP):
                slot = step * GROUP + member
                if member > 0:
                    present = slot < live
                    block = jnp.where(
                        present, meta_ref[2 + jnp.minimum(slot, slots - 1)], 0
                    )
                    biases.append(jnp.where(present, 0.0, LOWEST).astype(jnp.float32))
                else:
                    block = meta_ref[2 + slot]
                    biases.append(None)
                row = pl.multiple_of(block * KEY_BLOCK_TOKENS, KEY_BLOCK_TOKENS)
                tiles.append(kv_ref[pl.ds(row, KEY_BLOCK_TOKENS), :])
            tile = jnp.concatenate(tiles, axis=0)
            key_tile = tile[:, :HEAD_SIZE]
            value_tile = tile[:, HEAD_SIZE:].T
            value_tile = jnp.concatenate(
                [value_tile, jnp.ones((16, value_tile.shape[1]), jnp.bfloat16)], axis=0
            )
            for head in range(heads):
                query = q_ref[:, head * HEAD_SIZE : (head + 1) * HEAD_SIZE]
                scores = lax.dot_general(
                    key_tile, query, (((1,), (1,)), ((), ())), preferred_element_type=jnp.float32
                )
                parts = [
                    scores[member * KEY_BLOCK_TOKENS : (member + 1) * KEY_BLOCK_TOKENS]
                    for member in range(GROUP)
                ]
                parts = [p if b is None else p + b for p, b in zip(parts, biases)]
                top = functools.reduce(jnp.maximum, parts)
                old_peak = peak_ref[head]
                peak = jnp.maximum(old_peak, jnp.max(top, axis=0, keepdims=True))
                decay = jnp.exp2((old_peak - peak) * EXP2_SCALE)
                parts = [jnp.exp2((p - peak) * EXP2_SCALE) for p in parts]
                peak_ref[head] = peak
                weights = jnp.concatenate([p.astype(jnp.bfloat16) for p in parts], axis=0)
                update = lax.dot_general(
                    value_tile, weights, (((1,), (0,)), ((), ())), preferred_element_type=jnp.float32
                )
                denom_ref[head] = denom_ref[head] * decay + update[HEAD_SIZE : HEAD_SIZE + 1]
                acc_ref[head] = acc_ref[head] * decay + update[:HEAD_SIZE]
            return carry

        lax.fori_loop(0, (live + GROUP - 1) // GROUP, group, 0)
        for head in range(heads):
            result = acc_ref[head] / denom_ref[head]
            out_ref[:, head * HEAD_SIZE : (head + 1) * HEAD_SIZE] = result.T.astype(jnp.bfloat16)


def attend(block_list, live, flag, queries, old, key_values):
    part_rows, sources = key_values
    arrays, first_rows, heads_at, targets, places = zip(*sources)
    rows, width = queries.shape
    heads = width // HEAD_SIZE
    slots = block_list.shape[0]
    spots = [value[None] for pair in zip(heads_at, places) for value in pair]
    meta = jnp.concatenate([live[None], flag[None], block_list, *spots])
    in_hbm = pl.BlockSpec(memory_space=pltpu.HBM)
    return pl.pallas_call(
        functools.partial(attention_kernel, heads, slots, part_rows, first_rows, targets),
        out_shape=jax.ShapeDtypeStruct((rows, width), jnp.bfloat16),
        in_specs=[pl.BlockSpec(memory_space=pltpu.SMEM)] + [in_hbm] * (2 + len(arrays)),
        out_specs=pl.BlockSpec(memory_space=pltpu.VMEM),
        scratch_shapes=[
            pltpu.VMEM((rows, width), jnp.bfloat16),
            pltpu.VMEM((part_rows * len(arrays) // 2, 2 * HEAD_SIZE), jnp.bfloat16),
            pltpu.VMEM((heads, 1, rows), jnp.float32),
            pltpu.VMEM((heads, 1, rows), jnp.float32),
            pltpu.VMEM((heads, HEAD_SIZE, rows), jnp.float32),
            pltpu.SemaphoreType.DMA((1 + len(arrays),)),
        ],
        compiler_params=pltpu.CompilerParams(vmem_limit_bytes=24 << 20),
        cost_estimate=pl.CostEstimate(
            flops=1 << 20, transcendentals=0, bytes_accessed=1 << 20
        ),
        name="attend",
    )(
        meta,
        *[
            pltpu.with_memory_space_constraint(x, pltpu.HBM)
            for x in (queries, old, *arrays)
        ],
    )


def own_head_keys_values(keys, values, gate=lambda x: x):
    groups = lax.axis_size("ka")
    me = lax.axis_index("ka")
    rows = keys.shape[0]
    if groups == KEY_VALUE_HEADS == 4:
        x, core = me // 2, me % 2
        pair = 2 * HEAD_SIZE

        def heads_of(array, chip):
            return lax.dynamic_slice(array, (0, chip * pair), (rows, pair))

        def head_of(array, head):
            return lax.dynamic_slice(array, (0, head * HEAD_SIZE), (rows, HEAD_SIZE))

        across = [
            lax.ppermute(heads_of(a, 1 - x), "ka", [(i, i ^ 2) for i in range(4)])
            for a in (keys, values)
        ]
        across = gate(across)
        beside = lax.ppermute(
            jnp.concatenate(
                [
                    jnp.concatenate([head_of(a, 2 * x + 1 - core) for a in (keys, values)], axis=1),
                    jnp.concatenate([head_of(a, 1 - core) for a in across], axis=1),
                ],
                axis=0,
            ),
            "ka",
            [(i, i ^ 1) for i in range(4)],
        )
        near, far = jnp.bitwise_xor(me, 1), jnp.bitwise_xor(me, 3)
        sources = [
            (keys, 0, me, 0, me),
            (values, 0, me, 1, me),
            (across[0], 0, core, 0, jnp.bitwise_xor(me, 2)),
            (across[1], 0, core, 1, jnp.bitwise_xor(me, 2)),
        ]
        for side in range(2):
            for row, place in ((0, near), (rows, far)):
                sources.append((beside, row, jnp.int32(side), side, place))
        return rows, sources
    both = jnp.concatenate(
        [
            keys.reshape(rows, KEY_VALUE_HEADS, HEAD_SIZE),
            values.reshape(rows, KEY_VALUE_HEADS, HEAD_SIZE),
        ],
        axis=2,
    )
    both = jnp.repeat(both, groups // KEY_VALUE_HEADS, axis=1)
    everything = lax.all_to_all(
        both.reshape(rows, groups * 2 * HEAD_SIZE), "ka", split_axis=1, concat_axis=0, tiled=True
    )
    first = jnp.int32(0)
    return everything.shape[0], [(everything, 0, jnp.int32(side), side, first) for side in range(2)]


def ring_of(pb_size):
    if pb_size == 8:
        return [0, 2, 4, 6, 7, 5, 3, 1]
    return list(range(pb_size))


ROW_TILE = 128
IN_HBM = pl.BlockSpec(memory_space=pltpu.HBM)
IN_VMEM = pl.BlockSpec(memory_space=pltpu.VMEM)
IN_SMEM = pl.BlockSpec(memory_space=pltpu.SMEM)
SMALL_COST = pl.CostEstimate(flops=1 << 20, transcendentals=0, bytes_accessed=1 << 20)


def pinned(values, space):
    return [pltpu.with_memory_space_constraint(x, space) for x in values]


def ring_product_kernel(steps, spare_step, where_ref, *refs):
    count = len(steps)
    blocks, slabs, refs = refs[:4], (refs[4 : 4 + count], refs[4 + count : 4 + 2 * count]), refs[4 + 2 * count :]
    if spare_step is not None:
        base_ref, out_ref, spare_ref = refs[:3]
        refs = refs[3:]
    else:
        out_ref, refs = refs[0], refs[1:]
    left, right, block_sems, slab_sems = refs
    rows, depth = left.shape[0], right.shape[1] // count
    per = blocks[0].shape[1] // depth
    me = where_ref[where_ref.shape[0] - 1]

    def block_copy(index, slot, shift):
        target = spare_ref if index == count else left.at[:, pl.ds(index * depth, depth)]
        return pltpu.make_async_copy(
            blocks[slot].at[:, pl.ds(shift, depth)], target, block_sems.at[index]
        )

    def slab_copy(half, index):
        return pltpu.make_async_copy(
            slabs[half][index],
            right.at[half, pl.ds(index * depth, depth), :],
            slab_sems.at[half, index],
        )

    all_steps = steps if spare_step is None else (*steps, spare_step)
    for index, step in enumerate(all_steps):
        source = where_ref[step]
        slot_here = jnp.bitwise_xor(source // per, me)
        shift = pl.multiple_of((source % per) * depth, depth)
        for slot in range(4):

            @pl.when(slot_here == slot)
            def _(slot=slot):
                block_copy(index, slot, shift).start()

    for half in range(2):
        for index in range(count):
            slab_copy(half, index).start()
    for index in range(len(all_steps)):
        block_copy(index, 0, 0).wait()
    half_columns = right.shape[2]
    for half in range(2):
        columns = pl.ds(half * half_columns, half_columns)
        for index in range(count):
            slab_copy(half, index).wait()

        def rows_tile(step, carry):
            at = pl.ds(pl.multiple_of(step * ROW_TILE, ROW_TILE), ROW_TILE)
            product = jnp.dot(left[at, :], right[half], preferred_element_type=jnp.float32)
            if spare_step is not None:
                product = product + base_ref[at, columns]
            out_ref[at, columns] = product
            return carry

        lax.fori_loop(0, rows // ROW_TILE, rows_tile, 0)


def ring_product(where, blocks, steps, slabs, base=None, spare_step=None):
    count = len(steps)
    rows = blocks[0].shape[0]
    depth, half = slabs[0][0].shape
    spare = spare_step is not None
    out_shape = [jax.ShapeDtypeStruct((rows, 2 * half), jnp.float32)]
    if spare:
        out_shape.append(jax.ShapeDtypeStruct((rows, depth), jnp.bfloat16))
    return pl.pallas_call(
        functools.partial(ring_product_kernel, steps, spare_step),
        out_shape=out_shape,
        in_specs=[IN_SMEM] + [IN_HBM] * (4 + 2 * count) + [IN_VMEM] * spare,
        out_specs=[IN_VMEM] * len(out_shape),
        scratch_shapes=[
            pltpu.VMEM((rows, count * depth), jnp.bfloat16),
            pltpu.VMEM((2, count * depth, half), jnp.bfloat16),
            pltpu.SemaphoreType.DMA((count + spare,)),
            pltpu.SemaphoreType.DMA((2, count)),
        ],
        compiler_params=pltpu.CompilerParams(vmem_limit_bytes=(6 + 4 * count) << 20),
        cost_estimate=SMALL_COST,
        name="ring_product",
    )(
        where,
        *pinned([*blocks, *slabs[0], *slabs[1]], pltpu.HBM),
        *(pinned([base], pltpu.VMEM) if spare else []),
    )


def last_product_kernel(start, block_ref, slab_ref, base_ref, *refs):
    out_ref, staged, sems = refs[-3:]
    columns = pl.ds(start, slab_ref.shape[1])

    def tile_copy(tile):
        at = pl.ds(tile * ROW_TILE, ROW_TILE)
        return pltpu.make_async_copy(staged.at[at, :], out_ref.at[at, columns], sems.at[tile])

    tiles = block_ref.shape[0] // ROW_TILE
    for tile in range(tiles):
        at = pl.ds(tile * ROW_TILE, ROW_TILE)
        product = jnp.dot(block_ref[at, :], slab_ref[...], preferred_element_type=jnp.float32)
        staged[at, :] = (product + base_ref[at, columns]).astype(jnp.bfloat16)
        tile_copy(tile).start()
    for tile in range(tiles):
        tile_copy(tile).wait()


def last_product(block, slab, base, start, partly=None):
    rows, columns = base.shape
    operands = pinned([block, slab, base], pltpu.VMEM)
    if partly is not None:
        operands.append(partly)
    return pl.pallas_call(
        functools.partial(last_product_kernel, start),
        out_shape=jax.ShapeDtypeStruct((rows, columns), jnp.bfloat16),
        in_specs=[IN_VMEM] * 3 + [IN_HBM] * (partly is not None),
        out_specs=IN_HBM,
        scratch_shapes=[
            pltpu.VMEM((rows, slab.shape[1]), jnp.bfloat16),
            pltpu.SemaphoreType.DMA((rows // ROW_TILE,)),
        ],
        input_output_aliases={} if partly is None else {3: 0},
        compiler_params=pltpu.CompilerParams(vmem_limit_bytes=8 << 20),
        cost_estimate=SMALL_COST,
        name="last_product",
    )(*operands)


def project_ring(wo, inputs, attend_with):
    pb_size = lax.axis_size("pb")
    depth, columns = wo.shape
    ring = ring_of(pb_size)
    forward = [(ring[i], ring[(i + 1) % pb_size]) for i in range(pb_size)]
    backward = [(b, a) for a, b in forward]
    half = columns // 2
    far = pb_size // 2
    parts = [wo[:, :half]]
    wo, parts[0] = lax.optimization_barrier((wo, parts[0]))
    parts.append(wo[:, half:])
    inputs, parts[1] = lax.optimization_barrier((inputs, parts[1]))
    slabs = [[(0, part)] for part in parts]
    moving = [[part, part] for part in parts]

    def travel(hop):
        for part in range(2):
            if hop < far or part == 0:
                moving[part][0] = lax.ppermute(moving[part][0], "pb", forward)
            if hop < far or part == 1:
                moving[part][1] = lax.ppermute(moving[part][1], "pb", backward)

    def keep(hop):
        for part in range(2):
            if hop < far or part == 0:
                slabs[part].append((-hop, moving[part][0]))
            if hop < far or part == 1:
                slabs[part].append((hop, moving[part][1]))

    def gate(value):
        value, moving[0][0], moving[0][1] = lax.optimization_barrier(
            (value, moving[0][0], moving[0][1])
        )
        return value

    travel(1)
    attn = attend_with(inputs, gate)
    keep(1)
    for hop in range(2, far + 1):
        travel(hop)
        keep(hop)
    across = lax.ppermute(attn, "ka", [(i, i ^ 2) for i in range(4)])
    beside = lax.ppermute(attn, "ka", [(i, i ^ 1) for i in range(4)])
    corner = lax.ppermute(attn, "ka", [(i, i ^ 3) for i in range(4)])
    around = jnp.asarray(
        [[ring[(ring.index(p) + step) % pb_size] for step in range(pb_size)] for p in range(pb_size)],
        jnp.int32,
    )
    mine = lax.dynamic_slice(around, (lax.axis_index("pb"), 0), (1, pb_size))[0]
    where = jnp.concatenate([mine, lax.axis_index("ka")[None].astype(jnp.int32)])
    blocks = [attn, beside, across, corner]
    at_step = [{offset % pb_size: slab for offset, slab in slabs[part]} for part in range(2)]

    def chosen(offsets):
        return [[at_step[part][offset % pb_size] for offset in offsets] for part in range(2)]

    def steps(offsets):
        return tuple(offset % pb_size for offset in offsets)

    early, late = (0, -1, 1, -2, 2), (-3, 3)
    (base,) = ring_product(where, blocks, steps(early), chosen(early))
    base, block = ring_product(where, blocks, steps(late), chosen(late), base, far)
    left = last_product(block, at_step[0][far], base, 0)
    return last_product(block, at_step[1][far], base, half, left)


def shards(queries, keys, values, block_ids, counts, refresh, cached_attn, wo):
    groups = lax.axis_size("ka")

    def attend_with(inputs, gate=lambda x: x):
        queries, keys, values, old = inputs
        return attend(
            block_ids[0, 0], counts[0, 0], refresh[0, 0], queries, old, own_head_keys_values(keys, values, gate)
        )

    inputs = (queries[0], keys, values, cached_attn[0])
    if lax.axis_size("pb") == 8 and groups == 4:
        mixed = project_ring(wo, inputs, attend_with)
    else:
        attn_full = lax.all_gather(attend_with(inputs), "ka", axis=1, tiled=True)
        mixed = jnp.dot(
            attn_full, lax.all_gather(wo, "pb", axis=0, tiled=True), preferred_element_type=jnp.float32
        ).astype(jnp.bfloat16)
    return mixed[None]


def solution(mesh):
    placed = (
        P(None, "pb", "ka"),
        P("ka", None),
        P("ka", None),
        P(None, "pb", None),
        P(None, "pb"),
        P(None, "pb"),
        P(None, "pb", "ka"),
        P("pb", "ka"),
    )
    return jax.shard_map(
        shards, mesh=mesh, in_specs=placed, out_specs=P(None, "pb", "ka"), check_vma=False
    )
```

```python
import functools
import math

import jax
import jax.numpy as jnp
from jax import lax
from jax.experimental import pallas as pl
from jax.experimental.pallas import tpu as pltpu
from jax.sharding import PartitionSpec as P

HEAD_SIZE = 128
QUERY_HEAD_COUNT = 32
KEY_VALUE_HEADS = 4
QUERY_BLOCK_SIZE = 512
KEY_BLOCK_TOKENS = 128
RATIO = QUERY_HEAD_COUNT // KEY_VALUE_HEADS
LOWEST = -1e30
EXP2_SCALE = math.log2(math.e) / math.sqrt(HEAD_SIZE)


GROUP = 4


def attention_kernel(
    heads, slots, part_rows, first_rows, targets, meta_ref, q_hbm, old_hbm, *refs
):
    kv_parts, (out_ref, q_ref, kv_ref, peak_ref, denom_ref, acc_ref, sems) = refs[:-7], refs[-7:]
    live = meta_ref[0]
    flag = meta_ref[1]

    @pl.when(flag <= 0)
    def _():
        copy = pltpu.make_async_copy(old_hbm, out_ref, sems.at[0])
        copy.start()
        copy.wait()

    @pl.when(flag > 0)
    def _():
        copies = [pltpu.make_async_copy(q_hbm, q_ref, sems.at[0])]
        for index, (part, first_row, target) in enumerate(zip(kv_parts, first_rows, targets)):
            column = pl.multiple_of(meta_ref[2 + slots + 2 * index] * HEAD_SIZE, HEAD_SIZE)
            start = pl.multiple_of(meta_ref[3 + slots + 2 * index] * part_rows, part_rows)
            copies.append(
                pltpu.make_async_copy(
                    part.at[pl.ds(first_row, part_rows), pl.ds(column, HEAD_SIZE)],
                    kv_ref.at[pl.ds(start, part_rows), pl.ds(target * HEAD_SIZE, HEAD_SIZE)],
                    sems.at[1 + index],
                )
            )
        for copy in copies:
            copy.start()
        peak_ref[...] = jnp.full_like(peak_ref, LOWEST)
        denom_ref[...] = jnp.zeros_like(denom_ref)
        acc_ref[...] = jnp.zeros_like(acc_ref)
        for copy in copies:
            copy.wait()

        def group(step, carry):
            tiles, biases = [], []
            for member in range(GROUP):
                slot = step * GROUP + member
                if member > 0:
                    present = slot < live
                    block = jnp.where(
                        present, meta_ref[2 + jnp.minimum(slot, slots - 1)], 0
                    )
                    biases.append(jnp.where(present, 0.0, LOWEST).astype(jnp.float32))
                else:
                    block = meta_ref[2 + slot]
                    biases.append(None)
                row = pl.multiple_of(block * KEY_BLOCK_TOKENS, KEY_BLOCK_TOKENS)
                tiles.append(kv_ref[pl.ds(row, KEY_BLOCK_TOKENS), :])
            tile = jnp.concatenate(tiles, axis=0)
            key_tile = tile[:, :HEAD_SIZE]
            value_tile = tile[:, HEAD_SIZE:].T
            value_tile = jnp.concatenate(
                [value_tile, jnp.ones((16, value_tile.shape[1]), jnp.bfloat16)], axis=0
            )
            for head in range(heads):
                query = q_ref[:, head * HEAD_SIZE : (head + 1) * HEAD_SIZE]
                scores = lax.dot_general(
                    key_tile, query, (((1,), (1,)), ((), ())), preferred_element_type=jnp.float32
                )
                parts = [
                    scores[member * KEY_BLOCK_TOKENS : (member + 1) * KEY_BLOCK_TOKENS]
                    for member in range(GROUP)
                ]
                parts = [p if b is None else p + b for p, b in zip(parts, biases)]
                top = functools.reduce(jnp.maximum, parts)
                old_peak = peak_ref[head]
                peak = jnp.maximum(old_peak, jnp.max(top, axis=0, keepdims=True))
                decay = jnp.exp2((old_peak - peak) * EXP2_SCALE)
                parts = [jnp.exp2((p - peak) * EXP2_SCALE) for p in parts]
                peak_ref[head] = peak
                weights = jnp.concatenate([p.astype(jnp.bfloat16) for p in parts], axis=0)
                update = lax.dot_general(
                    value_tile, weights, (((1,), (0,)), ((), ())), preferred_element_type=jnp.float32
                )
                denom_ref[head] = denom_ref[head] * decay + update[HEAD_SIZE : HEAD_SIZE + 1]
                acc_ref[head] = acc_ref[head] * decay + update[:HEAD_SIZE]
            return carry

        lax.fori_loop(0, (live + GROUP - 1) // GROUP, group, 0)
        for head in range(heads):
            result = acc_ref[head] / denom_ref[head]
            out_ref[:, head * HEAD_SIZE : (head + 1) * HEAD_SIZE] = result.T.astype(jnp.bfloat16)


def attend(block_list, live, flag, queries, old, key_values):
    part_rows, sources = key_values
    arrays, first_rows, heads_at, targets, places = zip(*sources)
    rows, width = queries.shape
    heads = width // HEAD_SIZE
    slots = block_list.shape[0]
    spots = [value[None] for pair in zip(heads_at, places) for value in pair]
    meta = jnp.concatenate([live[None], flag[None], block_list, *spots])
    in_hbm = pl.BlockSpec(memory_space=pltpu.HBM)
    return pl.pallas_call(
        functools.partial(attention_kernel, heads, slots, part_rows, first_rows, targets),
        out_shape=jax.ShapeDtypeStruct((rows, width), jnp.bfloat16),
        in_specs=[pl.BlockSpec(memory_space=pltpu.SMEM)] + [in_hbm] * (2 + len(arrays)),
        out_specs=pl.BlockSpec(memory_space=pltpu.VMEM),
        scratch_shapes=[
            pltpu.VMEM((rows, width), jnp.bfloat16),
            pltpu.VMEM((part_rows * len(arrays) // 2, 2 * HEAD_SIZE), jnp.bfloat16),
            pltpu.VMEM((heads, 1, rows), jnp.float32),
            pltpu.VMEM((heads, 1, rows), jnp.float32),
            pltpu.VMEM((heads, HEAD_SIZE, rows), jnp.float32),
            pltpu.SemaphoreType.DMA((1 + len(arrays),)),
        ],
        compiler_params=pltpu.CompilerParams(vmem_limit_bytes=24 << 20),
        cost_estimate=pl.CostEstimate(
            flops=1 << 20, transcendentals=0, bytes_accessed=1 << 20
        ),
        name="attend",
    )(
        meta,
        *[
            pltpu.with_memory_space_constraint(x, pltpu.HBM)
            for x in (queries, old, *arrays)
        ],
    )


def own_head_keys_values(keys, values, gate=lambda x: x):
    groups = lax.axis_size("ka")
    me = lax.axis_index("ka")
    rows = keys.shape[0]
    if groups == KEY_VALUE_HEADS == 4:
        x, core = me // 2, me % 2
        pair = 2 * HEAD_SIZE

        def heads_of(array, chip):
            return lax.dynamic_slice(array, (0, chip * pair), (rows, pair))

        def head_of(array, head):
            return lax.dynamic_slice(array, (0, head * HEAD_SIZE), (rows, HEAD_SIZE))

        across = [
            lax.ppermute(heads_of(a, 1 - x), "ka", [(i, i ^ 2) for i in range(4)])
            for a in (keys, values)
        ]
        across = gate(across)
        beside = lax.ppermute(
            jnp.concatenate(
                [
                    jnp.concatenate([head_of(a, 2 * x + 1 - core) for a in (keys, values)], axis=1),
                    jnp.concatenate([head_of(a, 1 - core) for a in across], axis=1),
                ],
                axis=0,
            ),
            "ka",
            [(i, i ^ 1) for i in range(4)],
        )
        near, far = jnp.bitwise_xor(me, 1), jnp.bitwise_xor(me, 3)
        sources = [
            (keys, 0, me, 0, me),
            (values, 0, me, 1, me),
            (across[0], 0, core, 0, jnp.bitwise_xor(me, 2)),
            (across[1], 0, core, 1, jnp.bitwise_xor(me, 2)),
        ]
        for side in range(2):
            for row, place in ((0, near), (rows, far)):
                sources.append((beside, row, jnp.int32(side), side, place))
        return rows, sources
    both = jnp.concatenate(
        [
            keys.reshape(rows, KEY_VALUE_HEADS, HEAD_SIZE),
            values.reshape(rows, KEY_VALUE_HEADS, HEAD_SIZE),
        ],
        axis=2,
    )
    both = jnp.repeat(both, groups // KEY_VALUE_HEADS, axis=1)
    everything = lax.all_to_all(
        both.reshape(rows, groups * 2 * HEAD_SIZE), "ka", split_axis=1, concat_axis=0, tiled=True
    )
    first = jnp.int32(0)
    return everything.shape[0], [(everything, 0, jnp.int32(side), side, first) for side in range(2)]


def ring_of(pb_size):
    if pb_size == 8:
        return [0, 2, 4, 6, 7, 5, 3, 1]
    return list(range(pb_size))


ROW_TILE = 128
IN_HBM = pl.BlockSpec(memory_space=pltpu.HBM)
IN_VMEM = pl.BlockSpec(memory_space=pltpu.VMEM)
IN_SMEM = pl.BlockSpec(memory_space=pltpu.SMEM)
SMALL_COST = pl.CostEstimate(flops=1 << 20, transcendentals=0, bytes_accessed=1 << 20)


def pinned(values, space):
    return [pltpu.with_memory_space_constraint(x, space) for x in values]


def ring_product_kernel(steps, spare_step, where_ref, *refs):
    count = len(steps)
    blocks, slabs, refs = refs[:4], (refs[4 : 4 + count], refs[4 + count : 4 + 2 * count]), refs[4 + 2 * count :]
    if spare_step is not None:
        base_ref, out_ref, spare_ref = refs[:3]
        refs = refs[3:]
    else:
        out_ref, refs = refs[0], refs[1:]
    left, right, block_sems, slab_sems = refs
    rows, depth = left.shape[0], right.shape[1] // count
    per = blocks[0].shape[1] // depth
    me = where_ref[where_ref.shape[0] - 1]

    def block_copy(index, slot, shift):
        target = spare_ref if index == count else left.at[:, pl.ds(index * depth, depth)]
        return pltpu.make_async_copy(
            blocks[slot].at[:, pl.ds(shift, depth)], target, block_sems.at[index]
        )

    def slab_copy(half, index):
        return pltpu.make_async_copy(
            slabs[half][index],
            right.at[half, pl.ds(index * depth, depth), :],
            slab_sems.at[half, index],
        )

    all_steps = steps if spare_step is None else (*steps, spare_step)
    for index, step in enumerate(all_steps):
        source = where_ref[step]
        slot_here = jnp.bitwise_xor(source // per, me)
        shift = pl.multiple_of((source % per) * depth, depth)
        for slot in range(4):

            @pl.when(slot_here == slot)
            def _(slot=slot):
                block_copy(index, slot, shift).start()

    for half in range(2):
        for index in range(count):
            slab_copy(half, index).start()
    for index in range(len(all_steps)):
        block_copy(index, 0, 0).wait()
    half_columns = right.shape[2]
    for half in range(2):
        columns = pl.ds(half * half_columns, half_columns)
        for index in range(count):
            slab_copy(half, index).wait()

        def rows_tile(step, carry):
            at = pl.ds(pl.multiple_of(step * ROW_TILE, ROW_TILE), ROW_TILE)
            product = jnp.dot(left[at, :], right[half], preferred_element_type=jnp.float32)
            if spare_step is not None:
                product = product + base_ref[at, columns]
            out_ref[at, columns] = product
            return carry

        lax.fori_loop(0, rows // ROW_TILE, rows_tile, 0)


def ring_product(where, blocks, steps, slabs, base=None, spare_step=None):
    count = len(steps)
    rows = blocks[0].shape[0]
    depth, half = slabs[0][0].shape
    spare = spare_step is not None
    out_shape = [jax.ShapeDtypeStruct((rows, 2 * half), jnp.float32)]
    if spare:
        out_shape.append(jax.ShapeDtypeStruct((rows, depth), jnp.bfloat16))
    return pl.pallas_call(
        functools.partial(ring_product_kernel, steps, spare_step),
        out_shape=out_shape,
        in_specs=[IN_SMEM] + [IN_HBM] * (4 + 2 * count) + [IN_VMEM] * spare,
        out_specs=[IN_VMEM] * len(out_shape),
        scratch_shapes=[
            pltpu.VMEM((rows, count * depth), jnp.bfloat16),
            pltpu.VMEM((2, count * depth, half), jnp.bfloat16),
            pltpu.SemaphoreType.DMA((count + spare,)),
            pltpu.SemaphoreType.DMA((2, count)),
        ],
        compiler_params=pltpu.CompilerParams(vmem_limit_bytes=(6 + 4 * count) << 20),
        cost_estimate=SMALL_COST,
        name="ring_product",
    )(
        where,
        *pinned([*blocks, *slabs[0], *slabs[1]], pltpu.HBM),
        *(pinned([base], pltpu.VMEM) if spare else []),
    )


def last_product_kernel(start, block_ref, slab_ref, base_ref, *refs):
    out_ref, staged, sems = refs[-3:]
    columns = pl.ds(start, slab_ref.shape[1])

    def tile_copy(tile):
        at = pl.ds(tile * ROW_TILE, ROW_TILE)
        return pltpu.make_async_copy(staged.at[at, :], out_ref.at[at, columns], sems.at[tile])

    tiles = block_ref.shape[0] // ROW_TILE
    for tile in range(tiles):
        at = pl.ds(tile * ROW_TILE, ROW_TILE)
        product = jnp.dot(block_ref[at, :], slab_ref[...], preferred_element_type=jnp.float32)
        staged[at, :] = (product + base_ref[at, columns]).astype(jnp.bfloat16)
        tile_copy(tile).start()
    for tile in range(tiles):
        tile_copy(tile).wait()


def last_product(block, slab, base, start, partly=None):
    rows, columns = base.shape
    operands = pinned([block, slab, base], pltpu.VMEM)
    if partly is not None:
        operands.append(partly)
    return pl.pallas_call(
        functools.partial(last_product_kernel, start),
        out_shape=jax.ShapeDtypeStruct((rows, columns), jnp.bfloat16),
        in_specs=[IN_VMEM] * 3 + [IN_HBM] * (partly is not None),
        out_specs=IN_HBM,
        scratch_shapes=[
            pltpu.VMEM((rows, slab.shape[1]), jnp.bfloat16),
            pltpu.SemaphoreType.DMA((rows // ROW_TILE,)),
        ],
        input_output_aliases={} if partly is None else {3: 0},
        compiler_params=pltpu.CompilerParams(vmem_limit_bytes=8 << 20),
        cost_estimate=SMALL_COST,
        name="last_product",
    )(*operands)


def project_ring(wo, inputs, attend_with):
    pb_size = lax.axis_size("pb")
    depth, columns = wo.shape
    ring = ring_of(pb_size)
    forward = [(ring[i], ring[(i + 1) % pb_size]) for i in range(pb_size)]
    backward = [(b, a) for a, b in forward]
    half = columns // 2
    far = pb_size // 2
    parts = [wo[:, :half]]
    wo, parts[0] = lax.optimization_barrier((wo, parts[0]))
    parts.append(wo[:, half:])
    inputs, parts[1] = lax.optimization_barrier((inputs, parts[1]))
    slabs = [[(0, part)] for part in parts]
    moving = [[part, part] for part in parts]

    def travel(hop):
        for part in range(2):
            if hop < far or part == 0:
                moving[part][0] = lax.ppermute(moving[part][0], "pb", forward)
            if hop < far or part == 1:
                moving[part][1] = lax.ppermute(moving[part][1], "pb", backward)

    def keep(hop):
        for part in range(2):
            if hop < far or part == 0:
                slabs[part].append((-hop, moving[part][0]))
            if hop < far or part == 1:
                slabs[part].append((hop, moving[part][1]))

    def gate(value):
        value, moving[0][0], moving[1][1] = lax.optimization_barrier(
            (value, moving[0][0], moving[1][1])
        )
        return value

    travel(1)
    attn = attend_with(inputs, gate)
    keep(1)
    for hop in range(2, far + 1):
        travel(hop)
        keep(hop)
    across = lax.ppermute(attn, "ka", [(i, i ^ 2) for i in range(4)])
    beside = lax.ppermute(attn, "ka", [(i, i ^ 1) for i in range(4)])
    corner = lax.ppermute(attn, "ka", [(i, i ^ 3) for i in range(4)])
    around = jnp.asarray(
        [[ring[(ring.index(p) + step) % pb_size] for step in range(pb_size)] for p in range(pb_size)],
        jnp.int32,
    )
    mine = lax.dynamic_slice(around, (lax.axis_index("pb"), 0), (1, pb_size))[0]
    where = jnp.concatenate([mine, lax.axis_index("ka")[None].astype(jnp.int32)])
    blocks = [attn, beside, across, corner]
    at_step = [{offset % pb_size: slab for offset, slab in slabs[part]} for part in range(2)]

    def chosen(offsets):
        return [[at_step[part][offset % pb_size] for offset in offsets] for part in range(2)]

    def steps(offsets):
        return tuple(offset % pb_size for offset in offsets)

    early, late = (0, -1, 1, -2, 2), (-3, 3)
    (base,) = ring_product(where, blocks, steps(early), chosen(early))
    base, block = ring_product(where, blocks, steps(late), chosen(late), base, far)
    left = last_product(block, at_step[0][far], base, 0)
    return last_product(block, at_step[1][far], base, half, left)


def shards(queries, keys, values, block_ids, counts, refresh, cached_attn, wo):
    groups = lax.axis_size("ka")

    def attend_with(inputs, gate=lambda x: x):
        queries, keys, values, old = inputs
        return attend(
            block_ids[0, 0], counts[0, 0], refresh[0, 0], queries, old, own_head_keys_values(keys, values, gate)
        )

    inputs = (queries[0], keys, values, cached_attn[0])
    if lax.axis_size("pb") == 8 and groups == 4:
        mixed = project_ring(wo, inputs, attend_with)
    else:
        attn_full = lax.all_gather(attend_with(inputs), "ka", axis=1, tiled=True)
        mixed = jnp.dot(
            attn_full, lax.all_gather(wo, "pb", axis=0, tiled=True), preferred_element_type=jnp.float32
        ).astype(jnp.bfloat16)
    return mixed[None]


def solution(mesh):
    placed = (
        P(None, "pb", "ka"),
        P("ka", None),
        P("ka", None),
        P(None, "pb", None),
        P(None, "pb"),
        P(None, "pb"),
        P(None, "pb", "ka"),
        P("pb", "ka"),
    )
    return jax.shard_map(
        shards, mesh=mesh, in_specs=placed, out_specs=P(None, "pb", "ka"), check_vma=False
    )
```

```python
import functools
import math

import jax
import jax.numpy as jnp
from jax import lax
from jax.experimental import pallas as pl
from jax.experimental.pallas import tpu as pltpu
from jax.sharding import PartitionSpec as P

HEAD_SIZE = 128
QUERY_HEAD_COUNT = 32
KEY_VALUE_HEADS = 4
QUERY_BLOCK_SIZE = 512
KEY_BLOCK_TOKENS = 128
RATIO = QUERY_HEAD_COUNT // KEY_VALUE_HEADS
LOWEST = -1e30
EXP2_SCALE = math.log2(math.e) / math.sqrt(HEAD_SIZE)


GROUP = 4


def attention_kernel(
    heads, slots, part_rows, first_rows, targets, meta_ref, q_hbm, old_hbm, *refs
):
    kv_parts, (out_ref, q_ref, kv_ref, peak_ref, denom_ref, acc_ref, sems) = refs[:-7], refs[-7:]
    live = meta_ref[0]
    flag = meta_ref[1]

    @pl.when(flag <= 0)
    def _():
        copy = pltpu.make_async_copy(old_hbm, out_ref, sems.at[0])
        copy.start()
        copy.wait()

    @pl.when(flag > 0)
    def _():
        copies = [pltpu.make_async_copy(q_hbm, q_ref, sems.at[0])]
        for index, (part, first_row, target) in enumerate(zip(kv_parts, first_rows, targets)):
            column = pl.multiple_of(meta_ref[2 + slots + 2 * index] * HEAD_SIZE, HEAD_SIZE)
            start = pl.multiple_of(meta_ref[3 + slots + 2 * index] * part_rows, part_rows)
            copies.append(
                pltpu.make_async_copy(
                    part.at[pl.ds(first_row, part_rows), pl.ds(column, HEAD_SIZE)],
                    kv_ref.at[pl.ds(start, part_rows), pl.ds(target * HEAD_SIZE, HEAD_SIZE)],
                    sems.at[1 + index],
                )
            )
        for copy in copies:
            copy.start()
        peak_ref[...] = jnp.full_like(peak_ref, LOWEST)
        denom_ref[...] = jnp.zeros_like(denom_ref)
        acc_ref[...] = jnp.zeros_like(acc_ref)
        for copy in copies:
            copy.wait()

        def group(step, carry):
            tiles, biases = [], []
            for member in range(GROUP):
                slot = step * GROUP + member
                if member > 0:
                    present = slot < live
                    block = jnp.where(
                        present, meta_ref[2 + jnp.minimum(slot, slots - 1)], 0
                    )
                    biases.append(jnp.where(present, 0.0, LOWEST).astype(jnp.float32))
                else:
                    block = meta_ref[2 + slot]
                    biases.append(None)
                row = pl.multiple_of(block * KEY_BLOCK_TOKENS, KEY_BLOCK_TOKENS)
                tiles.append(kv_ref[pl.ds(row, KEY_BLOCK_TOKENS), :])
            tile = jnp.concatenate(tiles, axis=0)
            key_tile = tile[:, :HEAD_SIZE]
            value_tile = tile[:, HEAD_SIZE:].T
            value_tile = jnp.concatenate(
                [value_tile, jnp.ones((16, value_tile.shape[1]), jnp.bfloat16)], axis=0
            )
            for head in range(heads):
                query = q_ref[:, head * HEAD_SIZE : (head + 1) * HEAD_SIZE]
                scores = lax.dot_general(
                    key_tile, query, (((1,), (1,)), ((), ())), preferred_element_type=jnp.float32
                )
                parts = [
                    scores[member * KEY_BLOCK_TOKENS : (member + 1) * KEY_BLOCK_TOKENS]
                    for member in range(GROUP)
                ]
                parts = [p if b is None else p + b for p, b in zip(parts, biases)]
                top = functools.reduce(jnp.maximum, parts)
                old_peak = peak_ref[head]
                peak = jnp.maximum(old_peak, jnp.max(top, axis=0, keepdims=True))
                decay = jnp.exp2((old_peak - peak) * EXP2_SCALE)
                parts = [jnp.exp2((p - peak) * EXP2_SCALE) for p in parts]
                peak_ref[head] = peak
                weights = jnp.concatenate([p.astype(jnp.bfloat16) for p in parts], axis=0)
                update = lax.dot_general(
                    value_tile, weights, (((1,), (0,)), ((), ())), preferred_element_type=jnp.float32
                )
                denom_ref[head] = denom_ref[head] * decay + update[HEAD_SIZE : HEAD_SIZE + 1]
                acc_ref[head] = acc_ref[head] * decay + update[:HEAD_SIZE]
            return carry

        lax.fori_loop(0, (live + GROUP - 1) // GROUP, group, 0)
        for head in range(heads):
            result = acc_ref[head] / denom_ref[head]
            out_ref[:, head * HEAD_SIZE : (head + 1) * HEAD_SIZE] = result.T.astype(jnp.bfloat16)


def attend(block_list, live, flag, queries, old, key_values):
    part_rows, sources = key_values
    arrays, first_rows, heads_at, targets, places = zip(*sources)
    rows, width = queries.shape
    heads = width // HEAD_SIZE
    slots = block_list.shape[0]
    spots = [value[None] for pair in zip(heads_at, places) for value in pair]
    meta = jnp.concatenate([live[None], flag[None], block_list, *spots])
    in_hbm = pl.BlockSpec(memory_space=pltpu.HBM)
    return pl.pallas_call(
        functools.partial(attention_kernel, heads, slots, part_rows, first_rows, targets),
        out_shape=jax.ShapeDtypeStruct((rows, width), jnp.bfloat16),
        in_specs=[pl.BlockSpec(memory_space=pltpu.SMEM)] + [in_hbm] * (2 + len(arrays)),
        out_specs=pl.BlockSpec(memory_space=pltpu.VMEM),
        scratch_shapes=[
            pltpu.VMEM((rows, width), jnp.bfloat16),
            pltpu.VMEM((part_rows * len(arrays) // 2, 2 * HEAD_SIZE), jnp.bfloat16),
            pltpu.VMEM((heads, 1, rows), jnp.float32),
            pltpu.VMEM((heads, 1, rows), jnp.float32),
            pltpu.VMEM((heads, HEAD_SIZE, rows), jnp.float32),
            pltpu.SemaphoreType.DMA((1 + len(arrays),)),
        ],
        compiler_params=pltpu.CompilerParams(vmem_limit_bytes=24 << 20),
        cost_estimate=pl.CostEstimate(
            flops=1 << 20, transcendentals=0, bytes_accessed=1 << 20
        ),
        name="attend",
    )(
        meta,
        *[
            pltpu.with_memory_space_constraint(x, pltpu.HBM)
            for x in (queries, old, *arrays)
        ],
    )


def own_head_keys_values(keys, values, gate=lambda x: x):
    groups = lax.axis_size("ka")
    me = lax.axis_index("ka")
    rows = keys.shape[0]
    if groups == KEY_VALUE_HEADS == 4:
        x, core = me // 2, me % 2
        pair = 2 * HEAD_SIZE

        def heads_of(array, chip):
            return lax.dynamic_slice(array, (0, chip * pair), (rows, pair))

        def head_of(array, head):
            return lax.dynamic_slice(array, (0, head * HEAD_SIZE), (rows, HEAD_SIZE))

        across = [
            lax.ppermute(heads_of(a, 1 - x), "ka", [(i, i ^ 2) for i in range(4)])
            for a in (keys, values)
        ]
        across = gate(across)
        beside = lax.ppermute(
            jnp.concatenate(
                [
                    jnp.concatenate([head_of(a, 2 * x + 1 - core) for a in (keys, values)], axis=1),
                    jnp.concatenate([head_of(a, 1 - core) for a in across], axis=1),
                ],
                axis=0,
            ),
            "ka",
            [(i, i ^ 1) for i in range(4)],
        )
        near, far = jnp.bitwise_xor(me, 1), jnp.bitwise_xor(me, 3)
        sources = [
            (keys, 0, me, 0, me),
            (values, 0, me, 1, me),
            (across[0], 0, core, 0, jnp.bitwise_xor(me, 2)),
            (across[1], 0, core, 1, jnp.bitwise_xor(me, 2)),
        ]
        for side in range(2):
            for row, place in ((0, near), (rows, far)):
                sources.append((beside, row, jnp.int32(side), side, place))
        return rows, sources
    both = jnp.concatenate(
        [
            keys.reshape(rows, KEY_VALUE_HEADS, HEAD_SIZE),
            values.reshape(rows, KEY_VALUE_HEADS, HEAD_SIZE),
        ],
        axis=2,
    )
    both = jnp.repeat(both, groups // KEY_VALUE_HEADS, axis=1)
    everything = lax.all_to_all(
        both.reshape(rows, groups * 2 * HEAD_SIZE), "ka", split_axis=1, concat_axis=0, tiled=True
    )
    first = jnp.int32(0)
    return everything.shape[0], [(everything, 0, jnp.int32(side), side, first) for side in range(2)]


def ring_of(pb_size):
    if pb_size == 8:
        return [0, 2, 4, 6, 7, 5, 3, 1]
    return list(range(pb_size))


ROW_TILE = 128
IN_HBM = pl.BlockSpec(memory_space=pltpu.HBM)
IN_VMEM = pl.BlockSpec(memory_space=pltpu.VMEM)
IN_SMEM = pl.BlockSpec(memory_space=pltpu.SMEM)
SMALL_COST = pl.CostEstimate(flops=1 << 20, transcendentals=0, bytes_accessed=1 << 20)


def pinned(values, space):
    return [pltpu.with_memory_space_constraint(x, space) for x in values]


def ring_product_kernel(steps, spare_step, where_ref, *refs):
    count = len(steps)
    blocks, slabs, refs = refs[:4], (refs[4 : 4 + count], refs[4 + count : 4 + 2 * count]), refs[4 + 2 * count :]
    if spare_step is not None:
        base_ref, out_ref, spare_ref = refs[:3]
        refs = refs[3:]
    else:
        out_ref, refs = refs[0], refs[1:]
    left, right, block_sems, slab_sems = refs
    rows, depth = left.shape[0], right.shape[1] // count
    per = blocks[0].shape[1] // depth
    me = where_ref[where_ref.shape[0] - 1]

    def block_copy(index, slot, shift):
        target = spare_ref if index == count else left.at[:, pl.ds(index * depth, depth)]
        return pltpu.make_async_copy(
            blocks[slot].at[:, pl.ds(shift, depth)], target, block_sems.at[index]
        )

    def slab_copy(half, index):
        return pltpu.make_async_copy(
            slabs[half][index],
            right.at[half, pl.ds(index * depth, depth), :],
            slab_sems.at[half, index],
        )

    all_steps = steps if spare_step is None else (*steps, spare_step)
    for index, step in enumerate(all_steps):
        source = where_ref[step]
        slot_here = jnp.bitwise_xor(source // per, me)
        shift = pl.multiple_of((source % per) * depth, depth)
        for slot in range(4):

            @pl.when(slot_here == slot)
            def _(slot=slot):
                block_copy(index, slot, shift).start()

    for half in range(2):
        for index in range(count):
            slab_copy(half, index).start()
    for index in range(len(all_steps)):
        block_copy(index, 0, 0).wait()
    half_columns = right.shape[2]
    for half in range(2):
        columns = pl.ds(half * half_columns, half_columns)
        for index in range(count):
            slab_copy(half, index).wait()

        def rows_tile(step, carry):
            at = pl.ds(pl.multiple_of(step * ROW_TILE, ROW_TILE), ROW_TILE)
            product = jnp.dot(left[at, :], right[half], preferred_element_type=jnp.float32)
            if spare_step is not None:
                product = product + base_ref[at, columns]
            out_ref[at, columns] = product
            return carry

        lax.fori_loop(0, rows // ROW_TILE, rows_tile, 0)


def ring_product(where, blocks, steps, slabs, base=None, spare_step=None):
    count = len(steps)
    rows = blocks[0].shape[0]
    depth, half = slabs[0][0].shape
    spare = spare_step is not None
    out_shape = [jax.ShapeDtypeStruct((rows, 2 * half), jnp.float32)]
    if spare:
        out_shape.append(jax.ShapeDtypeStruct((rows, depth), jnp.bfloat16))
    return pl.pallas_call(
        functools.partial(ring_product_kernel, steps, spare_step),
        out_shape=out_shape,
        in_specs=[IN_SMEM] + [IN_HBM] * (4 + 2 * count) + [IN_VMEM] * spare,
        out_specs=[IN_VMEM] * len(out_shape),
        scratch_shapes=[
            pltpu.VMEM((rows, count * depth), jnp.bfloat16),
            pltpu.VMEM((2, count * depth, half), jnp.bfloat16),
            pltpu.SemaphoreType.DMA((count + spare,)),
            pltpu.SemaphoreType.DMA((2, count)),
        ],
        compiler_params=pltpu.CompilerParams(vmem_limit_bytes=(6 + 4 * count) << 20),
        cost_estimate=SMALL_COST,
        name="ring_product",
    )(
        where,
        *pinned([*blocks, *slabs[0], *slabs[1]], pltpu.HBM),
        *(pinned([base], pltpu.VMEM) if spare else []),
    )


def last_product_kernel(start, block_ref, slab_ref, base_ref, *refs):
    out_ref, staged, sems = refs[-3:]
    columns = pl.ds(start, slab_ref.shape[1])

    def tile_copy(tile):
        at = pl.ds(tile * ROW_TILE, ROW_TILE)
        return pltpu.make_async_copy(staged.at[at, :], out_ref.at[at, columns], sems.at[tile])

    tiles = block_ref.shape[0] // ROW_TILE
    for tile in range(tiles):
        at = pl.ds(tile * ROW_TILE, ROW_TILE)
        product = jnp.dot(block_ref[at, :], slab_ref[...], preferred_element_type=jnp.float32)
        staged[at, :] = (product + base_ref[at, columns]).astype(jnp.bfloat16)
        tile_copy(tile).start()
    for tile in range(tiles):
        tile_copy(tile).wait()


def last_product(block, slab, base, start, partly=None):
    rows, columns = base.shape
    operands = pinned([block, slab, base], pltpu.VMEM)
    if partly is not None:
        operands.append(partly)
    return pl.pallas_call(
        functools.partial(last_product_kernel, start),
        out_shape=jax.ShapeDtypeStruct((rows, columns), jnp.bfloat16),
        in_specs=[IN_VMEM] * 3 + [IN_HBM] * (partly is not None),
        out_specs=IN_HBM,
        scratch_shapes=[
            pltpu.VMEM((rows, slab.shape[1]), jnp.bfloat16),
            pltpu.SemaphoreType.DMA((rows // ROW_TILE,)),
        ],
        input_output_aliases={} if partly is None else {3: 0},
        compiler_params=pltpu.CompilerParams(vmem_limit_bytes=8 << 20),
        cost_estimate=SMALL_COST,
        name="last_product",
    )(*operands)


def project_ring(wo, inputs, attend_with):
    pb_size = lax.axis_size("pb")
    depth, columns = wo.shape
    ring = ring_of(pb_size)
    forward = [(ring[i], ring[(i + 1) % pb_size]) for i in range(pb_size)]
    backward = [(b, a) for a, b in forward]
    half = columns // 2
    far = pb_size // 2
    parts = [wo[:, :half]]
    wo, parts[0] = lax.optimization_barrier((wo, parts[0]))
    parts.append(wo[:, half:])
    inputs, parts[1] = lax.optimization_barrier((inputs, parts[1]))
    slabs = [[(0, part)] for part in parts]
    moving = [[part, part] for part in parts]

    def travel(hop):
        for part in range(2):
            if hop < far or part == 0:
                moving[part][0] = lax.ppermute(moving[part][0], "pb", forward)
            if hop < far or part == 1:
                moving[part][1] = lax.ppermute(moving[part][1], "pb", backward)

    def keep(hop):
        for part in range(2):
            if hop < far or part == 0:
                slabs[part].append((-hop, moving[part][0]))
            if hop < far or part == 1:
                slabs[part].append((hop, moving[part][1]))

    def gate(value):
        value, moving[0][0], moving[0][1] = lax.optimization_barrier(
            (value, moving[0][0], moving[0][1])
        )
        return value

    travel(1)
    attn = attend_with(inputs, gate)
    keep(1)
    for hop in range(2, far + 1):
        travel(hop)
        if hop == 2:
            attn, moving[0][:], moving[1][:] = lax.optimization_barrier(
                (attn, moving[0], moving[1])
            )
        keep(hop)
    across = lax.ppermute(attn, "ka", [(i, i ^ 2) for i in range(4)])
    beside = lax.ppermute(attn, "ka", [(i, i ^ 1) for i in range(4)])
    corner = lax.ppermute(attn, "ka", [(i, i ^ 3) for i in range(4)])
    around = jnp.asarray(
        [[ring[(ring.index(p) + step) % pb_size] for step in range(pb_size)] for p in range(pb_size)],
        jnp.int32,
    )
    mine = lax.dynamic_slice(around, (lax.axis_index("pb"), 0), (1, pb_size))[0]
    where = jnp.concatenate([mine, lax.axis_index("ka")[None].astype(jnp.int32)])
    blocks = [attn, beside, across, corner]
    at_step = [{offset % pb_size: slab for offset, slab in slabs[part]} for part in range(2)]

    def chosen(offsets):
        return [[at_step[part][offset % pb_size] for offset in offsets] for part in range(2)]

    def steps(offsets):
        return tuple(offset % pb_size for offset in offsets)

    early, late = (0, -1, 1, -2, 2), (-3, 3)
    (base,) = ring_product(where, blocks, steps(early), chosen(early))
    base, block = ring_product(where, blocks, steps(late), chosen(late), base, far)
    left = last_product(block, at_step[0][far], base, 0)
    return last_product(block, at_step[1][far], base, half, left)


def shards(queries, keys, values, block_ids, counts, refresh, cached_attn, wo):
    groups = lax.axis_size("ka")

    def attend_with(inputs, gate=lambda x: x):
        queries, keys, values, old = inputs
        return attend(
            block_ids[0, 0], counts[0, 0], refresh[0, 0], queries, old, own_head_keys_values(keys, values, gate)
        )

    inputs = (queries[0], keys, values, cached_attn[0])
    if lax.axis_size("pb") == 8 and groups == 4:
        mixed = project_ring(wo, inputs, attend_with)
    else:
        attn_full = lax.all_gather(attend_with(inputs), "ka", axis=1, tiled=True)
        mixed = jnp.dot(
            attn_full, lax.all_gather(wo, "pb", axis=0, tiled=True), preferred_element_type=jnp.float32
        ).astype(jnp.bfloat16)
    return mixed[None]


def solution(mesh):
    placed = (
        P(None, "pb", "ka"),
        P("ka", None),
        P("ka", None),
        P(None, "pb", None),
        P(None, "pb"),
        P(None, "pb"),
        P(None, "pb", "ka"),
        P("pb", "ka"),
    )
    return jax.shard_map(
        shards, mesh=mesh, in_specs=placed, out_specs=P(None, "pb", "ka"), check_vma=False
    )
```

```python
import functools
import math

import jax
import jax.numpy as jnp
from jax import lax
from jax.experimental import pallas as pl
from jax.experimental.pallas import tpu as pltpu
from jax.sharding import PartitionSpec as P

HEAD_SIZE = 128
QUERY_HEAD_COUNT = 32
KEY_VALUE_HEADS = 4
QUERY_BLOCK_SIZE = 512
KEY_BLOCK_TOKENS = 128
RATIO = QUERY_HEAD_COUNT // KEY_VALUE_HEADS
LOWEST = -1e30
EXP2_SCALE = math.log2(math.e) / math.sqrt(HEAD_SIZE)


GROUP = 4


def attention_kernel(
    heads, slots, part_rows, first_rows, targets, meta_ref, q_hbm, old_hbm, *refs
):
    kv_parts, (out_ref, q_ref, kv_ref, peak_ref, denom_ref, acc_ref, sems) = refs[:-7], refs[-7:]
    live = meta_ref[0]
    flag = meta_ref[1]

    @pl.when(flag <= 0)
    def _():
        copy = pltpu.make_async_copy(old_hbm, out_ref, sems.at[0])
        copy.start()
        copy.wait()

    @pl.when(flag > 0)
    def _():
        copies = [pltpu.make_async_copy(q_hbm, q_ref, sems.at[0])]
        for index, (part, first_row, target) in enumerate(zip(kv_parts, first_rows, targets)):
            column = pl.multiple_of(meta_ref[2 + slots + 2 * index] * HEAD_SIZE, HEAD_SIZE)
            start = pl.multiple_of(meta_ref[3 + slots + 2 * index] * part_rows, part_rows)
            copies.append(
                pltpu.make_async_copy(
                    part.at[pl.ds(first_row, part_rows), pl.ds(column, HEAD_SIZE)],
                    kv_ref.at[pl.ds(start, part_rows), pl.ds(target * HEAD_SIZE, HEAD_SIZE)],
                    sems.at[1 + index],
                )
            )
        for copy in copies:
            copy.start()
        peak_ref[...] = jnp.full_like(peak_ref, LOWEST)
        denom_ref[...] = jnp.zeros_like(denom_ref)
        acc_ref[...] = jnp.zeros_like(acc_ref)
        for copy in copies:
            copy.wait()

        def group(step, carry):
            tiles, biases = [], []
            for member in range(GROUP):
                slot = step * GROUP + member
                if member > 0:
                    present = slot < live
                    block = jnp.where(
                        present, meta_ref[2 + jnp.minimum(slot, slots - 1)], 0
                    )
                    biases.append(jnp.where(present, 0.0, LOWEST).astype(jnp.float32))
                else:
                    block = meta_ref[2 + slot]
                    biases.append(None)
                row = pl.multiple_of(block * KEY_BLOCK_TOKENS, KEY_BLOCK_TOKENS)
                tiles.append(kv_ref[pl.ds(row, KEY_BLOCK_TOKENS), :])
            tile = jnp.concatenate(tiles, axis=0)
            key_tile = tile[:, :HEAD_SIZE]
            value_tile = tile[:, HEAD_SIZE:].T
            value_tile = jnp.concatenate(
                [value_tile, jnp.ones((16, value_tile.shape[1]), jnp.bfloat16)], axis=0
            )
            for head in range(heads):
                query = q_ref[:, head * HEAD_SIZE : (head + 1) * HEAD_SIZE]
                scores = lax.dot_general(
                    key_tile, query, (((1,), (1,)), ((), ())), preferred_element_type=jnp.float32
                )
                parts = [
                    scores[member * KEY_BLOCK_TOKENS : (member + 1) * KEY_BLOCK_TOKENS]
                    for member in range(GROUP)
                ]
                parts = [p if b is None else p + b for p, b in zip(parts, biases)]
                top = functools.reduce(jnp.maximum, parts)
                old_peak = peak_ref[head]
                peak = jnp.maximum(old_peak, jnp.max(top, axis=0, keepdims=True))
                decay = jnp.exp2((old_peak - peak) * EXP2_SCALE)
                parts = [jnp.exp2((p - peak) * EXP2_SCALE) for p in parts]
                peak_ref[head] = peak
                weights = jnp.concatenate([p.astype(jnp.bfloat16) for p in parts], axis=0)
                update = lax.dot_general(
                    value_tile, weights, (((1,), (0,)), ((), ())), preferred_element_type=jnp.float32
                )
                denom_ref[head] = denom_ref[head] * decay + update[HEAD_SIZE : HEAD_SIZE + 1]
                acc_ref[head] = acc_ref[head] * decay + update[:HEAD_SIZE]
            return carry

        lax.fori_loop(0, (live + GROUP - 1) // GROUP, group, 0)
        for head in range(heads):
            result = acc_ref[head] / denom_ref[head]
            out_ref[:, head * HEAD_SIZE : (head + 1) * HEAD_SIZE] = result.T.astype(jnp.bfloat16)


def attend(block_list, live, flag, queries, old, key_values):
    part_rows, sources = key_values
    arrays, first_rows, heads_at, targets, places = zip(*sources)
    rows, width = queries.shape
    heads = width // HEAD_SIZE
    slots = block_list.shape[0]
    spots = [value[None] for pair in zip(heads_at, places) for value in pair]
    meta = jnp.concatenate([live[None], flag[None], block_list, *spots])
    in_hbm = pl.BlockSpec(memory_space=pltpu.HBM)
    return pl.pallas_call(
        functools.partial(attention_kernel, heads, slots, part_rows, first_rows, targets),
        out_shape=jax.ShapeDtypeStruct((rows, width), jnp.bfloat16),
        in_specs=[pl.BlockSpec(memory_space=pltpu.SMEM)] + [in_hbm] * (2 + len(arrays)),
        out_specs=pl.BlockSpec(memory_space=pltpu.VMEM),
        scratch_shapes=[
            pltpu.VMEM((rows, width), jnp.bfloat16),
            pltpu.VMEM((part_rows * len(arrays) // 2, 2 * HEAD_SIZE), jnp.bfloat16),
            pltpu.VMEM((heads, 1, rows), jnp.float32),
            pltpu.VMEM((heads, 1, rows), jnp.float32),
            pltpu.VMEM((heads, HEAD_SIZE, rows), jnp.float32),
            pltpu.SemaphoreType.DMA((1 + len(arrays),)),
        ],
        compiler_params=pltpu.CompilerParams(vmem_limit_bytes=24 << 20),
        cost_estimate=pl.CostEstimate(
            flops=1 << 20, transcendentals=0, bytes_accessed=1 << 20
        ),
        name="attend",
    )(
        meta,
        *[
            pltpu.with_memory_space_constraint(x, pltpu.HBM)
            for x in (queries, old, *arrays)
        ],
    )


def own_head_keys_values(keys, values, gate=lambda x: x):
    groups = lax.axis_size("ka")
    me = lax.axis_index("ka")
    rows = keys.shape[0]
    if groups == KEY_VALUE_HEADS == 4:
        x, core = me // 2, me % 2
        pair = 2 * HEAD_SIZE

        def heads_of(array, chip):
            return lax.dynamic_slice(array, (0, chip * pair), (rows, pair))

        def head_of(array, head):
            return lax.dynamic_slice(array, (0, head * HEAD_SIZE), (rows, HEAD_SIZE))

        across = [
            lax.ppermute(heads_of(a, 1 - x), "ka", [(i, i ^ 2) for i in range(4)])
            for a in (keys, values)
        ]
        across = gate(across)
        beside = lax.ppermute(
            jnp.concatenate(
                [
                    jnp.concatenate([head_of(a, 2 * x + 1 - core) for a in (keys, values)], axis=1),
                    jnp.concatenate([head_of(a, 1 - core) for a in across], axis=1),
                ],
                axis=0,
            ),
            "ka",
            [(i, i ^ 1) for i in range(4)],
        )
        near, far = jnp.bitwise_xor(me, 1), jnp.bitwise_xor(me, 3)
        sources = [
            (keys, 0, me, 0, me),
            (values, 0, me, 1, me),
            (across[0], 0, core, 0, jnp.bitwise_xor(me, 2)),
            (across[1], 0, core, 1, jnp.bitwise_xor(me, 2)),
        ]
        for side in range(2):
            for row, place in ((0, near), (rows, far)):
                sources.append((beside, row, jnp.int32(side), side, place))
        return rows, sources
    both = jnp.concatenate(
        [
            keys.reshape(rows, KEY_VALUE_HEADS, HEAD_SIZE),
            values.reshape(rows, KEY_VALUE_HEADS, HEAD_SIZE),
        ],
        axis=2,
    )
    both = jnp.repeat(both, groups // KEY_VALUE_HEADS, axis=1)
    everything = lax.all_to_all(
        both.reshape(rows, groups * 2 * HEAD_SIZE), "ka", split_axis=1, concat_axis=0, tiled=True
    )
    first = jnp.int32(0)
    return everything.shape[0], [(everything, 0, jnp.int32(side), side, first) for side in range(2)]


def ring_of(pb_size):
    if pb_size == 8:
        return [0, 2, 4, 6, 7, 5, 3, 1]
    return list(range(pb_size))


ROW_TILE = 128
IN_HBM = pl.BlockSpec(memory_space=pltpu.HBM)
IN_VMEM = pl.BlockSpec(memory_space=pltpu.VMEM)
IN_SMEM = pl.BlockSpec(memory_space=pltpu.SMEM)
SMALL_COST = pl.CostEstimate(flops=1 << 20, transcendentals=0, bytes_accessed=1 << 20)


def pinned(values, space):
    return [pltpu.with_memory_space_constraint(x, space) for x in values]


def ring_product_kernel(steps, spare_step, where_ref, *refs):
    count = len(steps)
    blocks, slabs, refs = refs[:4], (refs[4 : 4 + count], refs[4 + count : 4 + 2 * count]), refs[4 + 2 * count :]
    if spare_step is not None:
        base_ref, out_ref, spare_ref = refs[:3]
        refs = refs[3:]
    else:
        out_ref, refs = refs[0], refs[1:]
    left, right, block_sems, slab_sems = refs
    rows, depth = left.shape[0], right.shape[1] // count
    per = blocks[0].shape[1] // depth
    me = where_ref[where_ref.shape[0] - 1]

    def block_copy(index, slot, shift):
        target = spare_ref if index == count else left.at[:, pl.ds(index * depth, depth)]
        return pltpu.make_async_copy(
            blocks[slot].at[:, pl.ds(shift, depth)], target, block_sems.at[index]
        )

    def slab_copy(half, index):
        return pltpu.make_async_copy(
            slabs[half][index],
            right.at[half, pl.ds(index * depth, depth), :],
            slab_sems.at[half, index],
        )

    all_steps = steps if spare_step is None else (*steps, spare_step)
    for index, step in enumerate(all_steps):
        source = where_ref[step]
        slot_here = jnp.bitwise_xor(source // per, me)
        shift = pl.multiple_of((source % per) * depth, depth)
        for slot in range(4):

            @pl.when(slot_here == slot)
            def _(slot=slot):
                block_copy(index, slot, shift).start()

    for half in range(2):
        for index in range(count):
            slab_copy(half, index).start()
    for index in range(len(all_steps)):
        block_copy(index, 0, 0).wait()
    half_columns = right.shape[2]
    for half in range(2):
        columns = pl.ds(half * half_columns, half_columns)
        for index in range(count):
            slab_copy(half, index).wait()

        def rows_tile(step, carry):
            at = pl.ds(pl.multiple_of(step * ROW_TILE, ROW_TILE), ROW_TILE)
            product = jnp.dot(left[at, :], right[half], preferred_element_type=jnp.float32)
            if spare_step is not None:
                product = product + base_ref[at, columns]
            out_ref[at, columns] = product
            return carry

        lax.fori_loop(0, rows // ROW_TILE, rows_tile, 0)


def ring_product(where, blocks, steps, slabs, base=None, spare_step=None):
    count = len(steps)
    rows = blocks[0].shape[0]
    depth, half = slabs[0][0].shape
    spare = spare_step is not None
    out_shape = [jax.ShapeDtypeStruct((rows, 2 * half), jnp.float32)]
    if spare:
        out_shape.append(jax.ShapeDtypeStruct((rows, depth), jnp.bfloat16))
    return pl.pallas_call(
        functools.partial(ring_product_kernel, steps, spare_step),
        out_shape=out_shape,
        in_specs=[IN_SMEM] + [IN_HBM] * (4 + 2 * count) + [IN_VMEM] * spare,
        out_specs=[IN_VMEM] * len(out_shape),
        scratch_shapes=[
            pltpu.VMEM((rows, count * depth), jnp.bfloat16),
            pltpu.VMEM((2, count * depth, half), jnp.bfloat16),
            pltpu.SemaphoreType.DMA((count + spare,)),
            pltpu.SemaphoreType.DMA((2, count)),
        ],
        compiler_params=pltpu.CompilerParams(vmem_limit_bytes=(6 + 4 * count) << 20),
        cost_estimate=SMALL_COST,
        name="ring_product",
    )(
        where,
        *pinned([*blocks, *slabs[0], *slabs[1]], pltpu.HBM),
        *(pinned([base], pltpu.VMEM) if spare else []),
    )


def last_product_kernel(start, block_ref, slab_ref, base_ref, *refs):
    out_ref, staged, sems = refs[-3:]
    columns = pl.ds(start, slab_ref.shape[1])

    def tile_copy(tile):
        at = pl.ds(tile * ROW_TILE, ROW_TILE)
        return pltpu.make_async_copy(staged.at[at, :], out_ref.at[at, columns], sems.at[tile])

    tiles = block_ref.shape[0] // ROW_TILE
    for tile in range(tiles):
        at = pl.ds(tile * ROW_TILE, ROW_TILE)
        product = jnp.dot(block_ref[at, :], slab_ref[...], preferred_element_type=jnp.float32)
        staged[at, :] = (product + base_ref[at, columns]).astype(jnp.bfloat16)
        tile_copy(tile).start()
    for tile in range(tiles):
        tile_copy(tile).wait()


def last_product(block, slab, base, start, partly=None):
    rows, columns = base.shape
    operands = pinned([block, slab, base], pltpu.VMEM)
    if partly is not None:
        operands.append(partly)
    return pl.pallas_call(
        functools.partial(last_product_kernel, start),
        out_shape=jax.ShapeDtypeStruct((rows, columns), jnp.bfloat16),
        in_specs=[IN_VMEM] * 3 + [IN_HBM] * (partly is not None),
        out_specs=IN_HBM,
        scratch_shapes=[
            pltpu.VMEM((rows, slab.shape[1]), jnp.bfloat16),
            pltpu.SemaphoreType.DMA((rows // ROW_TILE,)),
        ],
        input_output_aliases={} if partly is None else {3: 0},
        compiler_params=pltpu.CompilerParams(vmem_limit_bytes=8 << 20),
        cost_estimate=SMALL_COST,
        name="last_product",
    )(*operands)


def project_ring(wo, inputs, attend_with):
    pb_size = lax.axis_size("pb")
    depth, columns = wo.shape
    ring = ring_of(pb_size)
    forward = [(ring[i], ring[(i + 1) % pb_size]) for i in range(pb_size)]
    backward = [(b, a) for a, b in forward]
    half = columns // 2
    far = pb_size // 2
    parts = [wo[:, :half]]
    wo, parts[0] = lax.optimization_barrier((wo, parts[0]))
    parts.append(wo[:, half:])
    inputs, parts[1] = lax.optimization_barrier((inputs, parts[1]))
    slabs = [[(0, part)] for part in parts]
    moving = [[part, part] for part in parts]

    def travel(hop):
        for part in range(2):
            if hop < far or part == 0:
                moving[part][0] = lax.ppermute(moving[part][0], "pb", forward)
            if hop < far or part == 1:
                moving[part][1] = lax.ppermute(moving[part][1], "pb", backward)

    def keep(hop):
        for part in range(2):
            if hop < far or part == 0:
                slabs[part].append((-hop, moving[part][0]))
            if hop < far or part == 1:
                slabs[part].append((hop, moving[part][1]))

    def gate(value):
        value, moving[1][1], moving[0][0], moving[0][1] = lax.optimization_barrier(
            (value, moving[1][1], moving[0][0], moving[0][1])
        )
        return value

    travel(1)
    attn = attend_with(inputs, gate)
    keep(1)
    for hop in range(2, far + 1):
        travel(hop)
        keep(hop)
    across = lax.ppermute(attn, "ka", [(i, i ^ 2) for i in range(4)])
    beside = lax.ppermute(attn, "ka", [(i, i ^ 1) for i in range(4)])
    corner = lax.ppermute(attn, "ka", [(i, i ^ 3) for i in range(4)])
    around = jnp.asarray(
        [[ring[(ring.index(p) + step) % pb_size] for step in range(pb_size)] for p in range(pb_size)],
        jnp.int32,
    )
    mine = lax.dynamic_slice(around, (lax.axis_index("pb"), 0), (1, pb_size))[0]
    where = jnp.concatenate([mine, lax.axis_index("ka")[None].astype(jnp.int32)])
    blocks = [attn, beside, across, corner]
    at_step = [{offset % pb_size: slab for offset, slab in slabs[part]} for part in range(2)]

    def chosen(offsets):
        return [[at_step[part][offset % pb_size] for offset in offsets] for part in range(2)]

    def steps(offsets):
        return tuple(offset % pb_size for offset in offsets)

    early, late = (0, -1, 1, -2, 2), (-3, 3)
    (base,) = ring_product(where, blocks, steps(early), chosen(early))
    base, block = ring_product(where, blocks, steps(late), chosen(late), base, far)
    left = last_product(block, at_step[0][far], base, 0)
    return last_product(block, at_step[1][far], base, half, left)


def shards(queries, keys, values, block_ids, counts, refresh, cached_attn, wo):
    groups = lax.axis_size("ka")

    def attend_with(inputs, gate=lambda x: x):
        queries, keys, values, old = inputs
        return attend(
            block_ids[0, 0], counts[0, 0], refresh[0, 0], queries, old, own_head_keys_values(keys, values, gate)
        )

    inputs = (queries[0], keys, values, cached_attn[0])
    if lax.axis_size("pb") == 8 and groups == 4:
        mixed = project_ring(wo, inputs, attend_with)
    else:
        attn_full = lax.all_gather(attend_with(inputs), "ka", axis=1, tiled=True)
        mixed = jnp.dot(
            attn_full, lax.all_gather(wo, "pb", axis=0, tiled=True), preferred_element_type=jnp.float32
        ).astype(jnp.bfloat16)
    return mixed[None]


def solution(mesh):
    placed = (
        P(None, "pb", "ka"),
        P("ka", None),
        P("ka", None),
        P(None, "pb", None),
        P(None, "pb"),
        P(None, "pb"),
        P(None, "pb", "ka"),
        P("pb", "ka"),
    )
    return jax.shard_map(
        shards, mesh=mesh, in_specs=placed, out_specs=P(None, "pb", "ka"), check_vma=False
    )
```

```python
import functools
import math

import jax
import jax.numpy as jnp
from jax import lax
from jax.experimental import pallas as pl
from jax.experimental.pallas import tpu as pltpu
from jax.sharding import PartitionSpec as P

HEAD_SIZE = 128
QUERY_HEAD_COUNT = 32
KEY_VALUE_HEADS = 4
QUERY_BLOCK_SIZE = 512
KEY_BLOCK_TOKENS = 128
RATIO = QUERY_HEAD_COUNT // KEY_VALUE_HEADS
LOWEST = -1e30
EXP2_SCALE = math.log2(math.e) / math.sqrt(HEAD_SIZE)


GROUP = 4


def attention_kernel(
    heads, slots, part_rows, first_rows, targets, meta_ref, q_hbm, old_hbm, *refs
):
    kv_parts, (out_ref, q_ref, kv_ref, peak_ref, denom_ref, acc_ref, sems) = refs[:-7], refs[-7:]
    live = meta_ref[0]
    flag = meta_ref[1]

    @pl.when(flag <= 0)
    def _():
        copy = pltpu.make_async_copy(old_hbm, out_ref, sems.at[0])
        copy.start()
        copy.wait()

    @pl.when(flag > 0)
    def _():
        copies = [pltpu.make_async_copy(q_hbm, q_ref, sems.at[0])]
        for index, (part, first_row, target) in enumerate(zip(kv_parts, first_rows, targets)):
            column = pl.multiple_of(meta_ref[2 + slots + 2 * index] * HEAD_SIZE, HEAD_SIZE)
            start = pl.multiple_of(meta_ref[3 + slots + 2 * index] * part_rows, part_rows)
            copies.append(
                pltpu.make_async_copy(
                    part.at[pl.ds(first_row, part_rows), pl.ds(column, HEAD_SIZE)],
                    kv_ref.at[pl.ds(start, part_rows), pl.ds(target * HEAD_SIZE, HEAD_SIZE)],
                    sems.at[1 + index],
                )
            )
        for copy in copies:
            copy.start()
        peak_ref[...] = jnp.full_like(peak_ref, LOWEST)
        denom_ref[...] = jnp.zeros_like(denom_ref)
        acc_ref[...] = jnp.zeros_like(acc_ref)
        for copy in copies:
            copy.wait()

        def group(step, carry):
            tiles, biases = [], []
            for member in range(GROUP):
                slot = step * GROUP + member
                if member > 0:
                    present = slot < live
                    block = jnp.where(
                        present, meta_ref[2 + jnp.minimum(slot, slots - 1)], 0
                    )
                    biases.append(jnp.where(present, 0.0, LOWEST).astype(jnp.float32))
                else:
                    block = meta_ref[2 + slot]
                    biases.append(None)
                row = pl.multiple_of(block * KEY_BLOCK_TOKENS, KEY_BLOCK_TOKENS)
                tiles.append(kv_ref[pl.ds(row, KEY_BLOCK_TOKENS), :])
            tile = jnp.concatenate(tiles, axis=0)
            key_tile = tile[:, :HEAD_SIZE]
            value_tile = tile[:, HEAD_SIZE:].T
            value_tile = jnp.concatenate(
                [value_tile, jnp.ones((16, value_tile.shape[1]), jnp.bfloat16)], axis=0
            )
            for head in range(heads):
                query = q_ref[:, head * HEAD_SIZE : (head + 1) * HEAD_SIZE]
                scores = lax.dot_general(
                    key_tile, query, (((1,), (1,)), ((), ())), preferred_element_type=jnp.float32
                )
                parts = [
                    scores[member * KEY_BLOCK_TOKENS : (member + 1) * KEY_BLOCK_TOKENS]
                    for member in range(GROUP)
                ]
                parts = [p if b is None else p + b for p, b in zip(parts, biases)]
                top = functools.reduce(jnp.maximum, parts)
                old_peak = peak_ref[head]
                peak = jnp.maximum(old_peak, jnp.max(top, axis=0, keepdims=True))
                decay = jnp.exp2((old_peak - peak) * EXP2_SCALE)
                parts = [jnp.exp2((p - peak) * EXP2_SCALE) for p in parts]
                peak_ref[head] = peak
                weights = jnp.concatenate([p.astype(jnp.bfloat16) for p in parts], axis=0)
                update = lax.dot_general(
                    value_tile, weights, (((1,), (0,)), ((), ())), preferred_element_type=jnp.float32
                )
                denom_ref[head] = denom_ref[head] * decay + update[HEAD_SIZE : HEAD_SIZE + 1]
                acc_ref[head] = acc_ref[head] * decay + update[:HEAD_SIZE]
            return carry

        lax.fori_loop(0, (live + GROUP - 1) // GROUP, group, 0)
        for head in range(heads):
            result = acc_ref[head] / denom_ref[head]
            out_ref[:, head * HEAD_SIZE : (head + 1) * HEAD_SIZE] = result.T.astype(jnp.bfloat16)


def attend(block_list, live, flag, queries, old, key_values):
    part_rows, sources = key_values
    arrays, first_rows, heads_at, targets, places = zip(*sources)
    rows, width = queries.shape
    heads = width // HEAD_SIZE
    slots = block_list.shape[0]
    spots = [value[None] for pair in zip(heads_at, places) for value in pair]
    meta = jnp.concatenate([live[None], flag[None], block_list, *spots])
    in_hbm = pl.BlockSpec(memory_space=pltpu.HBM)
    return pl.pallas_call(
        functools.partial(attention_kernel, heads, slots, part_rows, first_rows, targets),
        out_shape=jax.ShapeDtypeStruct((rows, width), jnp.bfloat16),
        in_specs=[pl.BlockSpec(memory_space=pltpu.SMEM)] + [in_hbm] * (2 + len(arrays)),
        out_specs=pl.BlockSpec(memory_space=pltpu.VMEM),
        scratch_shapes=[
            pltpu.VMEM((rows, width), jnp.bfloat16),
            pltpu.VMEM((part_rows * len(arrays) // 2, 2 * HEAD_SIZE), jnp.bfloat16),
            pltpu.VMEM((heads, 1, rows), jnp.float32),
            pltpu.VMEM((heads, 1, rows), jnp.float32),
            pltpu.VMEM((heads, HEAD_SIZE, rows), jnp.float32),
            pltpu.SemaphoreType.DMA((1 + len(arrays),)),
        ],
        compiler_params=pltpu.CompilerParams(vmem_limit_bytes=24 << 20),
        cost_estimate=pl.CostEstimate(
            flops=1 << 20, transcendentals=0, bytes_accessed=1 << 20
        ),
        name="attend",
    )(
        meta,
        *[
            pltpu.with_memory_space_constraint(x, pltpu.HBM)
            for x in (queries, old, *arrays)
        ],
    )


def own_head_keys_values(keys, values, gate=lambda x: x):
    groups = lax.axis_size("ka")
    me = lax.axis_index("ka")
    rows = keys.shape[0]
    if groups == KEY_VALUE_HEADS == 4:
        x, core = me // 2, me % 2
        pair = 2 * HEAD_SIZE

        def heads_of(array, chip):
            return lax.dynamic_slice(array, (0, chip * pair), (rows, pair))

        def head_of(array, head):
            return lax.dynamic_slice(array, (0, head * HEAD_SIZE), (rows, HEAD_SIZE))

        across = [
            lax.ppermute(heads_of(a, 1 - x), "ka", [(i, i ^ 2) for i in range(4)])
            for a in (keys, values)
        ]
        across = gate(across)
        beside = lax.ppermute(
            jnp.concatenate(
                [
                    jnp.concatenate([head_of(a, 2 * x + 1 - core) for a in (keys, values)], axis=1),
                    jnp.concatenate([head_of(a, 1 - core) for a in across], axis=1),
                ],
                axis=0,
            ),
            "ka",
            [(i, i ^ 1) for i in range(4)],
        )
        near, far = jnp.bitwise_xor(me, 1), jnp.bitwise_xor(me, 3)
        sources = [
            (keys, 0, me, 0, me),
            (values, 0, me, 1, me),
            (across[0], 0, core, 0, jnp.bitwise_xor(me, 2)),
            (across[1], 0, core, 1, jnp.bitwise_xor(me, 2)),
        ]
        for side in range(2):
            for row, place in ((0, near), (rows, far)):
                sources.append((beside, row, jnp.int32(side), side, place))
        return rows, sources
    both = jnp.concatenate(
        [
            keys.reshape(rows, KEY_VALUE_HEADS, HEAD_SIZE),
            values.reshape(rows, KEY_VALUE_HEADS, HEAD_SIZE),
        ],
        axis=2,
    )
    both = jnp.repeat(both, groups // KEY_VALUE_HEADS, axis=1)
    everything = lax.all_to_all(
        both.reshape(rows, groups * 2 * HEAD_SIZE), "ka", split_axis=1, concat_axis=0, tiled=True
    )
    first = jnp.int32(0)
    return everything.shape[0], [(everything, 0, jnp.int32(side), side, first) for side in range(2)]


def ring_of(pb_size):
    if pb_size == 8:
        return [0, 2, 4, 6, 7, 5, 3, 1]
    return list(range(pb_size))


ROW_TILE = 128
IN_HBM = pl.BlockSpec(memory_space=pltpu.HBM)
IN_VMEM = pl.BlockSpec(memory_space=pltpu.VMEM)
IN_SMEM = pl.BlockSpec(memory_space=pltpu.SMEM)
SMALL_COST = pl.CostEstimate(flops=1 << 20, transcendentals=0, bytes_accessed=1 << 20)


def pinned(values, space):
    return [pltpu.with_memory_space_constraint(x, space) for x in values]


def ring_product_kernel(steps, spare_step, where_ref, *refs):
    count = len(steps)
    blocks, slabs, refs = refs[:4], (refs[4 : 4 + count], refs[4 + count : 4 + 2 * count]), refs[4 + 2 * count :]
    if spare_step is not None:
        base_ref, out_ref, spare_ref = refs[:3]
        refs = refs[3:]
    else:
        out_ref, refs = refs[0], refs[1:]
    left, right, block_sems, slab_sems = refs
    rows, depth = left.shape[0], right.shape[1] // count
    per = blocks[0].shape[1] // depth
    me = where_ref[where_ref.shape[0] - 1]

    def block_copy(index, slot, shift):
        target = spare_ref if index == count else left.at[:, pl.ds(index * depth, depth)]
        return pltpu.make_async_copy(
            blocks[slot].at[:, pl.ds(shift, depth)], target, block_sems.at[index]
        )

    def slab_copy(half, index):
        return pltpu.make_async_copy(
            slabs[half][index],
            right.at[half, pl.ds(index * depth, depth), :],
            slab_sems.at[half, index],
        )

    all_steps = steps if spare_step is None else (*steps, spare_step)
    for index, step in enumerate(all_steps):
        source = where_ref[step]
        slot_here = jnp.bitwise_xor(source // per, me)
        shift = pl.multiple_of((source % per) * depth, depth)
        for slot in range(4):

            @pl.when(slot_here == slot)
            def _(slot=slot):
                block_copy(index, slot, shift).start()

    for half in range(2):
        for index in range(count):
            slab_copy(half, index).start()
    for index in range(len(all_steps)):
        block_copy(index, 0, 0).wait()
    half_columns = right.shape[2]
    for half in range(2):
        columns = pl.ds(half * half_columns, half_columns)
        for index in range(count):
            slab_copy(half, index).wait()

        def rows_tile(step, carry):
            at = pl.ds(pl.multiple_of(step * ROW_TILE, ROW_TILE), ROW_TILE)
            product = jnp.dot(left[at, :], right[half], preferred_element_type=jnp.float32)
            if spare_step is not None:
                product = product + base_ref[at, columns]
            out_ref[at, columns] = product
            return carry

        lax.fori_loop(0, rows // ROW_TILE, rows_tile, 0)


def ring_product(where, blocks, steps, slabs, base=None, spare_step=None):
    count = len(steps)
    rows = blocks[0].shape[0]
    depth, half = slabs[0][0].shape
    spare = spare_step is not None
    out_shape = [jax.ShapeDtypeStruct((rows, 2 * half), jnp.float32)]
    if spare:
        out_shape.append(jax.ShapeDtypeStruct((rows, depth), jnp.bfloat16))
    return pl.pallas_call(
        functools.partial(ring_product_kernel, steps, spare_step),
        out_shape=out_shape,
        in_specs=[IN_SMEM] + [IN_HBM] * (4 + 2 * count) + [IN_VMEM] * spare,
        out_specs=[IN_VMEM] * len(out_shape),
        scratch_shapes=[
            pltpu.VMEM((rows, count * depth), jnp.bfloat16),
            pltpu.VMEM((2, count * depth, half), jnp.bfloat16),
            pltpu.SemaphoreType.DMA((count + spare,)),
            pltpu.SemaphoreType.DMA((2, count)),
        ],
        compiler_params=pltpu.CompilerParams(vmem_limit_bytes=(6 + 4 * count) << 20),
        cost_estimate=SMALL_COST,
        name="ring_product",
    )(
        where,
        *pinned([*blocks, *slabs[0], *slabs[1]], pltpu.HBM),
        *(pinned([base], pltpu.VMEM) if spare else []),
    )


def last_product_kernel(start, block_ref, slab_ref, base_ref, *refs):
    out_ref, staged, sems = refs[-3:]
    columns = pl.ds(start, slab_ref.shape[1])

    def tile_copy(tile):
        at = pl.ds(tile * ROW_TILE, ROW_TILE)
        return pltpu.make_async_copy(staged.at[at, :], out_ref.at[at, columns], sems.at[tile])

    tiles = block_ref.shape[0] // ROW_TILE
    for tile in range(tiles):
        at = pl.ds(tile * ROW_TILE, ROW_TILE)
        product = jnp.dot(block_ref[at, :], slab_ref[...], preferred_element_type=jnp.float32)
        staged[at, :] = (product + base_ref[at, columns]).astype(jnp.bfloat16)
        tile_copy(tile).start()
    for tile in range(tiles):
        tile_copy(tile).wait()


def last_product(block, slab, base, start, partly=None):
    rows, columns = base.shape
    operands = pinned([block, slab, base], pltpu.VMEM)
    if partly is not None:
        operands.append(partly)
    return pl.pallas_call(
        functools.partial(last_product_kernel, start),
        out_shape=jax.ShapeDtypeStruct((rows, columns), jnp.bfloat16),
        in_specs=[IN_VMEM] * 3 + [IN_HBM] * (partly is not None),
        out_specs=IN_HBM,
        scratch_shapes=[
            pltpu.VMEM((rows, slab.shape[1]), jnp.bfloat16),
            pltpu.SemaphoreType.DMA((rows // ROW_TILE,)),
        ],
        input_output_aliases={} if partly is None else {3: 0},
        compiler_params=pltpu.CompilerParams(vmem_limit_bytes=8 << 20),
        cost_estimate=SMALL_COST,
        name="last_product",
    )(*operands)


def project_ring(wo, inputs, attend_with):
    pb_size = lax.axis_size("pb")
    depth, columns = wo.shape
    ring = ring_of(pb_size)
    forward = [(ring[i], ring[(i + 1) % pb_size]) for i in range(pb_size)]
    backward = [(b, a) for a, b in forward]
    half = columns // 2
    far = pb_size // 2
    parts = [wo[:, :half]]
    wo, parts[0] = lax.optimization_barrier((wo, parts[0]))
    parts.append(wo[:, half:])
    inputs, parts[1] = lax.optimization_barrier((inputs, parts[1]))
    slabs = [[(0, part)] for part in parts]
    moving = [[part, part] for part in parts]

    def travel(hop):
        for part in range(2):
            if hop < far or part == 0:
                moving[part][0] = lax.ppermute(moving[part][0], "pb", forward)
            if hop < far or part == 1:
                moving[part][1] = lax.ppermute(moving[part][1], "pb", backward)

    def keep(hop):
        for part in range(2):
            if hop < far or part == 0:
                slabs[part].append((-hop, moving[part][0]))
            if hop < far or part == 1:
                slabs[part].append((hop, moving[part][1]))

    travel(1)
    attn = attend_with(inputs)
    keep(1)
    for hop in range(2, far + 1):
        travel(hop)
        keep(hop)
    across = lax.ppermute(attn, "ka", [(i, i ^ 2) for i in range(4)])
    beside = lax.ppermute(attn, "ka", [(i, i ^ 1) for i in range(4)])
    corner = lax.ppermute(attn, "ka", [(i, i ^ 3) for i in range(4)])
    around = jnp.asarray(
        [[ring[(ring.index(p) + step) % pb_size] for step in range(pb_size)] for p in range(pb_size)],
        jnp.int32,
    )
    mine = lax.dynamic_slice(around, (lax.axis_index("pb"), 0), (1, pb_size))[0]
    where = jnp.concatenate([mine, lax.axis_index("ka")[None].astype(jnp.int32)])
    blocks = [attn, beside, across, corner]
    at_step = [{offset % pb_size: slab for offset, slab in slabs[part]} for part in range(2)]

    def chosen(offsets):
        return [[at_step[part][offset % pb_size] for offset in offsets] for part in range(2)]

    def steps(offsets):
        return tuple(offset % pb_size for offset in offsets)

    early, late = (0, -1, 1, -2, 2), (-3, 3)
    (base,) = ring_product(where, blocks, steps(early), chosen(early))
    base, block = ring_product(where, blocks, steps(late), chosen(late), base, far)
    left = last_product(block, at_step[0][far], base, 0)
    return last_product(block, at_step[1][far], base, half, left)


def shards(queries, keys, values, block_ids, counts, refresh, cached_attn, wo):
    groups = lax.axis_size("ka")

    def attend_with(inputs, gate=lambda x: x):
        queries, keys, values, old = inputs
        return attend(
            block_ids[0, 0], counts[0, 0], refresh[0, 0], queries, old, own_head_keys_values(keys, values, gate)
        )

    inputs = (queries[0], keys, values, cached_attn[0])
    if lax.axis_size("pb") == 8 and groups == 4:
        mixed = project_ring(wo, inputs, attend_with)
    else:
        attn_full = lax.all_gather(attend_with(inputs), "ka", axis=1, tiled=True)
        mixed = jnp.dot(
            attn_full, lax.all_gather(wo, "pb", axis=0, tiled=True), preferred_element_type=jnp.float32
        ).astype(jnp.bfloat16)
    return mixed[None]


def solution(mesh):
    placed = (
        P(None, "pb", "ka"),
        P("ka", None),
        P("ka", None),
        P(None, "pb", None),
        P(None, "pb"),
        P(None, "pb"),
        P(None, "pb", "ka"),
        P("pb", "ka"),
    )
    return jax.shard_map(
        shards, mesh=mesh, in_specs=placed, out_specs=P(None, "pb", "ka"), check_vma=False
    )
```
